256 devices in a mesh: grp: 16 (over y_lo, z), row: 16 (over y_hi, x, core).
Axes of the slice: x: 4, y: 4 (y_hi: 2, y_lo: 2; y = y_hi * 2 + y_lo), z: 8, core: 2. Of those that a mesh axis runs over, the one named last changes fastest.
Arguments:
- view_a: float32 [16384, 8192], P('row', 'grp'), may hold values from -40 to 40
- view_b: float32 [16384, 8192], P('row', 'grp'), may hold values from -40 to 40
Outputs:
- grad_a: float32 [16384, 8192], P('row', 'grp')
- grad_b: float32 [16384, 8192], P('row', 'grp')
The draws below stay inside these ranges and needn't reach their ends.
All inputs are finite; a program needn't handle non-finite values.
Results may differ from the reference program's by a relative error of at most 0.00025.
Values sent between devices are 32-bit elements; how exact they have to be, the bound alone decides.
No kernel may reach another device: no remote copies, remote signals or barrier semaphores. Data moves between devices by JAX's collectives and lax.ppermute only.
A program may use at most 64 MiB of HBM per device.

```python
import jax
import jax.numpy as jnp
from jax import lax

F = 8192
NROWS = 16384
N_GRP = 16


def make_views(key):
    keys = jax.random.split(jax.random.fold_in(key, 7), 4)
    base_part = jax.random.normal(keys[0], (NROWS, F), jnp.float32)
    common = jax.random.normal(keys[1], (NROWS, 1), jnp.float32)
    direction = jax.random.normal(keys[2], (1, F), jnp.float32)
    noise_part = jax.random.normal(keys[3], (NROWS, F), jnp.float32)
    first = base_part + 0.4 * common * direction
    second = 0.8 * first + 0.6 * noise_part
    return (jnp.clip(first, -40.0, 40.0), jnp.clip(second, -40.0, 40.0))


def draw_view_a(key, part):
    return make_views(key)[0]


def draw_view_b(key, part):
    return make_views(key)[1]


def setup_inputs(seed: int = 0) -> dict:
    splits = jax.random.split(jax.random.key(seed), 3)
    return {
        "view_a": draw_view_a(jax.random.fold_in(splits[2], 71), 0),
        "view_b": draw_view_b(jax.random.fold_in(splits[2], 71), 0),
    }


epsilon = 1e-05
off_weight = 0.0051

def normalize(view):
    mean_val = lax.optimization_barrier(jnp.sum(view, axis=0)) / NROWS
    square = lax.optimization_barrier(jnp.sum(view * view, axis=0)) / NROWS
    scale_val = jnp.sqrt(square - mean_val * mean_val + epsilon)
    return ((view - mean_val) / scale_val, scale_val)

def penalty_of(corr, row_offset, panel_width):
    row_index = row_offset + lax.iota(jnp.int32, corr.shape[0])[:, None]
    column = lax.iota(jnp.int32, corr.shape[1])[None, :]
    on_diagonal = column == row_index + panel_width
    return jnp.where(on_diagonal, -2.0 * (1.0 - corr), 2.0 * off_weight * corr)

def finish(grad, normed, scale_val):
    mean_grad = lax.optimization_barrier(jnp.sum(grad, axis=0)) / NROWS
    mean_cross = lax.optimization_barrier(jnp.sum(grad * normed, axis=0)) / NROWS
    return (grad - mean_grad - normed * mean_cross) / scale_val

def reference(view_a, view_b):
    highest = lax.Precision.HIGHEST
    norm_a, scale_a = normalize(view_a)
    norm_b, scale_b = normalize(view_b)
    panel_width = F // N_GRP
    panels_a = norm_a.reshape(NROWS, N_GRP, panel_width).transpose(1, 0, 2)
    panels_b = norm_b.reshape(NROWS, N_GRP, panel_width).transpose(1, 0, 2)
    neighbours = jnp.concatenate([jnp.roll(panels_b, 1, axis=0), panels_b, jnp.roll(panels_b, -1, axis=0)], axis=2)

    def one_group(pair):
        own, near = pair
        corr = jnp.dot(own.T, near, precision=highest, preferred_element_type=jnp.float32) / NROWS
        penalty = penalty_of(corr, 0, panel_width)
        grad_own = jnp.dot(near, penalty.T, precision=highest, preferred_element_type=jnp.float32)
        contrib = jnp.dot(own, penalty, precision=highest, preferred_element_type=jnp.float32)
        return (grad_own, contrib)
    grad_panels, contribs = lax.map(one_group, (panels_a, neighbours))
    left_part = contribs[:, :, :panel_width]
    middle_part = contribs[:, :, panel_width:2 * panel_width]
    right_part = contribs[:, :, 2 * panel_width:]
    grad_b_panels = middle_part + jnp.roll(left_part, -1, axis=0) + jnp.roll(right_part, 1, axis=0)
    grad_a_full = grad_panels.transpose(1, 0, 2).reshape(NROWS, F)
    grad_b_full = grad_b_panels.transpose(1, 0, 2).reshape(NROWS, F)
    return (finish(grad_a_full, norm_a, scale_a), finish(grad_b_full, norm_b, scale_b))
```

```python
import jax
import jax.numpy as jnp
from jax import lax
from jax.sharding import PartitionSpec as P

epsilon = 1e-05
off_weight = 0.0051


def across(block, axis, shift):
    count = lax.axis_size(axis)
    return lax.ppermute(block, axis, [(i, (i + shift) % count) for i in range(count)])


def to_core(block):
    return lax.ppermute(block, "row", [(i, i ^ 1) for i in range(16)])


def to_y(block):
    return lax.ppermute(block, "row", [(i, i ^ 8) for i in range(16)])


def to_x(block, shift):
    pairs = [(i, (i & 9) | ((((i >> 1) + shift) & 3) << 1)) for i in range(16)]
    return lax.ppermute(block, "row", pairs)


def pick(stack, index):
    return lax.dynamic_index_in_dim(stack, index, 0, keepdims=False)


def reduce_chunks(parts, core, x):
    mine = pick(parts, core) + to_core(pick(parts, 1 - core))
    total = pick(mine, x)
    for shift in (1, 2, 3):
        total = total + to_x(pick(mine, (x + shift) & 3), shift)
    return total


def gather_chunks(chunk, core, x):
    row = jnp.zeros((4,) + chunk.shape, chunk.dtype)
    row = lax.dynamic_update_index_in_dim(row, chunk, x, 0)
    for shift in (1, 2, 3):
        row = lax.dynamic_update_index_in_dim(row, to_x(chunk, shift), (x - shift) & 3, 0)
    other = to_core(row)
    low = jnp.where(core == 0, row, other)
    high = jnp.where(core == 0, other, row)
    return jnp.stack([low, high]).transpose(2, 0, 1, 3, 4)


def dot(a, b, a_dim, b_dim):
    return lax.dot_general(
        a,
        b,
        (((a_dim,), (b_dim,)), ((), ())),
        precision=lax.Precision.HIGH,
        preferred_element_type=jnp.float32,
    )


def after(block, *others):
    bound = [o.reshape(-1)[0] for o in others]
    held = lax.optimization_barrier((block, *bound))
    gate = sum(held[1:])
    return jnp.where(jnp.isnan(gate), gate, held[0])


def penalty_of(corr, own):
    off = 2.0 * off_weight * corr
    if not own:
        return off
    row_index = lax.iota(jnp.int32, corr.shape[0])[:, None]
    column = lax.iota(jnp.int32, corr.shape[1])[None, :]
    return jnp.where(column == row_index, -2.0 * (1.0 - corr), off)


def per_device(view_a, view_b):
    local_rows, width = view_a.shape
    batch = local_rows * lax.axis_size("row")
    index = lax.axis_index("row")
    core, x = index & 1, (index >> 1) & 3

    with jax.named_scope("stats"):
        sums = jnp.stack(
            [
                jnp.sum(view_a, axis=0),
                jnp.sum(view_a * view_a, axis=0),
                jnp.sum(view_b, axis=0),
                jnp.sum(view_b * view_b, axis=0),
            ]
        )
        sums = sums + to_y(sums)
        raw_b = view_b
    with jax.named_scope("halo_b"):
        prev_raw = across(raw_b, "grp", 1)
        next_raw = across(raw_b, "grp", -1)
    with jax.named_scope("stats"):
        sums = sums + to_core(sums)
        sums = sums + to_x(sums, 1) + to_x(sums, 2) + to_x(sums, 3)
        mean_a = sums[0] / batch
        scale_a = jnp.sqrt(sums[1] / batch - mean_a * mean_a + epsilon)
        mean_b = sums[2] / batch
        scale_b = jnp.sqrt(sums[3] / batch - mean_b * mean_b + epsilon)
        left_a = (sums[0] / batch - mean_a) / scale_a
        left_b = (sums[2] / batch - mean_b) / scale_b
        facts = jnp.stack([mean_b, scale_b, left_b, left_a])
        prev_facts = across(facts, "grp", 1)
        next_facts = across(facts, "grp", -1)
    norm_a = (view_a - mean_a) / scale_a
    norm_b = (view_b - mean_b) / scale_b

    def chunked(partial):
        return partial.reshape(2, 4, width // 8, width)

    with jax.named_scope("own"):
        own_part = chunked(dot(norm_a, norm_b, 0, 0) / batch)
        own_chunk = reduce_chunks(own_part, core, x)
        own_chunk = own_chunk + to_y(own_chunk)
        half = local_rows // 2
        top = norm_a[:half]
    with jax.named_scope("halo_a"):
        top = after(top, prev_raw, next_raw)
        prev_top = across(top, "grp", 1)
        next_top = across(top, "grp", -1)
    with jax.named_scope("side"):
        prev_b = (prev_raw - prev_facts[0]) / prev_facts[1]
        next_b = (next_raw - next_facts[0]) / next_facts[1]
        side_part = jnp.concatenate(
            [chunked(dot(norm_a, prev_b, 0, 0) / batch), chunked(dot(norm_a, next_b, 0, 0) / batch)],
            axis=2,
        )
        side_chunk = reduce_chunks(side_part, core, x)
        side_chunk = side_chunk + to_y(side_chunk)
        side_chunk = side_chunk.reshape(2, width // 8, width)
        from_next = across(side_chunk[0], "grp", -1)
        from_prev = across(side_chunk[1], "grp", 1)
    with jax.named_scope("halo_a"):
        low = after(norm_a[half:], side_chunk)
        prev_low = across(low, "grp", 1)
        next_low = across(low, "grp", -1)
    with jax.named_scope("own"):
        corr_own = gather_chunks(own_chunk[None], core, x).reshape(width, width)
        pen_own = penalty_of(corr_own, True)
        grad_own = dot(norm_b, pen_own, 1, 1)
        grad_other = dot(norm_a, pen_own, 1, 0)
    with jax.named_scope("side"):
        pack = jnp.stack([side_chunk[0], side_chunk[1], from_prev, from_next])
        corr = gather_chunks(pack, core, x).reshape(4, width, width)
        pen = penalty_of(corr, False)
        cross_a = jnp.sum(pen_own * corr_own, axis=1) + jnp.sum(
            pen[0] * corr[0] + pen[1] * corr[1], axis=1
        )
        cross_b = jnp.sum(pen_own * corr_own + pen[2] * corr[2] + pen[3] * corr[3], axis=0)
        mean_ga = jnp.sum(
            pen_own * left_b + pen[0] * prev_facts[2] + pen[1] * next_facts[2], axis=1
        )
        mean_gb = jnp.sum(
            pen_own * left_a[:, None]
            + pen[2] * prev_facts[3][:, None]
            + pen[3] * next_facts[3][:, None],
            axis=0,
        )
        prev_a = jnp.concatenate([prev_top, prev_low])
        next_a = jnp.concatenate([next_top, next_low])
        grad_own = grad_own + dot(prev_b, pen[0], 1, 1) + dot(next_b, pen[1], 1, 1)
        grad_a = (grad_own - mean_ga - norm_a * cross_a) / scale_a
        grad_other = grad_other + dot(prev_a, pen[2], 1, 0) + dot(next_a, pen[3], 1, 0)
        grad_b = (grad_other - mean_gb - norm_b * cross_b) / scale_b
    return (grad_a, grad_b)


def solution(mesh):
    placed = (P("row", "grp"), P("row", "grp"))
    return jax.shard_map(
        per_device,
        mesh=mesh,
        in_specs=placed,
        out_specs=(P("row", "grp"), P("row", "grp")),
        check_vma=False,
    )
```

```python
import functools

import jax
import jax.numpy as jnp
from jax import lax
from jax.experimental import pallas as pl
from jax.experimental.pallas import tpu as pltpu
from jax.sharding import PartitionSpec as P

epsilon = 1e-05
off_weight = 0.0051
f32 = jnp.float32
bf16 = jnp.bfloat16


any_spec = pl.BlockSpec(memory_space=pl.ANY)
smem_spec = pl.BlockSpec(memory_space=pltpu.SMEM)
vmem_spec = pl.BlockSpec(memory_space=pltpu.VMEM)
params = pltpu.CompilerParams(vmem_limit_bytes=48 * 1024 * 1024)


def shape(*dims):
    return jax.ShapeDtypeStruct(dims, f32)


def across(block, shift):
    count = lax.axis_size("grp")
    return lax.ppermute(block, "grp", [(i, (i + shift) % count) for i in range(count)])


def to_core(block):
    return lax.ppermute(block, "row", [(i, i ^ 1) for i in range(16)])


def to_y(block):
    return lax.ppermute(block, "row", [(i, i ^ 8) for i in range(16)])


def to_x(block, shift):
    pairs = [(i, (i & 9) | ((((i >> 1) + shift) & 3) << 1)) for i in range(16)]
    return lax.ppermute(block, "row", pairs)


def split(value):
    high = value.astype(bf16)
    return high, (value - high.astype(f32)).astype(bf16)


def mm(a, b):
    return lax.dot_general(a, b, (((1,), (0,)), ((), ())), preferred_element_type=f32)


def gram(a, b):
    a_high, a_low = split(a.T)
    b_high, b_low = split(b)
    return mm(
        jnp.concatenate([a_high, a_high, a_low], axis=1),
        jnp.concatenate([b_high, b_low, b_high], axis=0),
    )


def thrice(value):
    high, low = split(value)
    return jnp.concatenate([high, high, low], axis=1)


def sums_kernel(a_ref, b_ref, out_ref):
    @pl.when(pl.program_id(0) == 0)
    def _():
        out_ref[...] = jnp.zeros_like(out_ref)

    a, b = a_ref[...], b_ref[...]
    for row, value in enumerate((a, a * a, b, b * b)):
        out_ref[row : row + 1, :] += jnp.sum(value, axis=0, keepdims=True)


def sums_of(a, b):
    rows, width = a.shape
    tile = rows // 4
    spec = pl.BlockSpec((tile, width), lambda i: (i, 0))
    return pl.pallas_call(
        sums_kernel,
        grid=(4,),
        in_specs=[spec, spec],
        out_specs=pl.BlockSpec((8, width), lambda i: (0, 0)),
        out_shape=shape(8, width),
        name="sums",
    )(a, b)


def put_slots(at_ref, acc, keep_ref, send_ref, first, rows):
    core, x = at_ref[0], at_ref[1]
    for slot in range(4):
        chunk = (x + slot) & 3
        mine = pl.multiple_of((core * 4 + chunk) * rows, rows)
        theirs = pl.multiple_of(((1 - core) * 4 + chunk) * rows, rows)
        keep_ref[slot, first : first + rows, :] = acc[pl.ds(mine, rows), :]
        send_ref[slot, first : first + rows, :] = acc[pl.ds(theirs, rows), :]


def own_corr_kernel(batch, steps, at_ref, a_ref, b_ref, *refs):
    parts, (top_ref, facts_ref, keep_ref, send_ref, acc_ref) = refs[:4], refs[4:]
    step = pl.program_id(0)

    @pl.when(step == 0)
    def _():
        total = parts[0][...] + parts[1][...] + parts[2][...] + parts[3][...]
        total = total / batch
        rows = []
        for first in (0, 2):
            mean, square = total[first : first + 1], total[first + 1 : first + 2]
            rows += [mean, 1.0 / jnp.sqrt(square - mean * mean + epsilon)]
        facts_ref[0:1, :] = rows[0]
        facts_ref[1:2, :] = rows[1]
        facts_ref[2:3, :] = rows[2]
        facts_ref[3:4, :] = rows[3]
        facts_ref[4:5, :] = (total[0:1] - rows[0]) * rows[1]
        facts_ref[5:6, :] = (total[2:3] - rows[2]) * rows[3]
        facts_ref[6:8, :] = jnp.zeros((2, total.shape[1]), f32)
        acc_ref[...] = jnp.zeros_like(acc_ref)

    norm_a = (a_ref[...] - facts_ref[0:1, :]) * facts_ref[1:2, :]
    norm_b = (b_ref[...] - facts_ref[2:3, :]) * facts_ref[3:4, :]
    top_ref[...] = norm_a
    acc_ref[...] += gram(norm_a, norm_b)

    @pl.when(step == steps - 1)
    def _():
        acc_ref[...] = acc_ref[...] / batch
        put_slots(at_ref, acc_ref, keep_ref, send_ref, 0, keep_ref.shape[1])


def own_corr(at, a, b, parts, batch):
    rows, width = a.shape
    steps = 4
    tile = rows // steps
    spec = pl.BlockSpec((tile, width), lambda i: (i, 0))
    whole = pl.BlockSpec((8, width), lambda i: (0, 0))
    slots = pl.BlockSpec((4, width // 8, width), lambda i: (0, 0, 0))
    return pl.pallas_call(
        functools.partial(own_corr_kernel, batch, steps),
        grid=(steps,),
        in_specs=[smem_spec, spec, spec] + [whole] * 4,
        out_specs=[spec, whole, slots, slots],
        out_shape=[shape(rows, width), shape(8, width)] + [shape(4, width // 8, width)] * 2,
        scratch_shapes=[pltpu.VMEM((width, width), f32)],
        compiler_params=params,
        name="own_corr",
    )(at, a, b, *parts)


def side_corr_kernel(batch, steps, at_ref, a_ref, prev_ref, next_ref, pf_ref, nf_ref, *refs):
    keep_ref, send_ref, left_ref, right_ref = refs[-4:]
    step = pl.program_id(0)

    @pl.when(step == 0)
    def _():
        left_ref[...] = jnp.zeros_like(left_ref)
        right_ref[...] = jnp.zeros_like(right_ref)

    norm_a = a_ref[...]
    for acc_ref, b_ref, facts_ref in ((left_ref, prev_ref, pf_ref), (right_ref, next_ref, nf_ref)):
        norm_b = (b_ref[...] - facts_ref[2:3, :]) * facts_ref[3:4, :]
        acc_ref[...] += gram(norm_a, norm_b)

    @pl.when(step == steps - 1)
    def _():
        rows = keep_ref.shape[1] // 2
        for side, acc_ref in enumerate((left_ref, right_ref)):
            acc_ref[...] = acc_ref[...] / batch
            put_slots(at_ref, acc_ref, keep_ref, send_ref, side * rows, rows)


def side_corr(at, norm_a, prev_b, next_b, prev_facts, next_facts, batch, wait_for):
    rows, width = norm_a.shape
    steps = 4
    spec = pl.BlockSpec((rows // steps, width), lambda i: (i, 0))
    whole = pl.BlockSpec((8, width), lambda i: (0, 0))
    slots = pl.BlockSpec((4, width // 4, width), lambda i: (0, 0, 0))
    return pl.pallas_call(
        functools.partial(side_corr_kernel, batch, steps),
        grid=(steps,),
        in_specs=[smem_spec, spec, spec, spec, whole, whole] + [any_spec] * len(wait_for),
        out_specs=[slots, slots],
        out_shape=[shape(4, width // 4, width)] * 2,
        scratch_shapes=[pltpu.VMEM((width, width), f32)] * 2,
        compiler_params=params,
        name="side_corr",
    )(at, norm_a, prev_b, next_b, prev_facts, next_facts, *wait_for)


def fan_kernel(keep_ref, got_ref, *refs):
    outs = refs[-4:]
    for slot in range(4):
        outs[slot][...] = keep_ref[slot] + got_ref[slot]


def fan(keep, got, wait_for=()):
    return pl.pallas_call(
        fan_kernel,
        in_specs=[vmem_spec, vmem_spec] + [any_spec] * len(wait_for),
        out_specs=[vmem_spec] * 4,
        out_shape=[shape(*keep.shape[1:])] * 4,
        compiler_params=params,
        name="fan",
    )(keep, got, *wait_for)


def total_kernel(count, *refs):
    out = refs[0][...]
    for ref in refs[1:count]:
        out = out + ref[...]
    refs[-2][...] = out


def total(parts, carried, wait_for=()):
    count = len(parts)
    return pl.pallas_call(
        functools.partial(total_kernel, count),
        in_specs=[vmem_spec] * count + [any_spec] * (1 + len(wait_for)),
        out_specs=[vmem_spec, any_spec],
        out_shape=[shape(*parts[0].shape), shape(*carried.shape)],
        input_output_aliases={count: 1},
        compiler_params=params,
        name="total",
    )(*parts, carried, *wait_for)


def halves_kernel(a_ref, b_ref, *refs):
    out = a_ref[...] + b_ref[...]
    rows = out.shape[0] // 2
    refs[-2][...] = out[:rows]
    refs[-1][...] = out[rows:]


def halves(mine, got, wait_for=()):
    rows, width = mine.shape
    return pl.pallas_call(
        halves_kernel,
        in_specs=[vmem_spec] * 2 + [any_spec] * len(wait_for),
        out_specs=[vmem_spec] * 2,
        out_shape=[shape(rows // 2, width)] * 2,
        compiler_params=params,
        name="halves",
    )(mine, got, *wait_for)


def pack_kernel(*refs):
    out_ref = refs[4 if len(refs) == 5 else 5]
    for i in range(4):
        out_ref[i] = refs[i][...]


def pack(parts, carried=None):
    rows, width = parts[0].shape
    more = [] if carried is None else [carried]
    out = pl.pallas_call(
        pack_kernel,
        in_specs=[vmem_spec] * 4 + [any_spec] * len(more),
        out_specs=[vmem_spec] + [any_spec] * len(more),
        out_shape=[shape(4, rows, width)] + [shape(*c.shape) for c in more],
        input_output_aliases={4: 1} if more else {},
        compiler_params=params,
        name="pack",
    )(*parts, *more)
    return out[0] if carried is None else out


def row_of(at_ref, core_flip, slot, rows):
    core, x = at_ref[0], at_ref[1]
    core = 1 - core if core_flip else core
    return pl.multiple_of((core * 4 + ((x - slot) & 3)) * rows, rows)


def own_grad_kernel(at_ref, mine_ref, other_ref, a_ref, b_ref, facts_ref, *refs):
    ga_ref, gb_ref, sums_ref, corr_ref, pt_ref, p_ref = refs[-6:]
    width = corr_ref.shape[0]

    @pl.when(pl.program_id(0) == 0)
    def _():
        rows = mine_ref.shape[1]
        for flip, ref in ((False, mine_ref), (True, other_ref)):
            for slot in range(4):
                corr_ref[pl.ds(row_of(at_ref, flip, slot, rows), rows), :] = ref[slot]
        corr = corr_ref[...]
        row_index = lax.broadcasted_iota(jnp.int32, corr.shape, 0)
        column = lax.broadcasted_iota(jnp.int32, corr.shape, 1)
        pen = jnp.where(row_index == column, -2.0 * (1.0 - corr), 2.0 * off_weight * corr)
        cross = pen * corr
        pen_t = pen.T
        high, low = split(pen)
        p_ref[0:width, :] = high
        p_ref[width : 2 * width, :] = low
        p_ref[2 * width :, :] = high
        high, low = split(pen_t)
        pt_ref[0:width, :] = high
        pt_ref[width : 2 * width, :] = low
        pt_ref[2 * width :, :] = high
        left = thrice(facts_ref[...])
        sums_ref[0:1, :] = mm(left, pt_ref[...])[5:6]
        sums_ref[1:2, :] = jnp.sum(cross.T, axis=0, keepdims=True)
        sums_ref[2:3, :] = mm(left, p_ref[...])[4:5]
        sums_ref[3:4, :] = jnp.sum(cross, axis=0, keepdims=True)
        sums_ref[4:8, :] = jnp.zeros((4, width), f32)

    norm_b = (b_ref[...] - facts_ref[2:3, :]) * facts_ref[3:4, :]
    ga_ref[...] = mm(thrice(norm_b), pt_ref[...])
    gb_ref[...] = mm(thrice(a_ref[...]), p_ref[...])


def own_grad(at, mine, other, norm_a, b, facts, wait_for=()):
    rows, width = b.shape
    steps = 4
    spec = pl.BlockSpec((rows // steps, width), lambda i: (i, 0))
    whole = pl.BlockSpec((8, width), lambda i: (0, 0))
    slots = pl.BlockSpec(mine.shape, lambda i: (0, 0, 0))
    return pl.pallas_call(
        own_grad_kernel,
        grid=(steps,),
        in_specs=[smem_spec, slots, slots, spec, spec, whole] + [any_spec] * len(wait_for),
        out_specs=[spec, spec, whole],
        out_shape=[shape(rows, width)] * 2 + [shape(8, width)],
        scratch_shapes=[
            pltpu.VMEM((width, width), f32),
            pltpu.VMEM((3 * width, width), bf16),
            pltpu.VMEM((3 * width, width), bf16),
        ],
        compiler_params=params,
        name="own_grad",
    )(at, mine, other, norm_a, b, facts, *wait_for)


def finish_kernel(at_ref, *refs):
    packs, refs = refs[:8], refs[8:]
    facts_ref, pf_ref, nf_ref, sums_ref = refs[:4]
    ga_ref, gb_ref, na_ref, b_ref, pb_ref, nb_ref, pa_ref, xa_ref = refs[4:12]
    out_a_ref, out_b_ref, corr_ref, pt_ref, p_ref, vec_ref = refs[12:]
    width = corr_ref.shape[1]

    @pl.when(pl.program_id(0) == 0)
    def _():
        rows = packs[0].shape[1]
        for flip in (0, 1):
            for slot in range(4):
                at = row_of(at_ref, flip == 1, slot, rows)
                for kind in range(4):
                    corr_ref[kind, pl.ds(at, rows), :] = packs[4 * flip + slot][kind]
        vec = sums_ref[0:4, :]
        cross_a = vec[1:2]
        cross_b = vec[3:4]
        for kind in range(4):
            corr = corr_ref[kind]
            corr = corr.T if kind < 2 else corr
            pen = 2.0 * off_weight * corr
            cross = jnp.sum(pen * corr, axis=0, keepdims=True)
            into = pt_ref if kind < 2 else p_ref
            first = (kind % 2) * 3 * width
            high, low = split(pen)
            into[first : first + width, :] = high
            into[first + width : first + 2 * width, :] = low
            into[first + 2 * width : first + 3 * width, :] = high
            if kind < 2:
                cross_a = cross_a + cross
            else:
                cross_b = cross_b + cross
        left = jnp.concatenate([thrice(pf_ref[...]), thrice(nf_ref[...])], axis=1)
        vec_ref[0:1, :] = vec[0:1] + mm(left, pt_ref[...])[5:6]
        vec_ref[1:2, :] = cross_a
        vec_ref[2:3, :] = vec[2:3] + mm(left, p_ref[...])[4:5]
        vec_ref[3:4, :] = cross_b

    prev_b = (pb_ref[...] - pf_ref[2:3, :]) * pf_ref[3:4, :]
    next_b = (nb_ref[...] - nf_ref[2:3, :]) * nf_ref[3:4, :]
    ga = ga_ref[...] + mm(jnp.concatenate([thrice(prev_b), thrice(next_b)], axis=1), pt_ref[...])
    out_a_ref[...] = (ga - vec_ref[0:1, :] - na_ref[...] * vec_ref[1:2, :]) * facts_ref[1:2, :]
    both = jnp.concatenate([thrice(pa_ref[...]), thrice(xa_ref[...])], axis=1)
    gb = gb_ref[...] + mm(both, p_ref[...])
    norm_b = (b_ref[...] - facts_ref[2:3, :]) * facts_ref[3:4, :]
    out_b_ref[...] = (gb - vec_ref[2:3, :] - norm_b * vec_ref[3:4, :]) * facts_ref[3:4, :]


def finish(at, packs, facts, prev_facts, next_facts, sums, tiles):
    rows, width = tiles[0].shape
    steps = 4
    spec = pl.BlockSpec((rows // steps, width), lambda i: (i, 0))
    whole = pl.BlockSpec((8, width), lambda i: (0, 0))
    slots = pl.BlockSpec(packs[0].shape, lambda i: (0, 0, 0))
    return pl.pallas_call(
        finish_kernel,
        grid=(steps,),
        in_specs=[smem_spec] + [slots] * 8 + [whole] * 4 + [spec] * 8,
        out_specs=[spec, spec],
        out_shape=[shape(rows, width)] * 2,
        scratch_shapes=[
            pltpu.VMEM((4, width, width), f32),
            pltpu.VMEM((6 * width, width), bf16),
            pltpu.VMEM((6 * width, width), bf16),
            pltpu.VMEM((8, width), f32),
        ],
        compiler_params=params,
        name="finish",
    )(at, *packs, facts, prev_facts, next_facts, sums, *tiles)


def per_device(view_a, view_b):
    local_rows, width = view_a.shape
    batch = local_rows * lax.axis_size("row")
    index = lax.axis_index("row")
    at = jnp.stack([index & 1, (index >> 1) & 3])
    half = local_rows // 2

    sums = sums_of(view_a, view_b)
    sums = sums + to_y(sums)
    prev_raw = across(view_b, 1)
    next_raw = across(view_b, -1)
    sums = sums + to_core(sums)
    parts = [sums] + [to_x(sums, shift) for shift in (1, 2, 3)]

    norm_a, facts, keep, send = own_corr(at, view_a, view_b, parts, batch)
    prev_facts = across(facts, 1)
    next_facts = across(facts, -1)
    slots = fan(keep, to_core(send))
    got = [slots[0]] + [to_x(slots[shift], shift) for shift in (1, 2, 3)]
    own_chunk, norm_a = total(got, norm_a)
    prev_a = across(norm_a, 1)
    next_a = across(norm_a, -1)
    own_chunk = own_chunk + to_y(own_chunk)
    own_slots = [own_chunk] + [to_x(own_chunk, shift) for shift in (1, 2, 3)]

    keep, send = side_corr(
        at, norm_a, prev_raw, next_raw, prev_facts, next_facts, batch, [own_chunk]
    )
    own_mine = pack(own_slots)
    slots = fan(keep, to_core(send), [own_mine])
    own_other = to_core(own_mine)
    got = [slots[0]] + [to_x(slots[shift], shift) for shift in (1, 2, 3)]
    side_chunk, own_other = total(got, own_other)
    back = to_y(side_chunk)
    part_a, part_b, own_sums = own_grad(at, own_mine, own_other, norm_a, view_b, facts)
    left, right = halves(side_chunk, back, [own_sums])
    from_next = across(left, -1)
    from_prev = across(right, 1)
    packed = pack([left, right, from_prev, from_next])
    mine = [packed] + [to_x(packed, shift) for shift in (1, 2, 3)]
    other = [to_core(block) for block in mine]
    tiles = [part_a, part_b, norm_a, view_b, prev_raw, next_raw, prev_a, next_a]
    return tuple(
        finish(at, mine + other, facts, prev_facts, next_facts, own_sums, tiles)
    )


def solution(mesh):
    placed = (P("row", "grp"), P("row", "grp"))
    return jax.shard_map(
        per_device,
        mesh=mesh,
        in_specs=placed,
        out_specs=(P("row", "grp"), P("row", "grp")),
        check_vma=False,
    )
```

```python
import functools

import jax
import jax.numpy as jnp
from jax import lax
from jax.experimental import pallas as pl
from jax.experimental.pallas import tpu as pltpu
from jax.sharding import PartitionSpec as P

epsilon = 1e-05
off_weight = 0.0051
f32 = jnp.float32
bf16 = jnp.bfloat16


any_spec = pl.BlockSpec(memory_space=pl.ANY)
smem_spec = pl.BlockSpec(memory_space=pltpu.SMEM)
vmem_spec = pl.BlockSpec(memory_space=pltpu.VMEM)
params = pltpu.CompilerParams(vmem_limit_bytes=48 * 1024 * 1024)
cheap = pl.CostEstimate(flops=1, transcendentals=0, bytes_accessed=1)
call = functools.partial(pl.pallas_call, compiler_params=params, cost_estimate=cheap)
top_rows = 384


def shape(*dims):
    return jax.ShapeDtypeStruct(dims, f32)


def across(block, shift):
    count = lax.axis_size("grp")
    return lax.ppermute(block, "grp", [(i, (i + shift) % count) for i in range(count)])


def to_core(block):
    return lax.ppermute(block, "row", [(i, i ^ 1) for i in range(16)])


def to_y(block):
    return lax.ppermute(block, "row", [(i, i ^ 8) for i in range(16)])


def to_x(block, shift):
    pairs = [(i, (i & 9) | ((((i >> 1) + shift) & 3) << 1)) for i in range(16)]
    return lax.ppermute(block, "row", pairs)


def split(value):
    high = value.astype(bf16)
    return high, (value - high.astype(f32)).astype(bf16)


def mm(a, b):
    return lax.dot_general(a, b, (((1,), (0,)), ((), ())), preferred_element_type=f32)


def gram(a, b):
    a_high, a_low = split(a.T)
    b_high, b_low = split(b)
    return mm(
        jnp.concatenate([a_high, a_high, a_low], axis=1),
        jnp.concatenate([b_high, b_low, b_high], axis=0),
    )


def thrice(value):
    high, low = split(value)
    return jnp.concatenate([high, high, low], axis=1)


def sums_kernel(a_ref, b_ref, out_ref):
    @pl.when(pl.program_id(0) == 0)
    def _():
        out_ref[...] = jnp.zeros_like(out_ref)

    a, b = a_ref[...], b_ref[...]
    for row, value in enumerate((a, a * a, b, b * b)):
        out_ref[row : row + 1, :] += jnp.sum(value, axis=0, keepdims=True)


def sums_of(a, b):
    rows, width = a.shape
    tile = rows // 4
    spec = pl.BlockSpec((tile, width), lambda i: (i, 0))
    return call(
        sums_kernel,
        grid=(4,),
        in_specs=[spec, spec],
        out_specs=pl.BlockSpec((8, width), lambda i: (0, 0)),
        out_shape=shape(8, width),
        name="sums",
    )(a, b)


def put_slots(at_ref, acc, keep_ref, send_ref, first, rows):
    core, x = at_ref[0], at_ref[1]
    for slot in range(4):
        chunk = (x + slot) & 3
        mine = pl.multiple_of((core * 4 + chunk) * rows, rows)
        theirs = pl.multiple_of(((1 - core) * 4 + chunk) * rows, rows)
        keep_ref[slot, first : first + rows, :] = acc[pl.ds(mine, rows), :]
        send_ref[slot, first : first + rows, :] = acc[pl.ds(theirs, rows), :]


def own_corr_kernel(half_rows, steps, top_steps, at_ref, a_ref, b_ref, *refs):
    parts, (top_ref, low_ref, facts_ref, keep_ref, send_ref, acc_ref) = refs[:4], refs[4:]
    step = pl.program_id(0)

    @pl.when(step == 0)
    def _():
        total = parts[0][...] + parts[1][...] + parts[2][...] + parts[3][...]
        total = total / half_rows
        for view in (0, 1):
            mean, square = total[2 * view : 2 * view + 1], total[2 * view + 1 : 2 * view + 2]
            scale = jnp.sqrt(square - mean * mean + epsilon)
            facts_ref[2 * view : 2 * view + 1, :] = mean
            facts_ref[2 * view + 1 : 2 * view + 2, :] = 1.0 / scale
            facts_ref[4 + view : 5 + view, :] = square
            facts_ref[6 + view : 7 + view, :] = scale
        acc_ref[...] = jnp.zeros_like(acc_ref)

    norm_a = (a_ref[...] - facts_ref[0:1, :]) * facts_ref[1:2, :]
    norm_b = (b_ref[...] - facts_ref[2:3, :]) * facts_ref[3:4, :]

    @pl.when(step < top_steps)
    def _():
        top_ref[...] = norm_a

    @pl.when(step >= top_steps)
    def _():
        low_ref[...] = norm_a

    acc_ref[...] += gram(norm_a, norm_b)

    @pl.when(step == steps - 1)
    def _():
        put_slots(at_ref, acc_ref, keep_ref, send_ref, 0, keep_ref.shape[1])


def own_corr(at, a, b, parts, half_rows):
    rows, width = a.shape
    tile = 128
    steps, top_steps = rows // tile, top_rows // tile
    spec = pl.BlockSpec((tile, width), lambda i: (i, 0))
    top_spec = pl.BlockSpec((tile, width), lambda i: (jnp.minimum(i, top_steps - 1), 0))
    low_spec = pl.BlockSpec((tile, width), lambda i: (jnp.maximum(i - top_steps, 0), 0))
    whole = pl.BlockSpec((8, width), lambda i: (0, 0))
    slots = pl.BlockSpec((4, width // 8, width), lambda i: (0, 0, 0))
    return call(
        functools.partial(own_corr_kernel, half_rows, steps, top_steps),
        grid=(steps,),
        in_specs=[smem_spec, spec, spec] + [whole] * 4,
        out_specs=[top_spec, low_spec, whole, slots, slots],
        out_shape=[shape(top_rows, width), shape(rows - top_rows, width), shape(8, width)]
        + [shape(4, width // 8, width)] * 2,
        scratch_shapes=[pltpu.VMEM((width, width), f32)],
        name="own_corr",
    )(at, a, b, *parts)


def side_corr_kernel(steps, at_ref, a_ref, prev_ref, next_ref, f_ref, pf_ref, nf_ref, *refs):
    keep_ref, send_ref, left_ref, right_ref = refs[-4:]
    step = pl.program_id(0)

    @pl.when(step == 0)
    def _():
        left_ref[...] = jnp.zeros_like(left_ref)
        right_ref[...] = jnp.zeros_like(right_ref)

    norm_a = (a_ref[...] - f_ref[0:1, :]) * f_ref[1:2, :]
    for acc_ref, b_ref, facts_ref in ((left_ref, prev_ref, pf_ref), (right_ref, next_ref, nf_ref)):
        norm_b = (b_ref[...] - facts_ref[2:3, :]) * facts_ref[3:4, :]
        acc_ref[...] += gram(norm_a, norm_b)

    @pl.when(step == steps - 1)
    def _():
        rows = keep_ref.shape[1] // 2
        put_slots(at_ref, left_ref, keep_ref, send_ref, 0, rows)
        put_slots(at_ref, right_ref, keep_ref, send_ref, rows, rows)


def side_corr(at, a, prev_b, next_b, facts, prev_facts, next_facts, wait_for):
    rows, width = a.shape
    steps = 4
    spec = pl.BlockSpec((rows // steps, width), lambda i: (i, 0))
    whole = pl.BlockSpec((8, width), lambda i: (0, 0))
    slots = pl.BlockSpec((4, width // 4, width), lambda i: (0, 0, 0))
    return call(
        functools.partial(side_corr_kernel, steps),
        grid=(steps,),
        in_specs=[smem_spec, spec, spec, spec] + [whole] * 3 + [any_spec] * len(wait_for),
        out_specs=[slots, slots],
        out_shape=[shape(4, width // 4, width)] * 2,
        scratch_shapes=[pltpu.VMEM((width, width), f32)] * 2,
        name="side_corr",
    )(at, a, prev_b, next_b, facts, prev_facts, next_facts, *wait_for)


def fan_kernel(keep_ref, got_ref, *refs):
    outs = refs[-4:]
    for slot in range(4):
        outs[slot][...] = keep_ref[slot] + got_ref[slot]


def fan(keep, got):
    return call(
        fan_kernel,
        in_specs=[vmem_spec, vmem_spec],
        out_specs=[vmem_spec] * 4,
        out_shape=[shape(*keep.shape[1:])] * 4,
        name="fan",
    )(keep, got)


def message_kernel(extra, *refs):
    out_ref = refs[4 + extra]
    rows = refs[0].shape[0]
    out_ref[0:rows, :] = refs[0][...] + refs[1][...] + refs[2][...] + refs[3][...]
    for i in range(extra):
        out_ref[rows + 8 * i : rows + 8 * i + 8, :] = refs[4 + i][...]


def message(parts, facts, carried=None):
    rows, width = parts[0].shape
    more = [] if carried is None else [carried]
    count = 4 + len(facts)

    def kernel(*refs):
        message_kernel(len(facts), *refs[:count], refs[count + len(more)])

    return call(
        kernel,
        in_specs=[vmem_spec] * count + [any_spec] * len(more),
        out_specs=[vmem_spec] + [any_spec] * len(more),
        out_shape=[shape(rows + 8 * len(facts), width)] + [shape(*c.shape) for c in more],
        input_output_aliases={count: 1} if more else {},
        name="message",
    )(*parts, *facts, *more)


def full_facts(mine, other):
    rows = []
    for view in (0, 1):
        mean = 0.5 * (mine[2 * view : 2 * view + 1] + other[2 * view : 2 * view + 1])
        square = 0.5 * (mine[4 + view : 5 + view] + other[4 + view : 5 + view])
        rows += [mean, 1.0 / jnp.sqrt(square - mean * mean + epsilon)]
    for view in (0, 1):
        average = 0.5 * (mine[2 * view : 2 * view + 1] + other[2 * view : 2 * view + 1])
        rows.append((average - rows[2 * view]) * rows[2 * view + 1])
    rows += [mine[6:7] * rows[1], (mine[0:1] - rows[0]) * rows[1]]
    return rows


def merged(mine, other, a_cols, b_mine, b_other, b_full, half_rows):
    scale0, scale1, diff0, diff1, inverse = (a_cols[:, i : i + 1] for i in range(5))
    out = mine * (scale0 * b_mine[7:8]) + other * (scale1 * b_other[7:8])
    shift0, shift1 = b_mine[2:3] - b_full[2], b_other[2:3] - b_full[2]
    out = out + half_rows * (diff0 * shift0 + diff1 * shift1)
    return out * (inverse * (b_full[3] * (0.5 / half_rows)))


def columns_of(at_ref, mine, other, full, cols_ref, rows):
    width = mine.shape[1]
    stack = [mine[6:7], other[6:7], mine[0:1] - full[0], other[0:1] - full[0], full[1]]
    stack = jnp.concatenate(stack + [jnp.zeros((123, width), f32)], axis=0)
    cols_ref[...] = stack.T
    first = pl.multiple_of((at_ref[0] * 4 + at_ref[1]) * rows, rows)
    return cols_ref[pl.ds(first, rows), :]


def own_merge_kernel(half_rows, at_ref, mine_ref, got_ref, _, chunk_ref, full_ref, __, cols_ref):
    rows = chunk_ref.shape[0]
    mine, other = mine_ref[rows:, :], got_ref[rows:, :]
    full = full_facts(mine, other)
    for i in range(8):
        full_ref[i : i + 1, :] = full[i]
    cols = columns_of(at_ref, mine, other, full, cols_ref, rows)
    chunk_ref[...] = merged(
        mine_ref[0:rows, :], got_ref[0:rows, :], cols, mine, other, full, half_rows
    )


def own_merge(at, mine, got, carried, half_rows):
    rows, width = mine.shape
    return call(
        functools.partial(own_merge_kernel, half_rows),
        in_specs=[smem_spec, vmem_spec, vmem_spec, any_spec],
        out_specs=[vmem_spec, vmem_spec, any_spec],
        out_shape=[shape(rows - 8, width), shape(8, width), shape(*carried.shape)],
        input_output_aliases={3: 2},
        scratch_shapes=[pltpu.VMEM((width, 128), f32)],
        name="own_merge",
    )(at, mine, got, carried)


def side_merge_kernel(half_rows, at_ref, mine_ref, got_ref, own_ref, own_got_ref, *refs):
    left_ref, right_ref, pf_ref, nf_ref, cols_ref = refs[-5:]
    rows = left_ref.shape[0]
    mine, other = own_ref[rows:, :], own_got_ref[rows:, :]
    cols = columns_of(at_ref, mine, other, full_facts(mine, other), cols_ref, rows)
    for side, (out_ref, facts_ref) in enumerate(((left_ref, pf_ref), (right_ref, nf_ref))):
        first = side * rows
        fact = 2 * rows + 8 * side
        b_mine, b_other = mine_ref[fact : fact + 8, :], got_ref[fact : fact + 8, :]
        full = full_facts(b_mine, b_other)
        for i in range(8):
            facts_ref[i : i + 1, :] = full[i]
        out_ref[...] = merged(
            mine_ref[first : first + rows, :],
            got_ref[first : first + rows, :],
            cols,
            b_mine,
            b_other,
            full,
            half_rows,
        )


def side_merge(at, mine, got, own, own_got, half_rows, wait_for):
    rows, width = own.shape
    return call(
        functools.partial(side_merge_kernel, half_rows),
        in_specs=[smem_spec] + [vmem_spec] * 4 + [any_spec] * len(wait_for),
        out_specs=[vmem_spec] * 4,
        out_shape=[shape(rows - 8, width)] * 2 + [shape(8, width)] * 2,
        scratch_shapes=[pltpu.VMEM((width, 128), f32)],
        name="side_merge",
    )(at, mine, got, own, own_got, *wait_for)


def pack(parts, carried=None, wait_for=()):
    rows, width = parts[0].shape
    more = [] if carried is None else [carried]
    at_out = 4 + len(more) + len(wait_for)

    def kernel(*refs):
        for i in range(4):
            refs[at_out][i] = refs[i][...]

    out = call(
        kernel,
        in_specs=[vmem_spec] * 4 + [any_spec] * (len(more) + len(wait_for)),
        out_specs=[vmem_spec] + [any_spec] * len(more),
        out_shape=[shape(4, rows, width)] + [shape(*c.shape) for c in more],
        input_output_aliases={4: 1} if more else {},
        name="pack",
    )(*parts, *more, *wait_for)
    return out[0] if carried is None else out


def row_of(at_ref, core_flip, slot, rows):
    core, x = at_ref[0], at_ref[1]
    core = 1 - core if core_flip else core
    return pl.multiple_of((core * 4 + ((x - slot) & 3)) * rows, rows)


def own_grad_kernel(at_ref, mine_ref, other_ref, a_ref, b_ref, facts_ref, *refs):
    ga_ref, gb_ref, sums_ref, corr_ref, pt_ref, p_ref = refs[-6:]
    width = corr_ref.shape[0]

    @pl.when(pl.program_id(0) == 0)
    def _():
        rows = mine_ref.shape[1]
        for flip, ref in ((False, mine_ref), (True, other_ref)):
            for slot in range(4):
                corr_ref[pl.ds(row_of(at_ref, flip, slot, rows), rows), :] = ref[slot]
        corr = corr_ref[...]
        row_index = lax.broadcasted_iota(jnp.int32, corr.shape, 0)
        column = lax.broadcasted_iota(jnp.int32, corr.shape, 1)
        pen = jnp.where(row_index == column, -2.0 * (1.0 - corr), 2.0 * off_weight * corr)
        cross = pen * corr
        pen_t = pen.T
        high, low = split(pen)
        p_ref[0:width, :] = high
        p_ref[width : 2 * width, :] = low
        p_ref[2 * width :, :] = high
        high, low = split(pen_t)
        pt_ref[0:width, :] = high
        pt_ref[width : 2 * width, :] = low
        pt_ref[2 * width :, :] = high
        left = thrice(facts_ref[...])
        sums_ref[0:1, :] = mm(left, pt_ref[...])[5:6]
        sums_ref[1:2, :] = jnp.sum(cross.T, axis=0, keepdims=True)
        sums_ref[2:3, :] = mm(left, p_ref[...])[4:5]
        sums_ref[3:4, :] = jnp.sum(cross, axis=0, keepdims=True)
        sums_ref[4:8, :] = jnp.zeros((4, width), f32)

    norm_b = (b_ref[...] - facts_ref[2:3, :]) * facts_ref[3:4, :]
    ga_ref[...] = mm(thrice(norm_b), pt_ref[...])
    norm_a = (a_ref[...] - facts_ref[0:1, :]) * facts_ref[1:2, :]
    gb_ref[...] = mm(thrice(norm_a), p_ref[...])


def own_grad(at, mine, other, a, b, facts):
    rows, width = b.shape
    steps = 4
    spec = pl.BlockSpec((rows // steps, width), lambda i: (i, 0))
    whole = pl.BlockSpec((8, width), lambda i: (0, 0))
    slots = pl.BlockSpec(mine.shape, lambda i: (0, 0, 0))
    return call(
        own_grad_kernel,
        grid=(steps,),
        in_specs=[smem_spec, slots, slots, spec, spec, whole],
        out_specs=[spec, spec, whole],
        out_shape=[shape(rows, width)] * 2 + [shape(8, width)],
        scratch_shapes=[
            pltpu.VMEM((width, width), f32),
            pltpu.VMEM((3 * width, width), bf16),
            pltpu.VMEM((3 * width, width), bf16),
        ],
        name="own_grad",
    )(at, mine, other, a, b, facts)


def prep_kernel(at_ref, *refs):
    packs, refs = refs[:8], refs[8:]
    pf_ref, nf_ref, sums_ref, pt_ref, p_ref, vec_ref, corr_ref = refs
    width = corr_ref.shape[1]
    rows = packs[0].shape[1]
    for flip in (0, 1):
        for slot in range(4):
            at = row_of(at_ref, flip == 1, slot, rows)
            for kind in range(4):
                corr_ref[kind, pl.ds(at, rows), :] = packs[4 * flip + slot][kind]
    vec = sums_ref[0:4, :]
    cross_a = vec[1:2]
    cross_b = vec[3:4]
    for kind in range(4):
        corr = corr_ref[kind]
        corr = corr.T if kind < 2 else corr
        pen = 2.0 * off_weight * corr
        cross = jnp.sum(pen * corr, axis=0, keepdims=True)
        into = pt_ref if kind < 2 else p_ref
        first = (kind % 2) * 3 * width
        high, low = split(pen)
        into[first : first + width, :] = high
        into[first + width : first + 2 * width, :] = low
        into[first + 2 * width : first + 3 * width, :] = high
        if kind < 2:
            cross_a = cross_a + cross
        else:
            cross_b = cross_b + cross
    left = jnp.concatenate([thrice(pf_ref[...]), thrice(nf_ref[...])], axis=1)
    vec_ref[0:1, :] = vec[0:1] + mm(left, pt_ref[...])[5:6]
    vec_ref[1:2, :] = cross_a
    vec_ref[2:3, :] = vec[2:3] + mm(left, p_ref[...])[4:5]
    vec_ref[3:4, :] = cross_b
    vec_ref[4:8, :] = jnp.zeros((4, width), f32)


def prep(at, packs, prev_facts, next_facts, sums):
    width = sums.shape[1]
    return call(
        prep_kernel,
        in_specs=[smem_spec] + [vmem_spec] * 11,
        out_specs=[vmem_spec] * 3,
        out_shape=[jax.ShapeDtypeStruct((6 * width, width), bf16)] * 2 + [shape(8, width)],
        scratch_shapes=[pltpu.VMEM((4, width, width), f32)],
        name="prep",
    )(at, *packs, prev_facts, next_facts, sums)


def finish_kernel(pt_ref, p_ref, vec_ref, f_ref, pf_ref, nf_ref, *refs):
    ga_ref, gb_ref, a_ref, b_ref, pb_ref, nb_ref, pa_ref, xa_ref = refs[:8]
    out_a_ref, out_b_ref = refs[-2:]
    prev_b = (pb_ref[...] - pf_ref[2:3, :]) * pf_ref[3:4, :]
    next_b = (nb_ref[...] - nf_ref[2:3, :]) * nf_ref[3:4, :]
    ga = ga_ref[...] + mm(jnp.concatenate([thrice(prev_b), thrice(next_b)], axis=1), pt_ref[...])
    norm_a = (a_ref[...] - f_ref[0:1, :]) * f_ref[1:2, :]
    out_a_ref[...] = (ga - vec_ref[0:1, :] - norm_a * vec_ref[1:2, :]) * f_ref[1:2, :]
    prev_a = pa_ref[...] * pf_ref[6:7, :] + pf_ref[7:8, :]
    next_a = xa_ref[...] * nf_ref[6:7, :] + nf_ref[7:8, :]
    gb = gb_ref[...] + mm(jnp.concatenate([thrice(prev_a), thrice(next_a)], axis=1), p_ref[...])
    norm_b = (b_ref[...] - f_ref[2:3, :]) * f_ref[3:4, :]
    out_b_ref[...] = (gb - vec_ref[2:3, :] - norm_b * vec_ref[3:4, :]) * f_ref[3:4, :]


def finish(first, tile, mats, facts, whole_tiles, halo_tiles, partial=()):
    rows, width = whole_tiles[0].shape
    steps = halo_tiles[0].shape[0] // tile
    at = pl.BlockSpec((pl.Element(tile), pl.Element(width)), lambda i: (pl.multiple_of(first + i * tile, 64), 0))
    halo = pl.BlockSpec((tile, width), lambda i: (i, 0))
    whole = pl.BlockSpec((8, width), lambda i: (0, 0))
    mat = pl.BlockSpec(mats[0].shape, lambda i: (0, 0))
    count = 6 + 8
    return call(
        finish_kernel,
        grid=(steps,),
        in_specs=[mat, mat] + [whole] * 4 + [at] * 6 + [halo] * 2 + [any_spec] * len(partial),
        out_specs=[at, at],
        out_shape=[shape(rows, width)] * 2,
        input_output_aliases={count: 0, count + 1: 1} if partial else {},
        name="finish",
    )(*mats, *facts, *whole_tiles, *halo_tiles, *partial)


def per_device(view_a, view_b):
    local_rows, width = view_a.shape
    half_rows = local_rows * lax.axis_size("row") // 2
    index = lax.axis_index("row")
    at = jnp.stack([index & 1, (index >> 1) & 3])

    prev_raw = across(view_b, 1)
    next_raw = across(view_b, -1)
    sums = sums_of(view_a, view_b)
    sums = sums + to_core(sums)
    parts = [sums] + [to_x(sums, shift) for shift in (1, 2, 3)]

    a_top, a_low, half_facts, keep, send = own_corr(at, view_a, view_b, parts, half_rows)
    prev_half = across(half_facts, 1)
    next_half = across(half_facts, -1)
    slots = fan(keep, to_core(send))
    got = [slots[0]] + [to_x(slots[shift], shift) for shift in (1, 2, 3)]
    (own_mine,) = message(got, [half_facts])
    own_got = to_y(own_mine)
    own_chunk, facts, a_top = own_merge(at, own_mine, own_got, a_top, half_rows)
    prev_top = across(a_top, 1)
    next_top = across(a_top, -1)

    keep, send = side_corr(
        at, view_a, prev_raw, next_raw, half_facts, prev_half, next_half, [own_chunk]
    )
    slots = fan(keep, to_core(send))
    got = [slots[0]] + [to_x(slots[shift], shift) for shift in (1, 2, 3)]
    side_mine, own_chunk = message(got, [prev_half, next_half], own_chunk)
    own_slots = [own_chunk] + [to_x(own_chunk, shift) for shift in (1, 2, 3)]
    left, right, prev_facts, next_facts = side_merge(
        at, side_mine, to_y(side_mine), own_mine, own_got, half_rows, [prev_top, next_top]
    )
    from_next = across(left, -1)
    from_prev = across(right, 1)
    own_pack = pack(own_slots, None, [left])
    own_other = to_core(own_pack)
    packed, a_low = pack([left, right, from_prev, from_next], a_low, [own_other])
    prev_low = across(a_low, 1)
    next_low = across(a_low, -1)
    mine = [packed] + [to_x(packed, shift) for shift in (1, 2, 3)]
    part_a, part_b, own_sums = own_grad(at, own_pack, own_other, view_a, view_b, facts)
    other = [to_core(block) for block in mine]
    mats = prep(at, mine + other, prev_facts, next_facts, own_sums)
    all_facts = [facts, prev_facts, next_facts]
    whole = [part_a, part_b, view_a, view_b, prev_raw, next_raw]
    done = finish(0, top_rows, mats, all_facts, whole, [prev_top, next_top])
    low = (local_rows - top_rows) // 2
    return tuple(finish(top_rows, low, mats, all_facts, whole, [prev_low, next_low], done))


def solution(mesh):
    placed = (P("row", "grp"), P("row", "grp"))
    return jax.shard_map(
        per_device,
        mesh=mesh,
        in_specs=placed,
        out_specs=(P("row", "grp"), P("row", "grp")),
        check_vma=False,
    )
```

```python
import functools

import jax
import jax.numpy as jnp
from jax import lax
from jax.experimental import pallas as pl
from jax.experimental.pallas import tpu as pltpu
from jax.sharding import PartitionSpec as P

epsilon = 1e-05
off_weight = 0.0051
f32 = jnp.float32
bf16 = jnp.bfloat16


any_spec = pl.BlockSpec(memory_space=pl.ANY)
smem_spec = pl.BlockSpec(memory_space=pltpu.SMEM)
vmem_spec = pl.BlockSpec(memory_space=pltpu.VMEM)
cheap = pl.CostEstimate(flops=1, transcendentals=0, bytes_accessed=1)
top_rows = 256


def call(kernel, mib=8, **rest):
    params = pltpu.CompilerParams(vmem_limit_bytes=mib * 1024 * 1024)
    return pl.pallas_call(kernel, compiler_params=params, cost_estimate=cheap, **rest)


def shape(*dims):
    return jax.ShapeDtypeStruct(dims, f32)


def across(block, shift):
    count = lax.axis_size("grp")
    return lax.ppermute(block, "grp", [(i, (i + shift) % count) for i in range(count)])


def to_core(block):
    return lax.ppermute(block, "row", [(i, i ^ 1) for i in range(16)])


def to_y(block):
    return lax.ppermute(block, "row", [(i, i ^ 8) for i in range(16)])


def to_x(block, shift):
    pairs = [(i, (i & 9) | ((((i >> 1) + shift) & 3) << 1)) for i in range(16)]
    return lax.ppermute(block, "row", pairs)


def split(value):
    high = value.astype(bf16)
    return high, (value - high.astype(f32)).astype(bf16)


def mm(a, b):
    return lax.dot_general(a, b, (((1,), (0,)), ((), ())), preferred_element_type=f32)


def gram(a, b):
    a_high, a_low = split(a.T)
    b_high, b_low = split(b)
    return mm(
        jnp.concatenate([a_high, a_high, a_low], axis=1),
        jnp.concatenate([b_high, b_low, b_high], axis=0),
    )


def thrice(value):
    high, low = split(value)
    return jnp.concatenate([high, high, low], axis=1)


def sums_kernel(a_ref, b_ref, out_ref):
    @pl.when(pl.program_id(0) == 0)
    def _():
        out_ref[...] = jnp.zeros_like(out_ref)

    a, b = a_ref[...], b_ref[...]
    for row, value in enumerate((a, a * a, b, b * b)):
        out_ref[row : row + 1, :] += jnp.sum(value, axis=0, keepdims=True)


def sums_of(a, b):
    rows, width = a.shape
    tile = rows // 4
    spec = pl.BlockSpec((tile, width), lambda i: (i, 0))
    return call(
        sums_kernel,
        grid=(4,),
        in_specs=[spec, spec],
        out_specs=pl.BlockSpec((8, width), lambda i: (0, 0)),
        out_shape=shape(8, width),
        name="sums",
    )(a, b)


def put_slots(at_ref, acc, keep_ref, send_ref, first, rows):
    core, x = at_ref[0], at_ref[1]
    for slot in range(4):
        chunk = (x + slot) & 3
        mine = pl.multiple_of((core * 4 + chunk) * rows, rows)
        theirs = pl.multiple_of(((1 - core) * 4 + chunk) * rows, rows)
        keep_ref[slot, first : first + rows, :] = acc[pl.ds(mine, rows), :]
        send_ref[slot, first : first + rows, :] = acc[pl.ds(theirs, rows), :]


def own_corr_kernel(half_rows, steps, top_steps, at_ref, a_ref, b_ref, *refs):
    parts, (top_ref, low_ref, facts_ref, keep_ref, send_ref, acc_ref) = refs[:4], refs[4:]
    step = pl.program_id(0)

    @pl.when(step == 0)
    def _():
        total = parts[0][...] + parts[1][...] + parts[2][...] + parts[3][...]
        total = total / half_rows
        for view in (0, 1):
            mean, square = total[2 * view : 2 * view + 1], total[2 * view + 1 : 2 * view + 2]
            scale = jnp.sqrt(square - mean * mean + epsilon)
            facts_ref[2 * view : 2 * view + 1, :] = mean
            facts_ref[2 * view + 1 : 2 * view + 2, :] = 1.0 / scale
            facts_ref[4 + view : 5 + view, :] = square
            facts_ref[6 + view : 7 + view, :] = scale
        acc_ref[...] = jnp.zeros_like(acc_ref)

    norm_a = (a_ref[...] - facts_ref[0:1, :]) * facts_ref[1:2, :]
    norm_b = (b_ref[...] - facts_ref[2:3, :]) * facts_ref[3:4, :]

    @pl.when(step < top_steps)
    def _():
        top_ref[...] = norm_a

    @pl.when(step >= top_steps)
    def _():
        low_ref[...] = norm_a

    acc_ref[...] += gram(norm_a, norm_b)

    @pl.when(step == steps - 1)
    def _():
        put_slots(at_ref, acc_ref, keep_ref, send_ref, 0, keep_ref.shape[1])


def own_corr(at, a, b, parts, half_rows):
    rows, width = a.shape
    tile = 256
    steps, top_steps = rows // tile, top_rows // tile
    spec = pl.BlockSpec((tile, width), lambda i: (i, 0))
    top_spec = pl.BlockSpec((tile, width), lambda i: (jnp.minimum(i, top_steps - 1), 0))
    low_spec = pl.BlockSpec((tile, width), lambda i: (jnp.maximum(i - top_steps, 0), 0))
    whole = pl.BlockSpec((8, width), lambda i: (0, 0))
    slots = pl.BlockSpec((4, width // 8, width), lambda i: (0, 0, 0))
    return call(
        functools.partial(own_corr_kernel, half_rows, steps, top_steps),
        grid=(steps,),
        in_specs=[smem_spec, spec, spec] + [whole] * 4,
        out_specs=[top_spec, low_spec, whole, slots, slots],
        out_shape=[shape(top_rows, width), shape(rows - top_rows, width), shape(8, width)]
        + [shape(4, width // 8, width)] * 2,
        scratch_shapes=[pltpu.VMEM((width, width), f32)],
        mib=16,
        name="own_corr",
    )(at, a, b, *parts)


def side_corr_kernel(steps, at_ref, a_ref, prev_ref, next_ref, f_ref, pf_ref, nf_ref, *refs):
    keep_ref, send_ref, left_ref, right_ref = refs[-4:]
    step = pl.program_id(0)

    @pl.when(step == 0)
    def _():
        left_ref[...] = jnp.zeros_like(left_ref)
        right_ref[...] = jnp.zeros_like(right_ref)

    norm_a = (a_ref[...] - f_ref[0:1, :]) * f_ref[1:2, :]
    for acc_ref, b_ref, facts_ref in ((left_ref, prev_ref, pf_ref), (right_ref, next_ref, nf_ref)):
        norm_b = (b_ref[...] - facts_ref[2:3, :]) * facts_ref[3:4, :]
        acc_ref[...] += gram(norm_a, norm_b)

    @pl.when(step == steps - 1)
    def _():
        rows = keep_ref.shape[1] // 2
        put_slots(at_ref, left_ref, keep_ref, send_ref, 0, rows)
        put_slots(at_ref, right_ref, keep_ref, send_ref, rows, rows)


def side_corr(at, a, prev_b, next_b, facts, prev_facts, next_facts, wait_for):
    rows, width = a.shape
    steps = 4
    spec = pl.BlockSpec((rows // steps, width), lambda i: (i, 0))
    whole = pl.BlockSpec((8, width), lambda i: (0, 0))
    slots = pl.BlockSpec((4, width // 4, width), lambda i: (0, 0, 0))
    return call(
        functools.partial(side_corr_kernel, steps),
        grid=(steps,),
        in_specs=[smem_spec, spec, spec, spec] + [whole] * 3 + [any_spec] * len(wait_for),
        out_specs=[slots, slots],
        out_shape=[shape(4, width // 4, width)] * 2,
        scratch_shapes=[pltpu.VMEM((width, width), f32)] * 2,
        mib=24,
        name="side_corr",
    )(at, a, prev_b, next_b, facts, prev_facts, next_facts, *wait_for)


def fan_kernel(keep_ref, got_ref, *refs):
    outs = refs[-4:]
    for slot in range(4):
        outs[slot][...] = keep_ref[slot] + got_ref[slot]


def fan(keep, got):
    return call(
        fan_kernel,
        in_specs=[vmem_spec, vmem_spec],
        out_specs=[vmem_spec] * 4,
        out_shape=[shape(*keep.shape[1:])] * 4,
        name="fan",
    )(keep, got)


def message_kernel(extra, *refs):
    out_ref = refs[4 + extra]
    rows = refs[0].shape[0]
    out_ref[0:rows, :] = refs[0][...] + refs[1][...] + refs[2][...] + refs[3][...]
    for i in range(extra):
        out_ref[rows + 8 * i : rows + 8 * i + 8, :] = refs[4 + i][...]


def message(parts, facts, carried=None):
    rows, width = parts[0].shape
    more = [] if carried is None else [carried]
    count = 4 + len(facts)

    def kernel(*refs):
        message_kernel(len(facts), *refs[:count], refs[count + len(more)])

    return call(
        kernel,
        in_specs=[vmem_spec] * count + [any_spec] * len(more),
        out_specs=[vmem_spec] + [any_spec] * len(more),
        out_shape=[shape(rows + 8 * len(facts), width)] + [shape(*c.shape) for c in more],
        input_output_aliases={count: 1} if more else {},
        name="message",
    )(*parts, *facts, *more)


def full_facts(mine, other):
    rows = []
    for view in (0, 1):
        mean = 0.5 * (mine[2 * view : 2 * view + 1] + other[2 * view : 2 * view + 1])
        square = 0.5 * (mine[4 + view : 5 + view] + other[4 + view : 5 + view])
        rows += [mean, 1.0 / jnp.sqrt(square - mean * mean + epsilon)]
    for view in (0, 1):
        average = 0.5 * (mine[2 * view : 2 * view + 1] + other[2 * view : 2 * view + 1])
        rows.append((average - rows[2 * view]) * rows[2 * view + 1])
    rows += [mine[6:7] * rows[1], (mine[0:1] - rows[0]) * rows[1]]
    return rows


def merged(mine, other, a_cols, b_mine, b_other, b_full, half_rows):
    scale0, scale1, diff0, diff1, inverse = (a_cols[:, i : i + 1] for i in range(5))
    out = mine * (scale0 * b_mine[7:8]) + other * (scale1 * b_other[7:8])
    shift0, shift1 = b_mine[2:3] - b_full[2], b_other[2:3] - b_full[2]
    out = out + half_rows * (diff0 * shift0 + diff1 * shift1)
    return out * (inverse * (b_full[3] * (0.5 / half_rows)))


def columns_of(at_ref, mine, other, full, cols_ref, rows):
    width = mine.shape[1]
    stack = [mine[6:7], other[6:7], mine[0:1] - full[0], other[0:1] - full[0], full[1]]
    stack = jnp.concatenate(stack + [jnp.zeros((123, width), f32)], axis=0)
    cols_ref[...] = stack.T
    first = pl.multiple_of((at_ref[0] * 4 + at_ref[1]) * rows, rows)
    return cols_ref[pl.ds(first, rows), :]


def own_merge_kernel(half_rows, at_ref, mine_ref, got_ref, *refs):
    chunk_ref, full_ref, _, cols_ref = refs[-4:]
    rows = chunk_ref.shape[0]
    mine, other = mine_ref[rows:, :], got_ref[rows:, :]
    full = full_facts(mine, other)
    for i in range(8):
        full_ref[i : i + 1, :] = full[i]
    cols = columns_of(at_ref, mine, other, full, cols_ref, rows)
    chunk_ref[...] = merged(
        mine_ref[0:rows, :], got_ref[0:rows, :], cols, mine, other, full, half_rows
    )


def own_merge(at, mine, got, carried, half_rows, wait_for):
    rows, width = mine.shape
    return call(
        functools.partial(own_merge_kernel, half_rows),
        in_specs=[smem_spec, vmem_spec, vmem_spec, any_spec] + [any_spec] * len(wait_for),
        out_specs=[vmem_spec, vmem_spec, any_spec],
        out_shape=[shape(rows - 8, width), shape(8, width), shape(*carried.shape)],
        input_output_aliases={3: 2},
        scratch_shapes=[pltpu.VMEM((width, 128), f32)],
        name="own_merge",
    )(at, mine, got, carried, *wait_for)


def side_merge_kernel(half_rows, at_ref, mine_ref, got_ref, own_ref, own_got_ref, *refs):
    left_ref, right_ref, both_ref, pf_ref, nf_ref, cols_ref = refs[-6:]
    rows = left_ref.shape[0]
    mine, other = own_ref[rows:, :], own_got_ref[rows:, :]
    cols = columns_of(at_ref, mine, other, full_facts(mine, other), cols_ref, rows)
    for side, (out_ref, facts_ref) in enumerate(((left_ref, pf_ref), (right_ref, nf_ref))):
        first = side * rows
        fact = 2 * rows + 8 * side
        b_mine, b_other = mine_ref[fact : fact + 8, :], got_ref[fact : fact + 8, :]
        full = full_facts(b_mine, b_other)
        for i in range(8):
            facts_ref[i : i + 1, :] = full[i]
        chunk = merged(
            mine_ref[first : first + rows, :],
            got_ref[first : first + rows, :],
            cols,
            b_mine,
            b_other,
            full,
            half_rows,
        )
        out_ref[...] = chunk
        both_ref[first : first + rows, :] = chunk


def side_merge(at, mine, got, own, own_got, half_rows, wait_for):
    rows, width = own.shape
    return call(
        functools.partial(side_merge_kernel, half_rows),
        in_specs=[smem_spec] + [vmem_spec] * 4 + [any_spec] * len(wait_for),
        out_specs=[vmem_spec] * 5,
        out_shape=[shape(rows - 8, width)] * 2
        + [shape(2 * (rows - 8), width)]
        + [shape(8, width)] * 2,
        scratch_shapes=[pltpu.VMEM((width, 128), f32)],
        name="side_merge",
    )(at, mine, got, own, own_got, *wait_for)


def pack(parts, wait_for=()):
    rows, width = parts[0].shape

    def kernel(*refs):
        for i in range(4):
            refs[-1][i] = refs[i][...]

    return call(
        kernel,
        in_specs=[vmem_spec] * 4 + [any_spec] * len(wait_for),
        out_specs=vmem_spec,
        out_shape=shape(4, rows, width),
        name="pack",
    )(*parts, *wait_for)


def join(first, second, carried, wait_for=()):
    rows, width = first.shape

    def kernel(first_ref, second_ref, *refs):
        refs[-2][0:rows, :] = first_ref[...]
        refs[-2][rows:, :] = second_ref[...]

    return call(
        kernel,
        in_specs=[vmem_spec] * 2 + [any_spec] * (1 + len(wait_for)),
        out_specs=[vmem_spec, any_spec],
        out_shape=[shape(2 * rows, width), shape(*carried.shape)],
        input_output_aliases={2: 1},
        name="join",
    )(first, second, carried, *wait_for)


def row_of(at_ref, core_flip, slot, rows):
    core, x = at_ref[0], at_ref[1]
    core = 1 - core if core_flip else core
    return pl.multiple_of((core * 4 + ((x - slot) & 3)) * rows, rows)


def own_grad_kernel(at_ref, mine_ref, other_ref, a_ref, b_ref, facts_ref, *refs):
    ga_ref, gb_ref, sums_ref, corr_ref, pt_ref, p_ref = refs[-6:]
    width = corr_ref.shape[0]

    @pl.when(pl.program_id(0) == 0)
    def _():
        rows = mine_ref.shape[1]
        for flip, ref in ((False, mine_ref), (True, other_ref)):
            for slot in range(4):
                corr_ref[pl.ds(row_of(at_ref, flip, slot, rows), rows), :] = ref[slot]
        corr = corr_ref[...]
        row_index = lax.broadcasted_iota(jnp.int32, corr.shape, 0)
        column = lax.broadcasted_iota(jnp.int32, corr.shape, 1)
        pen = jnp.where(row_index == column, -2.0 * (1.0 - corr), 2.0 * off_weight * corr)
        cross = pen * corr
        pen_t = pen.T
        high, low = split(pen)
        p_ref[0:width, :] = high
        p_ref[width : 2 * width, :] = low
        p_ref[2 * width :, :] = high
        high, low = split(pen_t)
        pt_ref[0:width, :] = high
        pt_ref[width : 2 * width, :] = low
        pt_ref[2 * width :, :] = high
        left = thrice(facts_ref[...])
        sums_ref[0:1, :] = mm(left, pt_ref[...])[5:6]
        sums_ref[1:2, :] = jnp.sum(cross.T, axis=0, keepdims=True)
        sums_ref[2:3, :] = mm(left, p_ref[...])[4:5]
        sums_ref[3:4, :] = jnp.sum(cross, axis=0, keepdims=True)
        sums_ref[4:8, :] = jnp.zeros((4, width), f32)

    norm_b = (b_ref[...] - facts_ref[2:3, :]) * facts_ref[3:4, :]
    ga_ref[...] = mm(thrice(norm_b), pt_ref[...])
    norm_a = (a_ref[...] - facts_ref[0:1, :]) * facts_ref[1:2, :]
    gb_ref[...] = mm(thrice(norm_a), p_ref[...])


def own_grad(at, mine, other, a, b, facts, wait_for):
    rows, width = b.shape
    steps = 4
    spec = pl.BlockSpec((rows // steps, width), lambda i: (i, 0))
    whole = pl.BlockSpec((8, width), lambda i: (0, 0))
    slots = pl.BlockSpec(mine.shape, lambda i: (0, 0, 0))
    return call(
        own_grad_kernel,
        grid=(steps,),
        in_specs=[smem_spec, slots, slots, spec, spec, whole] + [any_spec] * len(wait_for),
        out_specs=[spec, spec, whole],
        out_shape=[shape(rows, width)] * 2 + [shape(8, width)],
        scratch_shapes=[
            pltpu.VMEM((width, width), f32),
            pltpu.VMEM((3 * width, width), bf16),
            pltpu.VMEM((3 * width, width), bf16),
        ],
        mib=24,
        name="own_grad",
    )(at, mine, other, a, b, facts, *wait_for)


def build(at_ref, mine_ref, other_ref, corr_ref, pen_ref, transposed):
    rows = mine_ref.shape[1] // 2
    width = corr_ref.shape[1]
    for flip, ref in ((False, mine_ref), (True, other_ref)):
        for slot in range(4):
            at = row_of(at_ref, flip, slot, rows)
            for side in (0, 1):
                corr_ref[side, pl.ds(at, rows), :] = ref[slot, side * rows : (side + 1) * rows, :]
    cross = jnp.zeros((1, width), f32)
    for side in (0, 1):
        corr = corr_ref[side]
        corr = corr.T if transposed else corr
        pen = 2.0 * off_weight * corr
        cross = cross + jnp.sum(pen * corr, axis=0, keepdims=True)
        high, low = split(pen)
        first = side * 3 * width
        pen_ref[first : first + width, :] = high
        pen_ref[first + width : first + 2 * width, :] = low
        pen_ref[first + 2 * width : first + 3 * width, :] = high
    return cross


def finish_kernel(for_a, at_ref, mine_ref, other_ref, f_ref, pf_ref, nf_ref, sums_ref, *refs):
    part_ref, view_ref = refs[:2]
    out_ref, corr_ref, pen_ref, vec_ref = refs[-4:]
    own = 0 if for_a else 2

    @pl.when(pl.program_id(0) == 0)
    def _():
        cross = build(at_ref, mine_ref, other_ref, corr_ref, pen_ref, for_a)
        left = jnp.concatenate([thrice(pf_ref[...]), thrice(nf_ref[...])], axis=1)
        mean = 5 if for_a else 4
        vec_ref[0:1, :] = sums_ref[own : own + 1, :] + mm(left, pen_ref[...])[mean : mean + 1]
        vec_ref[1:2, :] = sums_ref[own + 1 : own + 2, :] + cross

    if for_a:
        prev = (refs[2][...] - pf_ref[2:3, :]) * pf_ref[3:4, :]
        next_ = (refs[3][...] - nf_ref[2:3, :]) * nf_ref[3:4, :]
    else:
        in_top = pl.program_id(0) == 0
        prev = jnp.where(in_top, refs[2][...], refs[3][...]) * pf_ref[6:7, :] + pf_ref[7:8, :]
        next_ = jnp.where(in_top, refs[4][...], refs[5][...]) * nf_ref[6:7, :] + nf_ref[7:8, :]
    both = jnp.concatenate([thrice(prev), thrice(next_)], axis=1)
    grad = part_ref[...] + mm(both, pen_ref[...])
    inverse = f_ref[own + 1 : own + 2, :]
    normed = (view_ref[...] - f_ref[own : own + 1, :]) * inverse
    out_ref[...] = (grad - vec_ref[0:1, :] - normed * vec_ref[1:2, :]) * inverse


def finish(for_a, at, mine, other, facts, sums, part, view, halos):
    rows, width = view.shape
    tile = 256
    spec = pl.BlockSpec((tile, width), lambda i: (i, 0))
    top = pl.BlockSpec((tile, width), lambda i: (0, 0))
    low = pl.BlockSpec((tile, width), lambda i: (jnp.maximum(i - 1, 0), 0))
    whole = pl.BlockSpec((8, width), lambda i: (0, 0))
    slots = pl.BlockSpec(mine.shape, lambda i: (0, 0, 0))
    return call(
        functools.partial(finish_kernel, for_a),
        mib=24,
        grid=(rows // tile,),
        in_specs=[smem_spec, slots, slots]
        + [whole] * 4
        + [spec] * 2
        + ([spec] * 2 if for_a else [top, low] * 2),
        out_specs=spec,
        out_shape=shape(rows, width),
        scratch_shapes=[
            pltpu.VMEM((2, width, width), f32),
            pltpu.VMEM((6 * width, width), bf16),
            pltpu.VMEM((8, width), f32),
        ],
        name="finish_a" if for_a else "finish_b",
    )(at, mine, other, *facts, sums, part, view, *halos)


def per_device(view_a, view_b):
    local_rows, width = view_a.shape
    half_rows = local_rows * lax.axis_size("row") // 2
    index = lax.axis_index("row")
    at = jnp.stack([index & 1, (index >> 1) & 3])

    prev_raw = across(view_b, 1)
    next_raw = across(view_b, -1)
    sums = sums_of(view_a, view_b)
    sums = sums + to_core(sums)
    parts = [sums] + [to_x(sums, shift) for shift in (1, 2, 3)]

    a_top, a_low, half_facts, keep, send = own_corr(at, view_a, view_b, parts, half_rows)
    prev_half = across(half_facts, 1)
    next_half = across(half_facts, -1)
    slots = fan(keep, to_core(send))
    got = [slots[0]] + [to_x(slots[shift], shift) for shift in (1, 2, 3)]
    (own_mine,) = message(got, [half_facts])
    own_got = to_y(own_mine)

    keep, send = side_corr(
        at, view_a, prev_raw, next_raw, half_facts, prev_half, next_half, [own_mine]
    )
    own_chunk, facts, a_top = own_merge(at, own_mine, own_got, a_top, half_rows, [keep])
    prev_top = across(a_top, 1)
    next_top = across(a_top, -1)
    slots = fan(keep, to_core(send))
    got = [slots[0]] + [to_x(slots[shift], shift) for shift in (1, 2, 3)]
    side_mine, own_chunk = message(got, [prev_half, next_half], own_chunk)
    own_slots = [own_chunk] + [to_x(own_chunk, shift) for shift in (1, 2, 3)]
    left, right, sides, prev_facts, next_facts = side_merge(
        at, side_mine, to_y(side_mine), own_mine, own_got, half_rows, [prev_top, next_top]
    )
    from_next = across(left, -1)
    from_prev = across(right, 1)
    side_slots = [sides] + [to_x(sides, shift) for shift in (1, 2, 3)]
    own_pack = pack(own_slots)
    own_other = to_core(own_pack)
    ends, a_low = join(from_prev, from_next, a_low, [own_other])
    prev_low = across(a_low, 1)
    next_low = across(a_low, -1)
    end_slots = [ends] + [to_x(ends, shift) for shift in (1, 2, 3)]
    part_a, part_b, own_sums = own_grad(at, own_pack, own_other, view_a, view_b, facts, [ends])
    all_facts = [facts, prev_facts, next_facts]
    mine = pack(side_slots, [own_sums])
    grad_a = finish(
        True, at, mine, to_core(mine), all_facts, own_sums, part_a, view_a, [prev_raw, next_raw]
    )
    mine = pack(end_slots, [grad_a])
    halos = [prev_top, prev_low, next_top, next_low]
    grad_b = finish(
        False, at, mine, to_core(mine), all_facts, own_sums, part_b, view_b, halos
    )
    return (grad_a, grad_b)


def solution(mesh):
    placed = (P("row", "grp"), P("row", "grp"))
    return jax.shard_map(
        per_device,
        mesh=mesh,
        in_specs=placed,
        out_specs=(P("row", "grp"), P("row", "grp")),
        check_vma=False,
    )
```

```python
import functools

import jax
import jax.numpy as jnp
from jax import lax
from jax.experimental import pallas as pl
from jax.experimental.pallas import tpu as pltpu
from jax.sharding import PartitionSpec as P

epsilon = 1e-05
off_weight = 0.0051
f32 = jnp.float32
bf16 = jnp.bfloat16


any_spec = pl.BlockSpec(memory_space=pl.ANY)
smem_spec = pl.BlockSpec(memory_space=pltpu.SMEM)
vmem_spec = pl.BlockSpec(memory_space=pltpu.VMEM)
cheap = pl.CostEstimate(flops=1, transcendentals=0, bytes_accessed=1)
top_rows, mid_rows = 512, 128


def call(kernel, mib=8, **rest):
    params = pltpu.CompilerParams(vmem_limit_bytes=mib * 1024 * 1024)
    return pl.pallas_call(kernel, compiler_params=params, cost_estimate=cheap, **rest)


def shape(*dims):
    return jax.ShapeDtypeStruct(dims, f32)


def across(block, shift):
    count = lax.axis_size("grp")
    return lax.ppermute(block, "grp", [(i, (i + shift) % count) for i in range(count)])


def to_core(block):
    return lax.ppermute(block, "row", [(i, i ^ 1) for i in range(16)])


def to_y(block):
    return lax.ppermute(block, "row", [(i, i ^ 8) for i in range(16)])


def to_x(block, shift):
    pairs = [(i, (i & 9) | ((((i >> 1) + shift) & 3) << 1)) for i in range(16)]
    return lax.ppermute(block, "row", pairs)


def split(value):
    high = value.astype(bf16)
    return high, (value - high.astype(f32)).astype(bf16)


def mm(a, b):
    return lax.dot_general(a, b, (((1,), (0,)), ((), ())), preferred_element_type=f32)


def gram(a, b):
    a_high, a_low = split(a.T)
    b_high, b_low = split(b)
    return mm(
        jnp.concatenate([a_high, a_high, a_low], axis=1),
        jnp.concatenate([b_high, b_low, b_high], axis=0),
    )


def thrice(value):
    high, low = split(value)
    return jnp.concatenate([high, high, low], axis=1)


def sums_kernel(a_ref, b_ref, out_ref):
    @pl.when(pl.program_id(0) == 0)
    def _():
        out_ref[...] = jnp.zeros_like(out_ref)

    a, b = a_ref[...], b_ref[...]
    for row, value in enumerate((a, a * a, b, b * b)):
        out_ref[row : row + 1, :] += jnp.sum(value, axis=0, keepdims=True)


def sums_of(a, b):
    rows, width = a.shape
    tile = rows // 4
    spec = pl.BlockSpec((tile, width), lambda i: (i, 0))
    return call(
        sums_kernel,
        grid=(4,),
        in_specs=[spec, spec],
        out_specs=pl.BlockSpec((8, width), lambda i: (0, 0)),
        out_shape=shape(8, width),
        name="sums",
    )(a, b)


def put_slots(at_ref, acc, keep_ref, sends, first, rows):
    core, x = at_ref[0], at_ref[1]
    for slot in range(4):
        chunk = (x + slot) & 3
        mine = pl.multiple_of((core * 4 + chunk) * rows, rows)
        theirs = pl.multiple_of(((1 - core) * 4 + chunk) * rows, rows)
        keep_ref[slot, first : first + rows, :] = acc[pl.ds(mine, rows), :]
        each = 4 // len(sends)
        sends[slot // each][slot % each, first : first + rows, :] = acc[pl.ds(theirs, rows), :]


def own_corr_kernel(half_rows, steps, bounds, at_ref, a_ref, b_ref, *refs):
    parts, halos, (facts_ref, keep_ref, send_ref, acc_ref) = refs[:4], refs[4:7], refs[7:]
    step = pl.program_id(0)

    @pl.when(step == 0)
    def _():
        total = parts[0][...] + parts[1][...] + parts[2][...] + parts[3][...]
        total = total / half_rows
        for view in (0, 1):
            mean, square = total[2 * view : 2 * view + 1], total[2 * view + 1 : 2 * view + 2]
            scale = jnp.sqrt(square - mean * mean + epsilon)
            facts_ref[2 * view : 2 * view + 1, :] = mean
            facts_ref[2 * view + 1 : 2 * view + 2, :] = 1.0 / scale
            facts_ref[4 + view : 5 + view, :] = square
            facts_ref[6 + view : 7 + view, :] = scale
        acc_ref[...] = jnp.zeros_like(acc_ref)

    norm_a = (a_ref[...] - facts_ref[0:1, :]) * facts_ref[1:2, :]
    norm_b = (b_ref[...] - facts_ref[2:3, :]) * facts_ref[3:4, :]

    for ref, first, last in zip(halos, bounds[:-1], bounds[1:]):

        @pl.when((step >= first) & (step < last))
        def _(ref=ref):
            ref[...] = norm_a

    acc_ref[...] += gram(norm_a, norm_b)

    @pl.when(step == steps - 1)
    def _():
        put_slots(at_ref, acc_ref, keep_ref, [send_ref], 0, keep_ref.shape[1])


def halo_cuts(rows, tile):
    sizes = (top_rows, mid_rows, rows - top_rows - mid_rows)
    bounds = (0, sizes[0] // tile, (sizes[0] + sizes[1]) // tile, rows // tile)

    def spec(first, last):
        return lambda i: (jnp.clip(i - first, 0, last - first - 1), 0)

    maps = [spec(first, last) for first, last in zip(bounds[:-1], bounds[1:])]
    return sizes, bounds, maps


def own_corr(at, a, b, parts, half_rows):
    rows, width = a.shape
    tile = 128
    sizes, bounds, maps = halo_cuts(rows, tile)
    spec = pl.BlockSpec((tile, width), lambda i: (i, 0))
    whole = pl.BlockSpec((8, width), lambda i: (0, 0))
    slots = pl.BlockSpec((4, width // 8, width), lambda i: (0, 0, 0))
    return call(
        functools.partial(own_corr_kernel, half_rows, rows // tile, bounds),
        grid=(rows // tile,),
        in_specs=[smem_spec, spec, spec] + [whole] * 4,
        out_specs=[pl.BlockSpec((tile, width), part) for part in maps] + [whole, slots, slots],
        out_shape=[shape(size, width) for size in sizes]
        + [shape(8, width)]
        + [shape(4, width // 8, width)] * 2,
        scratch_shapes=[pltpu.VMEM((width, width), f32)],
        mib=16,
        name="own_corr",
    )(at, a, b, *parts)


def side_corr_kernel(steps, at_ref, a_ref, prev_ref, next_ref, f_ref, *refs):
    keep_ref, *sends, left_ref, right_ref = refs[-5:]
    step = pl.program_id(0)

    @pl.when(step == 0)
    def _():
        left_ref[...] = jnp.zeros_like(left_ref)
        right_ref[...] = jnp.zeros_like(right_ref)

    norm_a = (a_ref[...] - f_ref[0:1, :]) * f_ref[1:2, :]
    for acc_ref, b_ref in ((left_ref, prev_ref), (right_ref, next_ref)):
        acc_ref[...] += gram(norm_a, b_ref[...])

    @pl.when(step == steps - 1)
    def _():
        rows = keep_ref.shape[1] // 2
        put_slots(at_ref, left_ref, keep_ref, sends, 0, rows)
        put_slots(at_ref, right_ref, keep_ref, sends, rows, rows)


def side_corr(at, a, prev_b, next_b, facts, wait_for):
    rows, width = a.shape
    steps = 4
    spec = pl.BlockSpec((rows // steps, width), lambda i: (i, 0))
    whole = pl.BlockSpec((8, width), lambda i: (0, 0))
    slots = pl.BlockSpec((4, width // 4, width), lambda i: (0, 0, 0))
    pair = pl.BlockSpec((2, width // 4, width), lambda i: (0, 0, 0))
    return call(
        functools.partial(side_corr_kernel, steps),
        grid=(steps,),
        in_specs=[smem_spec, spec, spec, spec, whole] + [any_spec] * len(wait_for),
        out_specs=[slots, pair, pair],
        out_shape=[shape(4, width // 4, width)] + [shape(2, width // 4, width)] * 2,
        scratch_shapes=[pltpu.VMEM((width, width), f32)] * 2,
        mib=24,
        name="side_corr",
    )(at, a, prev_b, next_b, facts, *wait_for)


def fan_kernel(keep_ref, *refs):
    gots, outs = refs[:-4], refs[-4:]
    each = 4 // len(gots)
    for slot in range(4):
        outs[slot][...] = keep_ref[slot] + gots[slot // each][slot % each]


def fan(keep, *gots):
    return call(
        fan_kernel,
        in_specs=[vmem_spec] * (1 + len(gots)),
        out_specs=[vmem_spec] * 4,
        out_shape=[shape(*keep.shape[1:])] * 4,
        name="fan",
    )(keep, *gots)


def own_sum_kernel(*refs):
    top_ref, facts_ref, sum_ref, halo_ref = refs[4:]
    sum_ref[...] = refs[0][...] + refs[1][...] + refs[2][...] + refs[3][...]
    rows = top_ref.shape[0]
    halo_ref[0:rows, :] = top_ref[...]
    halo_ref[rows:, :] = facts_ref[...]


def own_sum(parts, top, facts):
    rows, width = top.shape
    return call(
        own_sum_kernel,
        in_specs=[vmem_spec] * 6,
        out_specs=[vmem_spec] * 2,
        out_shape=[shape(*parts[0].shape), shape(rows + 8, width)],
        name="own_sum",
    )(*parts, top, facts)


def message_kernel(own_ref, *refs):
    side, facts, out_ref = refs[:4], refs[4:7], refs[7]
    first = own_ref.shape[0]
    last = first + side[0].shape[0]
    out_ref[0:first, :] = own_ref[...]
    out_ref[first:last, :] = side[0][...] + side[1][...] + side[2][...] + side[3][...]
    for i, ref in enumerate(facts):
        out_ref[last + 8 * i : last + 8 * i + 8, :] = ref[...]


def message(own, side, facts, prev_top, next_top):
    rows = own.shape[0] + side[0].shape[0] + 24
    width = own.shape[1]
    below = pl.BlockSpec((8, width), lambda i: (top_rows // 8, 0))
    wholes = [pl.BlockSpec(block.shape, lambda i: (0, 0)) for block in (own, *side, facts)]
    return call(
        message_kernel,
        grid=(1,),
        in_specs=wholes + [below] * 2,
        out_specs=pl.BlockSpec((rows, width), lambda i: (0, 0)),
        out_shape=shape(rows, width),
        name="message",
    )(own, *side, facts, prev_top, next_top)


def full_facts(mine, other):
    rows = []
    for view in (0, 1):
        mean = 0.5 * (mine[2 * view : 2 * view + 1] + other[2 * view : 2 * view + 1])
        square = 0.5 * (mine[4 + view : 5 + view] + other[4 + view : 5 + view])
        rows += [mean, 1.0 / jnp.sqrt(square - mean * mean + epsilon)]
    for view in (0, 1):
        average = 0.5 * (mine[2 * view : 2 * view + 1] + other[2 * view : 2 * view + 1])
        rows.append((average - rows[2 * view]) * rows[2 * view + 1])
    rows += [mine[6:7] * rows[1], (mine[0:1] - rows[0]) * rows[1]]
    return rows


def merged(mine, other, a_cols, b_mine, b_other, b_full, half_rows, raw_b):
    scale0, scale1, diff0, diff1, inverse = (a_cols[:, i : i + 1] for i in range(5))
    if not raw_b:
        mine, other = mine * b_mine[7:8], other * b_other[7:8]
    out = mine * scale0 + other * scale1
    shift0, shift1 = b_mine[2:3] - b_full[2], b_other[2:3] - b_full[2]
    out = out + half_rows * (diff0 * shift0 + diff1 * shift1)
    return out * (inverse * (b_full[3] * (0.5 / half_rows)))


def columns_of(at_ref, mine, other, full, cols_ref, rows):
    width = mine.shape[1]
    stack = [mine[6:7], other[6:7], mine[0:1] - full[0], other[0:1] - full[0], full[1]]
    stack = jnp.concatenate(stack + [jnp.zeros((123, width), f32)], axis=0)
    cols_ref[...] = stack.T
    first = pl.multiple_of((at_ref[0] * 4 + at_ref[1]) * rows, rows)
    return cols_ref[pl.ds(first, rows), :]


def merge_kernel(half_rows, at_ref, mine_ref, got_ref, *refs):
    left_ref, right_ref, trio_ref, *facts_refs, cols_ref = refs[-7:]
    rows = left_ref.shape[0]
    facts = [
        (mine_ref[first : first + 8, :], got_ref[first : first + 8, :])
        for first in (3 * rows, 3 * rows + 8, 3 * rows + 16)
    ]
    full = [full_facts(*both) for both in facts]
    for ref, values in zip(facts_refs, full):
        for i in range(8):
            ref[i : i + 1, :] = values[i]
    cols = columns_of(at_ref, *facts[0], full[0], cols_ref, rows)
    for kind in range(3):
        first = kind * rows
        chunk = merged(
            mine_ref[first : first + rows, :],
            got_ref[first : first + rows, :],
            cols,
            *facts[kind],
            full[kind],
            half_rows,
            kind > 0,
        )
        trio_ref[first : first + rows, :] = chunk
        if kind == 1:
            left_ref[...] = chunk
        if kind == 2:
            right_ref[...] = chunk


def merge(at, mine, got, half_rows):
    width = mine.shape[1]
    rows = (mine.shape[0] - 24) // 3
    return call(
        functools.partial(merge_kernel, half_rows),
        in_specs=[smem_spec] + [vmem_spec] * 2,
        out_specs=[vmem_spec] * 6,
        out_shape=[shape(rows, width)] * 2 + [shape(3 * rows, width)] + [shape(8, width)] * 3,
        scratch_shapes=[pltpu.VMEM((width, 128), f32)],
        name="merge",
    )(at, mine, got)


def pack(parts, wait_for=()):
    rows, width = parts[0].shape

    def kernel(*refs):
        for i in range(4):
            refs[-1][i] = refs[i][...]

    return call(
        kernel,
        in_specs=[vmem_spec] * 4 + [any_spec] * len(wait_for),
        out_specs=vmem_spec,
        out_shape=shape(4, rows, width),
        name="pack",
    )(*parts, *wait_for)


def join(first, second, carried):
    rows, width = first.shape
    count = len(carried)

    def kernel(first_ref, second_ref, *refs):
        refs[count][0:rows, :] = first_ref[...]
        refs[count][rows:, :] = second_ref[...]

    return call(
        kernel,
        in_specs=[vmem_spec] * 2 + [any_spec] * count,
        out_specs=[vmem_spec] + [any_spec] * count,
        out_shape=[shape(2 * rows, width)] + [shape(*c.shape) for c in carried],
        input_output_aliases={2 + i: 1 + i for i in range(count)},
        name="join",
    )(first, second, *carried)


def row_of(at_ref, core_flip, slot, rows):
    core, x = at_ref[0], at_ref[1]
    core = 1 - core if core_flip else core
    return pl.multiple_of((core * 4 + ((x - slot) & 3)) * rows, rows)


def build(at_ref, mine_ref, other_ref, kinds, own, corr_ref, pen_ref, transposed):
    width = corr_ref.shape[1]
    rows = width // 8
    for flip, ref in ((False, mine_ref), (True, other_ref)):
        for slot in range(4):
            at = row_of(at_ref, flip, slot, rows)
            for i, kind in enumerate(kinds):
                corr_ref[i, pl.ds(at, rows), :] = ref[slot, kind * rows : (kind + 1) * rows, :]
    cross = jnp.zeros((1, width), f32)
    for i, kind in enumerate(kinds):
        corr = corr_ref[i]
        corr = corr.T if transposed else corr
        pen = 2.0 * off_weight * corr
        if kind == own:
            row_index = lax.broadcasted_iota(jnp.int32, corr.shape, 0)
            column = lax.broadcasted_iota(jnp.int32, corr.shape, 1)
            pen = jnp.where(row_index == column, -2.0 * (1.0 - corr), pen)
        cross = cross + jnp.sum(pen * corr, axis=0, keepdims=True)
        high, low = split(pen)
        first = i * 3 * width
        pen_ref[first : first + width, :] = high
        pen_ref[first + width : first + 2 * width, :] = low
        pen_ref[first + 2 * width : first + 3 * width, :] = high
    return cross


def scratch_for(kinds, width):
    return [
        pltpu.VMEM((kinds, width, width), f32),
        pltpu.VMEM((3 * kinds * width, width), bf16),
        pltpu.VMEM((8, width), f32),
    ]


def finish_a_kernel(at_ref, mine_ref, other_ref, *refs):
    facts, (a_ref, *b_refs) = refs[:3], refs[3:7]
    out_ref, corr_ref, pen_ref, vec_ref = refs[-4:]

    @pl.when(pl.program_id(0) == 0)
    def _():
        kinds = (0, 1, 2)
        cross = build(at_ref, mine_ref, other_ref, kinds, 0, corr_ref, pen_ref, True)
        left = jnp.concatenate([thrice(ref[...]) for ref in facts], axis=1)
        vec_ref[0:1, :] = mm(left, pen_ref[...])[5:6]
        vec_ref[1:2, :] = cross

    norms = [
        thrice((b_ref[...] - ref[2:3, :]) * ref[3:4, :]) for b_ref, ref in zip(b_refs, facts)
    ]
    grad = mm(jnp.concatenate(norms, axis=1), pen_ref[...])
    inverse = facts[0][1:2, :]
    normed = (a_ref[...] - facts[0][0:1, :]) * inverse
    out_ref[...] = (grad - vec_ref[0:1, :] - normed * vec_ref[1:2, :]) * inverse


def finish_a(at, mine, other, facts, a, b, prev_b, next_b):
    rows, width = a.shape
    tile = 256
    spec = pl.BlockSpec((tile, width), lambda i: (i, 0))
    whole = pl.BlockSpec((8, width), lambda i: (0, 0))
    slots = pl.BlockSpec(mine.shape, lambda i: (0, 0, 0))
    return call(
        finish_a_kernel,
        mib=40,
        grid=(rows // tile,),
        in_specs=[smem_spec, slots, slots] + [whole] * 3 + [spec] * 4,
        out_specs=spec,
        out_shape=shape(rows, width),
        scratch_shapes=scratch_for(3, width),
        name="finish_a",
    )(at, mine, other, *facts, a, b, prev_b, next_b)


def own_b_kernel(at_ref, mine_ref, other_ref, facts_ref, a_ref, *refs):
    out_ref, sums_ref, corr_ref, pen_ref, _ = refs[-5:]

    @pl.when(pl.program_id(0) == 0)
    def _():
        sums_ref[...] = jnp.zeros_like(sums_ref)
        cross = build(at_ref, mine_ref, other_ref, (0,), 0, corr_ref, pen_ref, False)
        sums_ref[0:1, :] = mm(thrice(facts_ref[...]), pen_ref[...])[4:5]
        sums_ref[1:2, :] = cross

    norm_a = (a_ref[...] - facts_ref[0:1, :]) * facts_ref[1:2, :]
    out_ref[...] = mm(thrice(norm_a), pen_ref[...])


def own_b(at, mine, other, facts, a, wait_for):
    rows, width = a.shape
    tile = 256
    spec = pl.BlockSpec((tile, width), lambda i: (i, 0))
    whole = pl.BlockSpec((8, width), lambda i: (0, 0))
    slots = pl.BlockSpec(mine.shape, lambda i: (0, 0, 0))
    return call(
        own_b_kernel,
        mib=24,
        grid=(rows // tile,),
        in_specs=[smem_spec, slots, slots, whole, spec] + [any_spec] * len(wait_for),
        out_specs=[spec, whole],
        out_shape=[shape(rows, width), shape(8, width)],
        scratch_shapes=scratch_for(1, width),
        name="own_b",
    )(at, mine, other, facts, a, *wait_for)


def finish_b_kernel(bounds, at_ref, mine_ref, other_ref, f_ref, pf_ref, nf_ref, *refs):
    sums_ref, part_ref, b_ref, *halos = refs[:9]
    out_ref, corr_ref, pen_ref, vec_ref = refs[-4:]
    step = pl.program_id(0)

    @pl.when(step == 0)
    def _():
        cross = build(at_ref, mine_ref, other_ref, (0, 1), 2, corr_ref, pen_ref, False)
        left = jnp.concatenate([thrice(pf_ref[...]), thrice(nf_ref[...])], axis=1)
        vec_ref[0:1, :] = sums_ref[0:1, :] + mm(left, pen_ref[...])[4:5]
        vec_ref[1:2, :] = sums_ref[1:2, :] + cross

    def current(parts):
        rest = jnp.where(step < bounds[2], parts[1][...], parts[2][...])
        return jnp.where(step < bounds[1], parts[0][...], rest)

    prev = current(halos[:3]) * pf_ref[6:7, :] + pf_ref[7:8, :]
    next_ = current(halos[3:]) * nf_ref[6:7, :] + nf_ref[7:8, :]
    both = jnp.concatenate([thrice(prev), thrice(next_)], axis=1)
    grad = part_ref[...] + mm(both, pen_ref[...])
    normed = (b_ref[...] - f_ref[2:3, :]) * f_ref[3:4, :]
    out_ref[...] = (grad - vec_ref[0:1, :] - normed * vec_ref[1:2, :]) * f_ref[3:4, :]


def finish_b(at, mine, other, facts, sums, part, b, halos):
    rows, width = b.shape
    tile = 128
    _, bounds, maps = halo_cuts(rows, tile)
    spec = pl.BlockSpec((tile, width), lambda i: (i, 0))
    parts = [pl.BlockSpec((tile, width), part) for part in maps]
    whole = pl.BlockSpec((8, width), lambda i: (0, 0))
    slots = pl.BlockSpec(mine.shape, lambda i: (0, 0, 0))
    return call(
        functools.partial(finish_b_kernel, bounds),
        mib=24,
        grid=(rows // tile,),
        in_specs=[smem_spec, slots, slots] + [whole] * 4 + [spec] * 2 + parts * 2,
        out_specs=spec,
        out_shape=shape(rows, width),
        scratch_shapes=scratch_for(2, width),
        name="finish_b",
    )(at, mine, other, *facts, sums, part, b, *halos)


def per_device(view_a, view_b):
    local_rows, width = view_a.shape
    half_rows = local_rows * lax.axis_size("row") // 2
    index = lax.axis_index("row")
    at = jnp.stack([index & 1, (index >> 1) & 3])

    prev_raw = across(view_b, 1)
    next_raw = across(view_b, -1)
    sums = sums_of(view_a, view_b)
    sums = sums + to_core(sums)
    parts = [sums] + [to_x(sums, shift) for shift in (1, 2, 3)]

    a_top, a_mid, a_low, half_facts, keep, send = own_corr(at, view_a, view_b, parts, half_rows)
    slots = fan(keep, to_core(send))
    own_parts = [slots[0]] + [to_x(slots[shift], shift) for shift in (1, 2, 3)]
    own, a_top = own_sum(own_parts, a_top, half_facts)
    prev_top = across(a_top, 1)
    next_top = across(a_top, -1)

    keep, *sends = side_corr(at, view_a, prev_raw, next_raw, half_facts, [own])
    slots = fan(keep, *[to_core(send) for send in sends])
    side_parts = [slots[0]] + [to_x(slots[shift], shift) for shift in (1, 2, 3)]
    mine = message(own, side_parts, half_facts, prev_top, next_top)
    left, right, trio, *facts = merge(at, mine, to_y(mine), half_rows)
    from_next = across(left, -1)
    from_prev = across(right, 1)
    trio_slots = [trio] + [to_x(trio, shift) for shift in (1, 2, 3)]
    ends, a_mid, a_low = join(from_prev, from_next, [a_mid, a_low])
    prev_mid = across(a_mid, 1)
    next_mid = across(a_mid, -1)
    prev_low = across(a_low, 1)
    next_low = across(a_low, -1)
    end_slots = [ends] + [to_x(ends, shift) for shift in (1, 2, 3)]
    mine = pack(trio_slots, [ends, prev_mid, next_mid])
    other = to_core(mine)
    grad_a = finish_a(at, mine, other, facts, view_a, view_b, prev_raw, next_raw)
    ends = pack(end_slots, [grad_a, prev_low, next_low])
    part_b, sums = own_b(at, mine, other, facts[0], view_a, [ends])
    halos = [prev_top, prev_mid, prev_low, next_top, next_mid, next_low]
    grad_b = finish_b(at, ends, to_core(ends), facts, sums, part_b, view_b, halos)
    return (grad_a, grad_b)


def solution(mesh):
    placed = (P("row", "grp"), P("row", "grp"))
    return jax.shard_map(
        per_device,
        mesh=mesh,
        in_specs=placed,
        out_specs=(P("row", "grp"), P("row", "grp")),
        check_vma=False,
    )
```

```python
import functools

import jax
import jax.numpy as jnp
from jax import lax
from jax.experimental import pallas as pl
from jax.experimental.pallas import tpu as pltpu
from jax.sharding import PartitionSpec as P

epsilon = 1e-05
off_weight = 0.0051
f32 = jnp.float32
bf16 = jnp.bfloat16


any_spec = pl.BlockSpec(memory_space=pl.ANY)
smem_spec = pl.BlockSpec(memory_space=pltpu.SMEM)
vmem_spec = pl.BlockSpec(memory_space=pltpu.VMEM)
cheap = pl.CostEstimate(flops=1, transcendentals=0, bytes_accessed=1)
top_rows, mid_rows = 640, 128


def call(kernel, mib=8, **rest):
    params = pltpu.CompilerParams(vmem_limit_bytes=mib * 1024 * 1024)
    return pl.pallas_call(kernel, compiler_params=params, cost_estimate=cheap, **rest)


def shape(*dims):
    return jax.ShapeDtypeStruct(dims, f32)


def across(block, shift):
    count = lax.axis_size("grp")
    return lax.ppermute(block, "grp", [(i, (i + shift) % count) for i in range(count)])


def to_core(block):
    return lax.ppermute(block, "row", [(i, i ^ 1) for i in range(16)])


def to_y(block):
    return lax.ppermute(block, "row", [(i, i ^ 8) for i in range(16)])


def to_x(block, shift):
    pairs = [(i, (i & 9) | ((((i >> 1) + shift) & 3) << 1)) for i in range(16)]
    return lax.ppermute(block, "row", pairs)


def split(value):
    high = value.astype(bf16)
    return high, (value - high.astype(f32)).astype(bf16)


def mm(a, b):
    return lax.dot_general(a, b, (((1,), (0,)), ((), ())), preferred_element_type=f32)


def gram(a, b):
    a_high, a_low = split(a.T)
    b_high, b_low = split(b)
    return mm(
        jnp.concatenate([a_high, a_high, a_low], axis=1),
        jnp.concatenate([b_high, b_low, b_high], axis=0),
    )


def thrice(value):
    high, low = split(value)
    return jnp.concatenate([high, high, low], axis=1)


def sums_kernel(a_ref, b_ref, out_ref):
    @pl.when(pl.program_id(0) == 0)
    def _():
        out_ref[...] = jnp.zeros_like(out_ref)

    a, b = a_ref[...], b_ref[...]
    for row, value in enumerate((a, a * a, b, b * b)):
        out_ref[row : row + 1, :] += jnp.sum(value, axis=0, keepdims=True)


def sums_of(a, b):
    rows, width = a.shape
    tile = rows // 4
    spec = pl.BlockSpec((tile, width), lambda i: (i, 0))
    return call(
        sums_kernel,
        grid=(4,),
        in_specs=[spec, spec],
        out_specs=pl.BlockSpec((8, width), lambda i: (0, 0)),
        out_shape=shape(8, width),
        name="sums",
    )(a, b)


def put_slots(at_ref, acc, keep_ref, sends, first, rows):
    core, x = at_ref[0], at_ref[1]
    for slot in range(4):
        chunk = (x + slot) & 3
        mine = pl.multiple_of((core * 4 + chunk) * rows, rows)
        theirs = pl.multiple_of(((1 - core) * 4 + chunk) * rows, rows)
        keep_ref[slot, first : first + rows, :] = acc[pl.ds(mine, rows), :]
        each = 4 // len(sends)
        sends[slot // each][slot % each, first : first + rows, :] = acc[pl.ds(theirs, rows), :]


def own_corr_kernel(half_rows, steps, bounds, at_ref, a_ref, b_ref, *refs):
    parts, halos, (facts_ref, keep_ref, send_ref, acc_ref) = refs[:4], refs[4:7], refs[7:]
    step = pl.program_id(0)

    @pl.when(step == 0)
    def _():
        total = parts[0][...] + parts[1][...] + parts[2][...] + parts[3][...]
        total = total / half_rows
        for view in (0, 1):
            mean, square = total[2 * view : 2 * view + 1], total[2 * view + 1 : 2 * view + 2]
            scale = jnp.sqrt(square - mean * mean + epsilon)
            facts_ref[2 * view : 2 * view + 1, :] = mean
            facts_ref[2 * view + 1 : 2 * view + 2, :] = 1.0 / scale
            facts_ref[4 + view : 5 + view, :] = square
            facts_ref[6 + view : 7 + view, :] = scale
        acc_ref[...] = jnp.zeros_like(acc_ref)

    norm_a = (a_ref[...] - facts_ref[0:1, :]) * facts_ref[1:2, :]
    norm_b = (b_ref[...] - facts_ref[2:3, :]) * facts_ref[3:4, :]

    for ref, first, last in zip(halos, bounds[:-1], bounds[1:]):

        @pl.when((step >= first) & (step < last))
        def _(ref=ref):
            ref[...] = norm_a

    acc_ref[...] += gram(norm_a, norm_b)

    @pl.when(step == steps - 1)
    def _():
        put_slots(at_ref, acc_ref, keep_ref, [send_ref], 0, keep_ref.shape[1])


def halo_cuts(rows, tile):
    sizes = (top_rows, mid_rows, rows - top_rows - mid_rows)
    bounds = (0, sizes[0] // tile, (sizes[0] + sizes[1]) // tile, rows // tile)

    def spec(first, last):
        return lambda i: (jnp.clip(i - first, 0, last - first - 1), 0)

    maps = [spec(first, last) for first, last in zip(bounds[:-1], bounds[1:])]
    return sizes, bounds, maps


def own_corr(at, a, b, parts, half_rows):
    rows, width = a.shape
    tile = 128
    sizes, bounds, maps = halo_cuts(rows, tile)
    spec = pl.BlockSpec((tile, width), lambda i: (i, 0))
    whole = pl.BlockSpec((8, width), lambda i: (0, 0))
    slots = pl.BlockSpec((4, width // 8, width), lambda i: (0, 0, 0))
    return call(
        functools.partial(own_corr_kernel, half_rows, rows // tile, bounds),
        grid=(rows // tile,),
        in_specs=[smem_spec, spec, spec] + [whole] * 4,
        out_specs=[pl.BlockSpec((tile, width), part) for part in maps] + [whole, slots, slots],
        out_shape=[shape(size, width) for size in sizes]
        + [shape(8, width)]
        + [shape(4, width // 8, width)] * 2,
        scratch_shapes=[pltpu.VMEM((width, width), f32)],
        mib=16,
        name="own_corr",
    )(at, a, b, *parts)


def side_corr_kernel(steps, at_ref, a_ref, prev_ref, next_ref, f_ref, *refs):
    keep_ref, *sends, left_ref, right_ref = refs[-5:]
    step = pl.program_id(0)

    @pl.when(step == 0)
    def _():
        left_ref[...] = jnp.zeros_like(left_ref)
        right_ref[...] = jnp.zeros_like(right_ref)

    norm_a = (a_ref[...] - f_ref[0:1, :]) * f_ref[1:2, :]
    for acc_ref, b_ref in ((left_ref, prev_ref), (right_ref, next_ref)):
        acc_ref[...] += gram(norm_a, b_ref[...])

    @pl.when(step == steps - 1)
    def _():
        rows = keep_ref.shape[1] // 2
        put_slots(at_ref, left_ref, keep_ref, sends, 0, rows)
        put_slots(at_ref, right_ref, keep_ref, sends, rows, rows)


def side_corr(at, a, prev_b, next_b, facts, wait_for):
    rows, width = a.shape
    steps = 4
    spec = pl.BlockSpec((rows // steps, width), lambda i: (i, 0))
    whole = pl.BlockSpec((8, width), lambda i: (0, 0))
    slots = pl.BlockSpec((4, width // 4, width), lambda i: (0, 0, 0))
    pair = pl.BlockSpec((2, width // 4, width), lambda i: (0, 0, 0))
    return call(
        functools.partial(side_corr_kernel, steps),
        grid=(steps,),
        in_specs=[smem_spec, spec, spec, spec, whole] + [any_spec] * len(wait_for),
        out_specs=[slots, pair, pair],
        out_shape=[shape(4, width // 4, width)] + [shape(2, width // 4, width)] * 2,
        scratch_shapes=[pltpu.VMEM((width, width), f32)] * 2,
        mib=24,
        name="side_corr",
    )(at, a, prev_b, next_b, facts, *wait_for)


def fan_kernel(keep_ref, *refs):
    gots, outs = refs[:-4], refs[-4:]
    each = 4 // len(gots)
    for slot in range(4):
        outs[slot][...] = keep_ref[slot] + gots[slot // each][slot % each]


def fan(keep, *gots):
    return call(
        fan_kernel,
        in_specs=[vmem_spec] * (1 + len(gots)),
        out_specs=[vmem_spec] * 4,
        out_shape=[shape(*keep.shape[1:])] * 4,
        name="fan",
    )(keep, *gots)


def own_sum_kernel(*refs):
    top_ref, facts_ref, sum_ref, halo_ref = refs[4:]
    sum_ref[...] = refs[0][...] + refs[1][...] + refs[2][...] + refs[3][...]
    rows = top_ref.shape[0]
    halo_ref[0:rows, :] = top_ref[...]
    halo_ref[rows:, :] = facts_ref[...]


def own_sum(parts, top, facts):
    rows, width = top.shape
    return call(
        own_sum_kernel,
        in_specs=[vmem_spec] * 6,
        out_specs=[vmem_spec] * 2,
        out_shape=[shape(*parts[0].shape), shape(rows + 8, width)],
        name="own_sum",
    )(*parts, top, facts)


def message_kernel(own_ref, *refs):
    side, facts, out_ref = refs[:4], refs[4:7], refs[7]
    first = own_ref.shape[0]
    last = first + side[0].shape[0]
    out_ref[0:first, :] = own_ref[...]
    out_ref[first:last, :] = side[0][...] + side[1][...] + side[2][...] + side[3][...]
    for i, ref in enumerate(facts):
        out_ref[last + 8 * i : last + 8 * i + 8, :] = ref[...]


def message(own, side, facts, prev_top, next_top):
    rows = own.shape[0] + side[0].shape[0] + 24
    width = own.shape[1]
    below = pl.BlockSpec((8, width), lambda i: (top_rows // 8, 0))
    wholes = [pl.BlockSpec(block.shape, lambda i: (0, 0)) for block in (own, *side, facts)]
    return call(
        message_kernel,
        grid=(1,),
        in_specs=wholes + [below] * 2,
        out_specs=pl.BlockSpec((rows, width), lambda i: (0, 0)),
        out_shape=shape(rows, width),
        name="message",
    )(own, *side, facts, prev_top, next_top)


def full_facts(mine, other):
    rows = []
    for view in (0, 1):
        mean = 0.5 * (mine[2 * view : 2 * view + 1] + other[2 * view : 2 * view + 1])
        square = 0.5 * (mine[4 + view : 5 + view] + other[4 + view : 5 + view])
        rows += [mean, 1.0 / jnp.sqrt(square - mean * mean + epsilon)]
    for view in (0, 1):
        average = 0.5 * (mine[2 * view : 2 * view + 1] + other[2 * view : 2 * view + 1])
        rows.append((average - rows[2 * view]) * rows[2 * view + 1])
    rows += [mine[6:7] * rows[1], (mine[0:1] - rows[0]) * rows[1]]
    return rows


def merged(mine, other, a_cols, b_mine, b_other, b_full, half_rows, raw_b):
    scale0, scale1, diff0, diff1, inverse = (a_cols[:, i : i + 1] for i in range(5))
    if not raw_b:
        mine, other = mine * b_mine[7:8], other * b_other[7:8]
    out = mine * scale0 + other * scale1
    shift0, shift1 = b_mine[2:3] - b_full[2], b_other[2:3] - b_full[2]
    out = out + half_rows * (diff0 * shift0 + diff1 * shift1)
    return out * (inverse * (b_full[3] * (0.5 / half_rows)))


def columns_of(at_ref, mine, other, full, cols_ref, rows):
    width = mine.shape[1]
    stack = [mine[6:7], other[6:7], mine[0:1] - full[0], other[0:1] - full[0], full[1]]
    stack = jnp.concatenate(stack + [jnp.zeros((123, width), f32)], axis=0)
    cols_ref[...] = stack.T
    first = pl.multiple_of((at_ref[0] * 4 + at_ref[1]) * rows, rows)
    return cols_ref[pl.ds(first, rows), :]


def merge_kernel(half_rows, at_ref, mine_ref, got_ref, *refs):
    left_ref, right_ref, trio_ref, *facts_refs, cols_ref = refs[-7:]
    rows = left_ref.shape[0]
    facts = [
        (mine_ref[first : first + 8, :], got_ref[first : first + 8, :])
        for first in (3 * rows, 3 * rows + 8, 3 * rows + 16)
    ]
    full = [full_facts(*both) for both in facts]
    for ref, values in zip(facts_refs, full):
        for i in range(8):
            ref[i : i + 1, :] = values[i]
    cols = columns_of(at_ref, *facts[0], full[0], cols_ref, rows)
    for kind in range(3):
        first = kind * rows
        chunk = merged(
            mine_ref[first : first + rows, :],
            got_ref[first : first + rows, :],
            cols,
            *facts[kind],
            full[kind],
            half_rows,
            kind > 0,
        )
        trio_ref[first : first + rows, :] = chunk
        if kind == 1:
            left_ref[...] = chunk
        if kind == 2:
            right_ref[...] = chunk


def merge(at, mine, got, half_rows):
    width = mine.shape[1]
    rows = (mine.shape[0] - 24) // 3
    return call(
        functools.partial(merge_kernel, half_rows),
        in_specs=[smem_spec] + [vmem_spec] * 2,
        out_specs=[vmem_spec] * 6,
        out_shape=[shape(rows, width)] * 2 + [shape(3 * rows, width)] + [shape(8, width)] * 3,
        scratch_shapes=[pltpu.VMEM((width, 128), f32)],
        name="merge",
    )(at, mine, got)


def pack(parts, wait_for=()):
    rows, width = parts[0].shape

    def kernel(*refs):
        for i in range(4):
            refs[-1][i] = refs[i][...]

    return call(
        kernel,
        in_specs=[vmem_spec] * 4 + [any_spec] * len(wait_for),
        out_specs=vmem_spec,
        out_shape=shape(4, rows, width),
        name="pack",
    )(*parts, *wait_for)


def join(first, second, carried):
    rows, width = first.shape
    count = len(carried)

    def kernel(first_ref, second_ref, *refs):
        refs[count][0:rows, :] = first_ref[...]
        refs[count][rows:, :] = second_ref[...]

    return call(
        kernel,
        in_specs=[vmem_spec] * 2 + [any_spec] * count,
        out_specs=[vmem_spec] + [any_spec] * count,
        out_shape=[shape(2 * rows, width)] + [shape(*c.shape) for c in carried],
        input_output_aliases={2 + i: 1 + i for i in range(count)},
        name="join",
    )(first, second, *carried)


def row_of(at_ref, core_flip, slot, rows):
    core, x = at_ref[0], at_ref[1]
    core = 1 - core if core_flip else core
    return pl.multiple_of((core * 4 + ((x - slot) & 3)) * rows, rows)


def build(at_ref, mine_ref, other_ref, kinds, own, corr_ref, pen_ref, transposed):
    width = corr_ref.shape[1]
    rows = width // 8
    for flip, ref in ((False, mine_ref), (True, other_ref)):
        for slot in range(4):
            at = row_of(at_ref, flip, slot, rows)
            for i, kind in enumerate(kinds):
                corr_ref[i, pl.ds(at, rows), :] = ref[slot, kind * rows : (kind + 1) * rows, :]
    cross = jnp.zeros((1, width), f32)
    for i, kind in enumerate(kinds):
        corr = corr_ref[i]
        corr = corr.T if transposed else corr
        pen = 2.0 * off_weight * corr
        if kind == own:
            row_index = lax.broadcasted_iota(jnp.int32, corr.shape, 0)
            column = lax.broadcasted_iota(jnp.int32, corr.shape, 1)
            pen = jnp.where(row_index == column, -2.0 * (1.0 - corr), pen)
        cross = cross + jnp.sum(pen * corr, axis=0, keepdims=True)
        high, low = split(pen)
        first = i * 3 * width
        pen_ref[first : first + width, :] = high
        pen_ref[first + width : first + 2 * width, :] = low
        pen_ref[first + 2 * width : first + 3 * width, :] = high
    return cross


def scratch_for(kinds, width):
    return [
        pltpu.VMEM((kinds, width, width), f32),
        pltpu.VMEM((3 * kinds * width, width), bf16),
        pltpu.VMEM((8, width), f32),
    ]


def finish_a_kernel(at_ref, mine_ref, other_ref, *refs):
    facts, (a_ref, *b_refs) = refs[:3], refs[3:7]
    out_ref, ready_ref, corr_ref, pen_ref, vec_ref = refs[-5:]

    @pl.when(pl.program_id(0) == 0)
    def _():
        ready_ref[...] = jnp.zeros_like(ready_ref)
        kinds = (0, 1, 2)
        cross = build(at_ref, mine_ref, other_ref, kinds, 0, corr_ref, pen_ref, True)
        left = jnp.concatenate([thrice(ref[...]) for ref in facts], axis=1)
        vec_ref[0:1, :] = mm(left, pen_ref[...])[5:6]
        vec_ref[1:2, :] = cross

    norms = [
        thrice((b_ref[...] - ref[2:3, :]) * ref[3:4, :]) for b_ref, ref in zip(b_refs, facts)
    ]
    grad = mm(jnp.concatenate(norms, axis=1), pen_ref[...])
    inverse = facts[0][1:2, :]
    normed = (a_ref[...] - facts[0][0:1, :]) * inverse
    out_ref[...] = (grad - vec_ref[0:1, :] - normed * vec_ref[1:2, :]) * inverse


def finish_a(at, mine, other, facts, a, b, prev_b, next_b):
    rows, width = a.shape
    tile = 256
    spec = pl.BlockSpec((tile, width), lambda i: (i, 0))
    whole = pl.BlockSpec((8, width), lambda i: (0, 0))
    slots = pl.BlockSpec(mine.shape, lambda i: (0, 0, 0))
    return call(
        finish_a_kernel,
        mib=40,
        grid=(rows // tile,),
        in_specs=[smem_spec, slots, slots] + [whole] * 3 + [spec] * 4,
        out_specs=[spec, whole],
        out_shape=[shape(rows, width), shape(8, width)],
        scratch_shapes=scratch_for(3, width),
        name="finish_a",
    )(at, mine, other, *facts, a, b, prev_b, next_b)


def own_b_kernel(at_ref, mine_ref, other_ref, facts_ref, a_ref, *refs):
    out_ref, sums_ref, corr_ref, pen_ref, _ = refs[-5:]

    @pl.when(pl.program_id(0) == 0)
    def _():
        sums_ref[...] = jnp.zeros_like(sums_ref)
        cross = build(at_ref, mine_ref, other_ref, (0,), 0, corr_ref, pen_ref, False)
        sums_ref[0:1, :] = mm(thrice(facts_ref[...]), pen_ref[...])[4:5]
        sums_ref[1:2, :] = cross

    norm_a = (a_ref[...] - facts_ref[0:1, :]) * facts_ref[1:2, :]
    out_ref[...] = mm(thrice(norm_a), pen_ref[...])


def own_b(at, mine, other, facts, a, wait_for):
    rows, width = a.shape
    tile = 256
    spec = pl.BlockSpec((tile, width), lambda i: (i, 0))
    whole = pl.BlockSpec((8, width), lambda i: (0, 0))
    slots = pl.BlockSpec(mine.shape, lambda i: (0, 0, 0))
    return call(
        own_b_kernel,
        mib=24,
        grid=(rows // tile,),
        in_specs=[smem_spec, slots, slots, whole, spec] + [any_spec] * len(wait_for),
        out_specs=[spec, whole],
        out_shape=[shape(rows, width), shape(8, width)],
        scratch_shapes=scratch_for(1, width),
        name="own_b",
    )(at, mine, other, facts, a, *wait_for)


def finish_b_kernel(bounds, at_ref, mine_ref, other_ref, f_ref, pf_ref, nf_ref, *refs):
    sums_ref, part_ref, b_ref, *halos = refs[:9]
    out_ref, corr_ref, pen_ref, vec_ref = refs[-4:]
    step = pl.program_id(0)

    @pl.when(step == 0)
    def _():
        cross = build(at_ref, mine_ref, other_ref, (0, 1), 2, corr_ref, pen_ref, False)
        left = jnp.concatenate([thrice(pf_ref[...]), thrice(nf_ref[...])], axis=1)
        vec_ref[0:1, :] = sums_ref[0:1, :] + mm(left, pen_ref[...])[4:5]
        vec_ref[1:2, :] = sums_ref[1:2, :] + cross

    def current(parts):
        rest = jnp.where(step < bounds[2], parts[1][...], parts[2][...])
        return jnp.where(step < bounds[1], parts[0][...], rest)

    prev = current(halos[:3]) * pf_ref[6:7, :] + pf_ref[7:8, :]
    next_ = current(halos[3:]) * nf_ref[6:7, :] + nf_ref[7:8, :]
    both = jnp.concatenate([thrice(prev), thrice(next_)], axis=1)
    grad = part_ref[...] + mm(both, pen_ref[...])
    normed = (b_ref[...] - f_ref[2:3, :]) * f_ref[3:4, :]
    out_ref[...] = (grad - vec_ref[0:1, :] - normed * vec_ref[1:2, :]) * f_ref[3:4, :]


def finish_b(at, mine, other, facts, sums, part, b, halos):
    rows, width = b.shape
    tile = 128
    _, bounds, maps = halo_cuts(rows, tile)
    spec = pl.BlockSpec((tile, width), lambda i: (i, 0))
    parts = [pl.BlockSpec((tile, width), part) for part in maps]
    whole = pl.BlockSpec((8, width), lambda i: (0, 0))
    slots = pl.BlockSpec(mine.shape, lambda i: (0, 0, 0))
    return call(
        functools.partial(finish_b_kernel, bounds),
        mib=24,
        grid=(rows // tile,),
        in_specs=[smem_spec, slots, slots] + [whole] * 4 + [spec] * 2 + parts * 2,
        out_specs=spec,
        out_shape=shape(rows, width),
        scratch_shapes=scratch_for(2, width),
        name="finish_b",
    )(at, mine, other, *facts, sums, part, b, *halos)


def per_device(view_a, view_b):
    local_rows, width = view_a.shape
    half_rows = local_rows * lax.axis_size("row") // 2
    index = lax.axis_index("row")
    at = jnp.stack([index & 1, (index >> 1) & 3])

    prev_raw = across(view_b, 1)
    next_raw = across(view_b, -1)
    sums = sums_of(view_a, view_b)
    sums = sums + to_core(sums)
    parts = [sums] + [to_x(sums, shift) for shift in (1, 2, 3)]

    a_top, a_mid, a_low, half_facts, keep, send = own_corr(at, view_a, view_b, parts, half_rows)
    slots = fan(keep, to_core(send))
    own_parts = [slots[0]] + [to_x(slots[shift], shift) for shift in (1, 2, 3)]
    own, a_top = own_sum(own_parts, a_top, half_facts)
    prev_top = across(a_top, 1)
    next_top = across(a_top, -1)

    keep, *sends = side_corr(at, view_a, prev_raw, next_raw, half_facts, [own])
    slots = fan(keep, *[to_core(send) for send in sends])
    side_parts = [slots[0]] + [to_x(slots[shift], shift) for shift in (1, 2, 3)]
    mine = message(own, side_parts, half_facts, prev_top, next_top)
    left, right, trio, *facts = merge(at, mine, to_y(mine), half_rows)
    from_next = across(left, -1)
    from_prev = across(right, 1)
    trio_slots = [trio] + [to_x(trio, shift) for shift in (1, 2, 3)]
    ends, a_mid, a_low = join(from_prev, from_next, [a_mid, a_low])
    prev_mid = across(a_mid, 1)
    next_mid = across(a_mid, -1)
    prev_low = across(a_low, 1)
    next_low = across(a_low, -1)
    end_slots = [ends] + [to_x(ends, shift) for shift in (1, 2, 3)]
    mine = pack(trio_slots, [ends, prev_mid, next_mid])
    other = to_core(mine)
    grad_a, ready = finish_a(at, mine, other, facts, view_a, view_b, prev_raw, next_raw)
    ends = pack(end_slots, [ready, prev_low, next_low])
    part_b, sums = own_b(at, mine, other, facts[0], view_a, [ends])
    halos = [prev_top, prev_mid, prev_low, next_top, next_mid, next_low]
    grad_b = finish_b(at, ends, to_core(ends), facts, sums, part_b, view_b, halos)
    return (grad_a, grad_b)


def solution(mesh):
    placed = (P("row", "grp"), P("row", "grp"))
    return jax.shard_map(
        per_device,
        mesh=mesh,
        in_specs=placed,
        out_specs=(P("row", "grp"), P("row", "grp")),
        check_vma=False,
    )
```

```python
import functools

import jax
import jax.numpy as jnp
from jax import lax
from jax.experimental import pallas as pl
from jax.experimental.pallas import tpu as pltpu
from jax.sharding import PartitionSpec as P

epsilon = 1e-05
off_weight = 0.0051
f32 = jnp.float32
bf16 = jnp.bfloat16


any_spec = pl.BlockSpec(memory_space=pl.ANY)
smem_spec = pl.BlockSpec(memory_space=pltpu.SMEM)
vmem_spec = pl.BlockSpec(memory_space=pltpu.VMEM)
cheap = pl.CostEstimate(flops=1, transcendentals=0, bytes_accessed=1)
top_rows, mid_rows = 384, 128


def call(kernel, mib=8, **rest):
    params = pltpu.CompilerParams(vmem_limit_bytes=mib * 1024 * 1024)
    return pl.pallas_call(kernel, compiler_params=params, cost_estimate=cheap, **rest)


def shape(*dims):
    return jax.ShapeDtypeStruct(dims, f32)


def across(block, shift):
    count = lax.axis_size("grp")
    return lax.ppermute(block, "grp", [(i, (i + shift) % count) for i in range(count)])


def to_core(block):
    return lax.ppermute(block, "row", [(i, i ^ 1) for i in range(16)])


def to_y(block):
    return lax.ppermute(block, "row", [(i, i ^ 8) for i in range(16)])


def to_x(block, shift):
    pairs = [(i, (i & 9) | ((((i >> 1) + shift) & 3) << 1)) for i in range(16)]
    return lax.ppermute(block, "row", pairs)


def split(value):
    high = value.astype(bf16)
    return high, (value - high.astype(f32)).astype(bf16)


def mm(a, b):
    return lax.dot_general(a, b, (((1,), (0,)), ((), ())), preferred_element_type=f32)


def gram(a, b):
    a_high, a_low = split(a.T)
    b_high, b_low = split(b)
    return mm(
        jnp.concatenate([a_high, a_high, a_low], axis=1),
        jnp.concatenate([b_high, b_low, b_high], axis=0),
    )


def thrice(value):
    high, low = split(value)
    return jnp.concatenate([high, high, low], axis=1)


def sums_kernel(a_ref, b_ref, out_ref):
    @pl.when(pl.program_id(0) == 0)
    def _():
        out_ref[...] = jnp.zeros_like(out_ref)

    a, b = a_ref[...], b_ref[...]
    for row, value in enumerate((a, a * a, b, b * b)):
        out_ref[row : row + 1, :] += jnp.sum(value, axis=0, keepdims=True)


def sums_of(a, b):
    rows, width = a.shape
    tile = rows // 4
    spec = pl.BlockSpec((tile, width), lambda i: (i, 0))
    return call(
        sums_kernel,
        grid=(4,),
        in_specs=[spec, spec],
        out_specs=pl.BlockSpec((8, width), lambda i: (0, 0)),
        out_shape=shape(8, width),
        name="sums",
    )(a, b)


def put_slots(at_ref, acc, keep_ref, sends, first, rows):
    core, x = at_ref[0], at_ref[1]
    for slot in range(4):
        chunk = (x + slot) & 3
        mine = pl.multiple_of((core * 4 + chunk) * rows, rows)
        theirs = pl.multiple_of(((1 - core) * 4 + chunk) * rows, rows)
        keep_ref[slot, first : first + rows, :] = acc[pl.ds(mine, rows), :]
        each = 4 // len(sends)
        sends[slot // each][slot % each, first : first + rows, :] = acc[pl.ds(theirs, rows), :]


def own_corr_kernel(half_rows, steps, bounds, at_ref, a_ref, b_ref, *refs):
    parts, halos, (facts_ref, keep_ref, send_ref, acc_ref) = refs[:4], refs[4:7], refs[7:]
    step = pl.program_id(0)

    @pl.when(step == 0)
    def _():
        total = parts[0][...] + parts[1][...] + parts[2][...] + parts[3][...]
        total = total / half_rows
        for view in (0, 1):
            mean, square = total[2 * view : 2 * view + 1], total[2 * view + 1 : 2 * view + 2]
            scale = jnp.sqrt(square - mean * mean + epsilon)
            facts_ref[2 * view : 2 * view + 1, :] = mean
            facts_ref[2 * view + 1 : 2 * view + 2, :] = 1.0 / scale
            facts_ref[4 + view : 5 + view, :] = square
            facts_ref[6 + view : 7 + view, :] = scale
        acc_ref[...] = jnp.zeros_like(acc_ref)

    norm_a = (a_ref[...] - facts_ref[0:1, :]) * facts_ref[1:2, :]
    norm_b = (b_ref[...] - facts_ref[2:3, :]) * facts_ref[3:4, :]

    for ref, first, last in zip(halos, bounds[:-1], bounds[1:]):

        @pl.when((step >= first) & (step < last))
        def _(ref=ref):
            ref[...] = norm_a

    acc_ref[...] += gram(norm_a, norm_b)

    @pl.when(step == steps - 1)
    def _():
        put_slots(at_ref, acc_ref, keep_ref, [send_ref], 0, keep_ref.shape[1])


def halo_cuts(rows, tile):
    sizes = (top_rows, mid_rows, rows - top_rows - mid_rows)
    bounds = (0, sizes[0] // tile, (sizes[0] + sizes[1]) // tile, rows // tile)

    def spec(first, last):
        return lambda i: (jnp.clip(i - first, 0, last - first - 1), 0)

    maps = [spec(first, last) for first, last in zip(bounds[:-1], bounds[1:])]
    return sizes, bounds, maps


def own_corr(at, a, b, parts, half_rows):
    rows, width = a.shape
    tile = 128
    sizes, bounds, maps = halo_cuts(rows, tile)
    spec = pl.BlockSpec((tile, width), lambda i: (i, 0))
    whole = pl.BlockSpec((8, width), lambda i: (0, 0))
    slots = pl.BlockSpec((4, width // 8, width), lambda i: (0, 0, 0))
    return call(
        functools.partial(own_corr_kernel, half_rows, rows // tile, bounds),
        grid=(rows // tile,),
        in_specs=[smem_spec, spec, spec] + [whole] * 4,
        out_specs=[pl.BlockSpec((tile, width), part) for part in maps] + [whole, slots, slots],
        out_shape=[shape(size, width) for size in sizes]
        + [shape(8, width)]
        + [shape(4, width // 8, width)] * 2,
        scratch_shapes=[pltpu.VMEM((width, width), f32)],
        mib=16,
        name="own_corr",
    )(at, a, b, *parts)


def side_corr_kernel(steps, at_ref, a_ref, b_ref, f_ref, *refs):
    keep_ref, send_ref, acc_ref = refs[-3:]
    step = pl.program_id(0)

    @pl.when(step == 0)
    def _():
        acc_ref[...] = jnp.zeros_like(acc_ref)

    norm_a = (a_ref[...] - f_ref[0:1, :]) * f_ref[1:2, :]
    acc_ref[...] += gram(norm_a, b_ref[...])

    @pl.when(step == steps - 1)
    def _():
        put_slots(at_ref, acc_ref, keep_ref, [send_ref], 0, keep_ref.shape[1])


def side_corr(at, a, b, facts, wait_for):
    rows, width = a.shape
    steps = 4
    spec = pl.BlockSpec((rows // steps, width), lambda i: (i, 0))
    whole = pl.BlockSpec((8, width), lambda i: (0, 0))
    slots = pl.BlockSpec((4, width // 8, width), lambda i: (0, 0, 0))
    return call(
        functools.partial(side_corr_kernel, steps),
        grid=(steps,),
        in_specs=[smem_spec, spec, spec, whole] + [any_spec] * len(wait_for),
        out_specs=[slots, slots],
        out_shape=[shape(4, width // 8, width)] * 2,
        scratch_shapes=[pltpu.VMEM((width, width), f32)],
        mib=16,
        name="side_corr",
    )(at, a, b, facts, *wait_for)


def fan_kernel(count, *refs):
    keeps, gots, outs = refs[:count], refs[count : 2 * count], refs[2 * count :]
    for i in range(count):
        for slot in range(4):
            outs[4 * i + slot][...] = keeps[i][slot] + gots[i][slot]


def fan(keeps, gots):
    count = len(keeps)
    return call(
        functools.partial(fan_kernel, count),
        in_specs=[vmem_spec] * (2 * count),
        out_specs=[vmem_spec] * (4 * count),
        out_shape=[shape(*keep.shape[1:]) for keep in keeps for _ in range(4)],
        name="fan",
    )(*keeps, *gots)


def own_sum_kernel(*refs):
    top_ref, facts_ref, sum_ref, halo_ref = refs[4:]
    sum_ref[...] = refs[0][...] + refs[1][...] + refs[2][...] + refs[3][...]
    rows = top_ref.shape[0]
    halo_ref[0:rows, :] = top_ref[...]
    halo_ref[rows:, :] = facts_ref[...]


def own_sum(parts, top, facts):
    rows, width = top.shape
    return call(
        own_sum_kernel,
        in_specs=[vmem_spec] * 6,
        out_specs=[vmem_spec] * 2,
        out_shape=[shape(*parts[0].shape), shape(rows + 8, width)],
        name="own_sum",
    )(*parts, top, facts)


def message_kernel(whole, summed, facts, *refs):
    out_ref = refs[-1]
    first = 0
    for ref in refs[:whole]:
        out_ref[first : first + ref.shape[0], :] = ref[...]
        first += ref.shape[0]
    parts = refs[whole : whole + summed]
    rows = parts[0].shape[0]
    out_ref[first : first + rows, :] = parts[0][...] + parts[1][...] + parts[2][...] + parts[3][...]
    first += rows
    for ref in refs[whole + summed : whole + summed + facts]:
        out_ref[first : first + 8, :] = ref[...]
        first += 8


def message(whole, summed, facts, halo_tops):
    rows, width = summed[0].shape
    below = pl.BlockSpec((8, width), lambda i: (top_rows // 8, 0))
    blocks = [*whole, *summed, *facts]
    size = rows * (len(whole) + 1) + 8 * (len(facts) + len(halo_tops))
    return call(
        functools.partial(
            message_kernel, len(whole), len(summed), len(facts) + len(halo_tops)
        ),
        grid=(1,),
        in_specs=[pl.BlockSpec(block.shape, lambda i: (0, 0)) for block in blocks]
        + [below] * len(halo_tops),
        out_specs=pl.BlockSpec((size, width), lambda i: (0, 0)),
        out_shape=shape(size, width),
        name="message",
    )(*blocks, *halo_tops)


def full_facts(mine, other):
    rows = []
    for view in (0, 1):
        mean = 0.5 * (mine[2 * view : 2 * view + 1] + other[2 * view : 2 * view + 1])
        square = 0.5 * (mine[4 + view : 5 + view] + other[4 + view : 5 + view])
        rows += [mean, 1.0 / jnp.sqrt(square - mean * mean + epsilon)]
    for view in (0, 1):
        average = 0.5 * (mine[2 * view : 2 * view + 1] + other[2 * view : 2 * view + 1])
        rows.append((average - rows[2 * view]) * rows[2 * view + 1])
    rows += [mine[6:7] * rows[1], (mine[0:1] - rows[0]) * rows[1]]
    return rows


def merged(mine, other, a_cols, b_mine, b_other, b_full, half_rows, raw_b):
    scale0, scale1, diff0, diff1, inverse = (a_cols[:, i : i + 1] for i in range(5))
    if not raw_b:
        mine, other = mine * b_mine[7:8], other * b_other[7:8]
    out = mine * scale0 + other * scale1
    shift0, shift1 = b_mine[2:3] - b_full[2], b_other[2:3] - b_full[2]
    out = out + half_rows * (diff0 * shift0 + diff1 * shift1)
    return out * (inverse * (b_full[3] * (0.5 / half_rows)))


def columns_of(at_ref, mine, other, full, cols_ref, rows):
    width = mine.shape[1]
    stack = [mine[6:7], other[6:7], mine[0:1] - full[0], other[0:1] - full[0], full[1]]
    stack = jnp.concatenate(stack + [jnp.zeros((123, width), f32)], axis=0)
    cols_ref[...] = stack.T
    first = pl.multiple_of((at_ref[0] * 4 + at_ref[1]) * rows, rows)
    return cols_ref[pl.ds(first, rows), :]


def merge_kernel(half_rows, at_ref, first_ref, first_got_ref, second_ref, second_got_ref, *refs):
    left_ref, right_ref, trio_ref, *facts_refs, cols_ref = refs
    rows = left_ref.shape[0]
    one, two = (first_ref, first_got_ref), (second_ref, second_got_ref)
    places = ((one, 2 * rows), (one, 2 * rows + 8), (one, 2 * rows + 16))
    facts = [tuple(ref[first : first + 8, :] for ref in both) for both, first in places]
    full = [full_facts(*both) for both in facts]
    for ref, values in zip(facts_refs, full):
        for i in range(8):
            ref[i : i + 1, :] = values[i]
    cols = columns_of(at_ref, *facts[0], full[0], cols_ref, rows)
    for kind, (both, first) in enumerate(((one, 0), (one, rows), (two, 0))):
        chunk = merged(
            both[0][first : first + rows, :],
            both[1][first : first + rows, :],
            cols,
            *facts[kind],
            full[kind],
            half_rows,
            kind > 0,
        )
        trio_ref[kind * rows : (kind + 1) * rows, :] = chunk
        if kind == 1:
            left_ref[...] = chunk
        if kind == 2:
            right_ref[...] = chunk


def merge(at, messages, half_rows):
    width = messages[0].shape[1]
    rows = width // 8
    return call(
        functools.partial(merge_kernel, half_rows),
        in_specs=[smem_spec] + [vmem_spec] * 4,
        out_specs=[vmem_spec] * 6,
        out_shape=[shape(rows, width)] * 2 + [shape(3 * rows, width)] + [shape(8, width)] * 3,
        scratch_shapes=[pltpu.VMEM((width, 128), f32)],
        name="merge",
    )(at, *messages)


def pack(parts, wait_for=()):
    rows, width = parts[0].shape

    def kernel(*refs):
        for i in range(4):
            refs[-1][i] = refs[i][...]

    return call(
        kernel,
        in_specs=[vmem_spec] * 4 + [any_spec] * len(wait_for),
        out_specs=vmem_spec,
        out_shape=shape(4, rows, width),
        name="pack",
    )(*parts, *wait_for)


def join(first, second, carried):
    rows, width = first.shape
    count = len(carried)

    def kernel(first_ref, second_ref, *refs):
        refs[count][0:rows, :] = first_ref[...]
        refs[count][rows:, :] = second_ref[...]

    return call(
        kernel,
        in_specs=[vmem_spec] * 2 + [any_spec] * count,
        out_specs=[vmem_spec] + [any_spec] * count,
        out_shape=[shape(2 * rows, width)] + [shape(*c.shape) for c in carried],
        input_output_aliases={2 + i: 1 + i for i in range(count)},
        name="join",
    )(first, second, *carried)


def row_of(at_ref, core_flip, slot, rows):
    core, x = at_ref[0], at_ref[1]
    core = 1 - core if core_flip else core
    return pl.multiple_of((core * 4 + ((x - slot) & 3)) * rows, rows)


def build(at_ref, mine_ref, other_ref, kinds, own, corr_ref, pen_ref, transposed):
    width = corr_ref.shape[1]
    rows = width // 8
    for flip, ref in ((False, mine_ref), (True, other_ref)):
        for slot in range(4):
            at = row_of(at_ref, flip, slot, rows)
            for i, kind in enumerate(kinds):
                corr_ref[i, pl.ds(at, rows), :] = ref[slot, kind * rows : (kind + 1) * rows, :]
    cross = jnp.zeros((1, width), f32)
    for i, kind in enumerate(kinds):
        corr = corr_ref[i]
        corr = corr.T if transposed else corr
        pen = 2.0 * off_weight * corr
        if kind == own:
            row_index = lax.broadcasted_iota(jnp.int32, corr.shape, 0)
            column = lax.broadcasted_iota(jnp.int32, corr.shape, 1)
            pen = jnp.where(row_index == column, -2.0 * (1.0 - corr), pen)
        cross = cross + jnp.sum(pen * corr, axis=0, keepdims=True)
        high, low = split(pen)
        first = i * 3 * width
        pen_ref[first : first + width, :] = high
        pen_ref[first + width : first + 2 * width, :] = low
        pen_ref[first + 2 * width : first + 3 * width, :] = high
    return cross


def scratch_for(kinds, width):
    return [
        pltpu.VMEM((kinds, width, width), f32),
        pltpu.VMEM((3 * kinds * width, width), bf16),
        pltpu.VMEM((8, width), f32),
    ]


def finish_a_kernel(at_ref, mine_ref, other_ref, *refs):
    facts, (a_ref, *b_refs) = refs[:3], refs[3:7]
    out_ref, ready_ref, corr_ref, pen_ref, vec_ref = refs[-5:]

    @pl.when(pl.program_id(0) == 0)
    def _():
        ready_ref[...] = jnp.zeros_like(ready_ref)
        kinds = (0, 1, 2)
        cross = build(at_ref, mine_ref, other_ref, kinds, 0, corr_ref, pen_ref, True)
        left = jnp.concatenate([thrice(ref[...]) for ref in facts], axis=1)
        vec_ref[0:1, :] = mm(left, pen_ref[...])[5:6]
        vec_ref[1:2, :] = cross

    norms = [
        thrice((b_ref[...] - ref[2:3, :]) * ref[3:4, :]) for b_ref, ref in zip(b_refs, facts)
    ]
    grad = mm(jnp.concatenate(norms, axis=1), pen_ref[...])
    inverse = facts[0][1:2, :]
    normed = (a_ref[...] - facts[0][0:1, :]) * inverse
    out_ref[...] = (grad - vec_ref[0:1, :] - normed * vec_ref[1:2, :]) * inverse


def finish_a(at, mine, other, facts, a, b, prev_b, next_b):
    rows, width = a.shape
    tile = 256
    spec = pl.BlockSpec((tile, width), lambda i: (i, 0))
    whole = pl.BlockSpec((8, width), lambda i: (0, 0))
    slots = pl.BlockSpec(mine.shape, lambda i: (0, 0, 0))
    return call(
        finish_a_kernel,
        mib=40,
        grid=(rows // tile,),
        in_specs=[smem_spec, slots, slots] + [whole] * 3 + [spec] * 4,
        out_specs=[spec, whole],
        out_shape=[shape(rows, width), shape(8, width)],
        scratch_shapes=scratch_for(3, width),
        name="finish_a",
    )(at, mine, other, *facts, a, b, prev_b, next_b)


def own_b_kernel(at_ref, mine_ref, other_ref, facts_ref, a_ref, *refs):
    out_ref, sums_ref, corr_ref, pen_ref, _ = refs[-5:]

    @pl.when(pl.program_id(0) == 0)
    def _():
        sums_ref[...] = jnp.zeros_like(sums_ref)
        cross = build(at_ref, mine_ref, other_ref, (0,), 0, corr_ref, pen_ref, False)
        sums_ref[0:1, :] = mm(thrice(facts_ref[...]), pen_ref[...])[4:5]
        sums_ref[1:2, :] = cross

    norm_a = (a_ref[...] - facts_ref[0:1, :]) * facts_ref[1:2, :]
    out_ref[...] = mm(thrice(norm_a), pen_ref[...])


def own_b(at, mine, other, facts, a, wait_for):
    rows, width = a.shape
    tile = 256
    spec = pl.BlockSpec((tile, width), lambda i: (i, 0))
    whole = pl.BlockSpec((8, width), lambda i: (0, 0))
    slots = pl.BlockSpec(mine.shape, lambda i: (0, 0, 0))
    return call(
        own_b_kernel,
        mib=24,
        grid=(rows // tile,),
        in_specs=[smem_spec, slots, slots, whole, spec] + [any_spec] * len(wait_for),
        out_specs=[spec, whole],
        out_shape=[shape(rows, width), shape(8, width)],
        scratch_shapes=scratch_for(1, width),
        name="own_b",
    )(at, mine, other, facts, a, *wait_for)


def finish_b_kernel(bounds, at_ref, mine_ref, other_ref, f_ref, pf_ref, nf_ref, *refs):
    sums_ref, part_ref, b_ref, *halos = refs[:15]
    out_ref, corr_ref, pen_ref, vec_ref = refs[-4:]
    step = pl.program_id(0)

    @pl.when(step == 0)
    def _():
        cross = build(at_ref, mine_ref, other_ref, (0, 1), 2, corr_ref, pen_ref, False)
        left = jnp.concatenate([thrice(pf_ref[...]), thrice(nf_ref[...])], axis=1)
        vec_ref[0:1, :] = sums_ref[0:1, :] + mm(left, pen_ref[...])[4:5]
        vec_ref[1:2, :] = sums_ref[1:2, :] + cross

    def current(parts):
        blocks = []
        for i in (0, 1):
            at = 2 * step + i
            rest = jnp.where(at < bounds[2], parts[3 * i + 1][...], parts[3 * i + 2][...])
            blocks.append(jnp.where(at < bounds[1], parts[3 * i][...], rest))
        return jnp.concatenate(blocks, axis=0)

    prev = current(halos[:6]) * pf_ref[6:7, :] + pf_ref[7:8, :]
    next_ = current(halos[6:]) * nf_ref[6:7, :] + nf_ref[7:8, :]
    both = jnp.concatenate([thrice(prev), thrice(next_)], axis=1)
    grad = part_ref[...] + mm(both, pen_ref[...])
    normed = (b_ref[...] - f_ref[2:3, :]) * f_ref[3:4, :]
    out_ref[...] = (grad - vec_ref[0:1, :] - normed * vec_ref[1:2, :]) * f_ref[3:4, :]


def finish_b(at, mine, other, facts, sums, part, b, halos):
    rows, width = b.shape
    block = 128
    tile = 2 * block
    _, bounds, maps = halo_cuts(rows, block)
    spec = pl.BlockSpec((tile, width), lambda i: (i, 0))
    parts = [
        pl.BlockSpec((block, width), lambda i, half=half, part=part: part(2 * i + half))
        for half in (0, 1)
        for part in maps
    ]
    whole = pl.BlockSpec((8, width), lambda i: (0, 0))
    slots = pl.BlockSpec(mine.shape, lambda i: (0, 0, 0))
    return call(
        functools.partial(finish_b_kernel, bounds),
        mib=24,
        grid=(rows // tile,),
        in_specs=[smem_spec, slots, slots] + [whole] * 4 + [spec] * 2 + parts * 2,
        out_specs=spec,
        out_shape=shape(rows, width),
        scratch_shapes=scratch_for(2, width),
        name="finish_b",
    )(at, mine, other, *facts, sums, part, b, *halos[:3] * 2, *halos[3:] * 2)


def per_device(view_a, view_b):
    local_rows, width = view_a.shape
    half_rows = local_rows * lax.axis_size("row") // 2
    index = lax.axis_index("row")
    at = jnp.stack([index & 1, (index >> 1) & 3])

    prev_raw = across(view_b, 1)
    next_raw = across(view_b, -1)
    sums = sums_of(view_a, view_b)
    sums = sums + to_core(sums)
    parts = [sums] + [to_x(sums, shift) for shift in (1, 2, 3)]

    a_top, a_mid, a_low, half_facts, keep, send = own_corr(at, view_a, view_b, parts, half_rows)
    slots = fan([keep], [to_core(send)])
    own_parts = [slots[0]] + [to_x(slots[shift], shift) for shift in (1, 2, 3)]
    own, a_top = own_sum(own_parts, a_top, half_facts)
    prev_top = across(a_top, 1)
    next_top = across(a_top, -1)

    left_keep, left_send = side_corr(at, view_a, prev_raw, half_facts, [own])
    right_keep, right_send = side_corr(at, view_a, next_raw, half_facts, [own])
    fans = fan([left_keep, right_keep], [to_core(left_send), to_core(right_send)])
    halves = []
    for slots, whole, known, tops in (
        (fans[:4], [own], [half_facts], [prev_top, next_top]),
        (fans[4:], [], [], []),
    ):
        summed = [slots[0]] + [to_x(slots[shift], shift) for shift in (1, 2, 3)]
        mine = message(whole, summed, known, tops)
        halves += [mine, to_y(mine)]
    left, right, trio, *facts = merge(at, halves, half_rows)
    from_next = across(left, -1)
    from_prev = across(right, 1)
    trio_slots = [trio] + [to_x(trio, shift) for shift in (1, 2, 3)]
    ends, a_mid, a_low = join(from_prev, from_next, [a_mid, a_low])
    prev_mid = across(a_mid, 1)
    next_mid = across(a_mid, -1)
    prev_low = across(a_low, 1)
    next_low = across(a_low, -1)
    end_slots = [ends] + [to_x(ends, shift) for shift in (1, 2, 3)]
    mine = pack(trio_slots, [ends, prev_mid, next_mid])
    other = to_core(mine)
    grad_a, ready = finish_a(at, mine, other, facts, view_a, view_b, prev_raw, next_raw)
    ends = pack(end_slots, [ready, prev_low, next_low])
    part_b, sums = own_b(at, mine, other, facts[0], view_a, [ends])
    halos = [prev_top, prev_mid, prev_low, next_top, next_mid, next_low]
    grad_b = finish_b(at, ends, to_core(ends), facts, sums, part_b, view_b, halos)
    return (grad_a, grad_b)


def solution(mesh):
    placed = (P("row", "grp"), P("row", "grp"))
    return jax.shard_map(
        per_device,
        mesh=mesh,
        in_specs=placed,
        out_specs=(P("row", "grp"), P("row", "grp")),
        check_vma=False,
    )
```

```python
import functools

import jax
import jax.numpy as jnp
from jax import lax
from jax.experimental import pallas as pl
from jax.experimental.pallas import tpu as pltpu
from jax.sharding import PartitionSpec as P

epsilon = 1e-05
off_weight = 0.0051
f32 = jnp.float32
bf16 = jnp.bfloat16


any_spec = pl.BlockSpec(memory_space=pl.ANY)
smem_spec = pl.BlockSpec(memory_space=pltpu.SMEM)
vmem_spec = pl.BlockSpec(memory_space=pltpu.VMEM)
cheap = pl.CostEstimate(flops=1, transcendentals=0, bytes_accessed=1)
top_rows, mid_rows = 640, 128


def call(kernel, mib=8, **rest):
    params = pltpu.CompilerParams(vmem_limit_bytes=mib * 1024 * 1024)
    return pl.pallas_call(kernel, compiler_params=params, cost_estimate=cheap, **rest)


def shape(*dims):
    return jax.ShapeDtypeStruct(dims, f32)


def across(block, shift):
    count = lax.axis_size("grp")
    return lax.ppermute(block, "grp", [(i, (i + shift) % count) for i in range(count)])


def to_core(block):
    return lax.ppermute(block, "row", [(i, i ^ 1) for i in range(16)])


def to_y(block):
    return lax.ppermute(block, "row", [(i, i ^ 8) for i in range(16)])


def to_x(block, shift):
    pairs = [(i, (i & 9) | ((((i >> 1) + shift) & 3) << 1)) for i in range(16)]
    return lax.ppermute(block, "row", pairs)


def split(value):
    high = value.astype(bf16)
    return high, (value - high.astype(f32)).astype(bf16)


def mm(a, b):
    return lax.dot_general(a, b, (((1,), (0,)), ((), ())), preferred_element_type=f32)


def gram(a, b):
    a_high, a_low = split(a.T)
    b_high, b_low = split(b)
    return mm(
        jnp.concatenate([a_high, a_high, a_low], axis=1),
        jnp.concatenate([b_high, b_low, b_high], axis=0),
    )


def thrice(value):
    high, low = split(value)
    return jnp.concatenate([high, high, low], axis=1)


def sums_kernel(a_ref, b_ref, out_ref):
    @pl.when(pl.program_id(0) == 0)
    def _():
        out_ref[...] = jnp.zeros_like(out_ref)

    a, b = a_ref[...], b_ref[...]
    for row, value in enumerate((a, a * a, b, b * b)):
        out_ref[row : row + 1, :] += jnp.sum(value, axis=0, keepdims=True)


def sums_of(a, b):
    rows, width = a.shape
    tile = rows // 4
    spec = pl.BlockSpec((tile, width), lambda i: (i, 0))
    return call(
        sums_kernel,
        grid=(4,),
        in_specs=[spec, spec],
        out_specs=pl.BlockSpec((8, width), lambda i: (0, 0)),
        out_shape=shape(8, width),
        name="sums",
    )(a, b)


def put_slots(at_ref, acc, keep_ref, sends, first, rows):
    core, x = at_ref[0], at_ref[1]
    for slot in range(4):
        chunk = (x + slot) & 3
        mine = pl.multiple_of((core * 4 + chunk) * rows, rows)
        theirs = pl.multiple_of(((1 - core) * 4 + chunk) * rows, rows)
        keep_ref[slot, first : first + rows, :] = acc[pl.ds(mine, rows), :]
        each = 4 // len(sends)
        sends[slot // each][slot % each, first : first + rows, :] = acc[pl.ds(theirs, rows), :]


def own_corr_kernel(half_rows, steps, bounds, at_ref, a_ref, b_ref, *refs):
    parts, halos, (facts_ref, keep_ref, send_ref, acc_ref) = refs[:4], refs[4:7], refs[7:]
    step = pl.program_id(0)

    @pl.when(step == 0)
    def _():
        total = parts[0][...] + parts[1][...] + parts[2][...] + parts[3][...]
        total = total / half_rows
        for view in (0, 1):
            mean, square = total[2 * view : 2 * view + 1], total[2 * view + 1 : 2 * view + 2]
            scale = jnp.sqrt(square - mean * mean + epsilon)
            facts_ref[2 * view : 2 * view + 1, :] = mean
            facts_ref[2 * view + 1 : 2 * view + 2, :] = 1.0 / scale
            facts_ref[4 + view : 5 + view, :] = square
            facts_ref[6 + view : 7 + view, :] = scale
        acc_ref[...] = jnp.zeros_like(acc_ref)

    norm_a = (a_ref[...] - facts_ref[0:1, :]) * facts_ref[1:2, :]
    norm_b = (b_ref[...] - facts_ref[2:3, :]) * facts_ref[3:4, :]

    for ref, first, last in zip(halos, bounds[:-1], bounds[1:]):

        @pl.when((step >= first) & (step < last))
        def _(ref=ref):
            ref[...] = norm_a

    acc_ref[...] += gram(norm_a, norm_b)

    @pl.when(step == steps - 1)
    def _():
        put_slots(at_ref, acc_ref, keep_ref, [send_ref], 0, keep_ref.shape[1])


def halo_cuts(rows, tile):
    sizes = (top_rows, mid_rows, rows - top_rows - mid_rows)
    bounds = (0, sizes[0] // tile, (sizes[0] + sizes[1]) // tile, rows // tile)

    def spec(first, last):
        return lambda i: (jnp.clip(i - first, 0, last - first - 1), 0)

    maps = [spec(first, last) for first, last in zip(bounds[:-1], bounds[1:])]
    return sizes, bounds, maps


def own_corr(at, a, b, parts, half_rows):
    rows, width = a.shape
    tile = 128
    sizes, bounds, maps = halo_cuts(rows, tile)
    spec = pl.BlockSpec((tile, width), lambda i: (i, 0))
    whole = pl.BlockSpec((8, width), lambda i: (0, 0))
    slots = pl.BlockSpec((4, width // 8, width), lambda i: (0, 0, 0))
    return call(
        functools.partial(own_corr_kernel, half_rows, rows // tile, bounds),
        grid=(rows // tile,),
        in_specs=[smem_spec, spec, spec] + [whole] * 4,
        out_specs=[pl.BlockSpec((tile, width), part) for part in maps] + [whole, slots, slots],
        out_shape=[shape(size, width) for size in sizes]
        + [shape(8, width)]
        + [shape(4, width // 8, width)] * 2,
        scratch_shapes=[pltpu.VMEM((width, width), f32)],
        mib=16,
        name="own_corr",
    )(at, a, b, *parts)


def side_corr_kernel(steps, at_ref, a_ref, prev_ref, next_ref, f_ref, *refs):
    keep_ref, *sends, left_ref, right_ref = refs[-5:]
    step = pl.program_id(0)

    @pl.when(step == 0)
    def _():
        left_ref[...] = jnp.zeros_like(left_ref)
        right_ref[...] = jnp.zeros_like(right_ref)

    norm_a = (a_ref[...] - f_ref[0:1, :]) * f_ref[1:2, :]
    for acc_ref, b_ref in ((left_ref, prev_ref), (right_ref, next_ref)):
        acc_ref[...] += gram(norm_a, b_ref[...])

    @pl.when(step == steps - 1)
    def _():
        rows = keep_ref.shape[1] // 2
        put_slots(at_ref, left_ref, keep_ref, sends, 0, rows)
        put_slots(at_ref, right_ref, keep_ref, sends, rows, rows)


def side_corr(at, a, prev_b, next_b, facts, wait_for):
    rows, width = a.shape
    steps = 4
    spec = pl.BlockSpec((rows // steps, width), lambda i: (i, 0))
    whole = pl.BlockSpec((8, width), lambda i: (0, 0))
    slots = pl.BlockSpec((4, width // 4, width), lambda i: (0, 0, 0))
    pair = pl.BlockSpec((2, width // 4, width), lambda i: (0, 0, 0))
    return call(
        functools.partial(side_corr_kernel, steps),
        grid=(steps,),
        in_specs=[smem_spec, spec, spec, spec, whole] + [any_spec] * len(wait_for),
        out_specs=[slots, pair, pair],
        out_shape=[shape(4, width // 4, width)] + [shape(2, width // 4, width)] * 2,
        scratch_shapes=[pltpu.VMEM((width, width), f32)] * 2,
        mib=24,
        name="side_corr",
    )(at, a, prev_b, next_b, facts, *wait_for)


def fan_kernel(keep_ref, *refs):
    gots, outs = refs[:-4], refs[-4:]
    each = 4 // len(gots)
    for slot in range(4):
        outs[slot][...] = keep_ref[slot] + gots[slot // each][slot % each]


def fan(keep, *gots):
    return call(
        fan_kernel,
        in_specs=[vmem_spec] * (1 + len(gots)),
        out_specs=[vmem_spec] * 4,
        out_shape=[shape(*keep.shape[1:])] * 4,
        name="fan",
    )(keep, *gots)


def own_sum_kernel(*refs):
    top_ref, facts_ref, sum_ref, halo_ref = refs[4:]
    sum_ref[...] = refs[0][...] + refs[1][...] + refs[2][...] + refs[3][...]
    rows = top_ref.shape[0]
    halo_ref[0:rows, :] = top_ref[...]
    halo_ref[rows:, :] = facts_ref[...]


def own_sum(parts, top, facts):
    rows, width = top.shape
    return call(
        own_sum_kernel,
        in_specs=[vmem_spec] * 6,
        out_specs=[vmem_spec] * 2,
        out_shape=[shape(*parts[0].shape), shape(rows + 8, width)],
        name="own_sum",
    )(*parts, top, facts)


def message_kernel(own_ref, *refs):
    side, facts, out_ref = refs[:4], refs[4:7], refs[7]
    first = own_ref.shape[0]
    last = first + side[0].shape[0]
    out_ref[0:first, :] = own_ref[...]
    out_ref[first:last, :] = side[0][...] + side[1][...] + side[2][...] + side[3][...]
    for i, ref in enumerate(facts):
        out_ref[last + 8 * i : last + 8 * i + 8, :] = ref[...]


def message(own, side, facts, prev_top, next_top):
    rows = own.shape[0] + side[0].shape[0] + 24
    width = own.shape[1]
    below = pl.BlockSpec((8, width), lambda i: (top_rows // 8, 0))
    wholes = [pl.BlockSpec(block.shape, lambda i: (0, 0)) for block in (own, *side, facts)]
    return call(
        message_kernel,
        grid=(1,),
        in_specs=wholes + [below] * 2,
        out_specs=pl.BlockSpec((rows, width), lambda i: (0, 0)),
        out_shape=shape(rows, width),
        name="message",
    )(own, *side, facts, prev_top, next_top)


def full_facts(mine, other):
    rows = []
    for view in (0, 1):
        mean = 0.5 * (mine[2 * view : 2 * view + 1] + other[2 * view : 2 * view + 1])
        square = 0.5 * (mine[4 + view : 5 + view] + other[4 + view : 5 + view])
        rows += [mean, 1.0 / jnp.sqrt(square - mean * mean + epsilon)]
    for view in (0, 1):
        average = 0.5 * (mine[2 * view : 2 * view + 1] + other[2 * view : 2 * view + 1])
        rows.append((average - rows[2 * view]) * rows[2 * view + 1])
    rows += [mine[6:7] * rows[1], (mine[0:1] - rows[0]) * rows[1]]
    return rows


def merged(mine, other, a_cols, b_mine, b_other, b_full, half_rows, raw_b):
    scale0, scale1, diff0, diff1, inverse = (a_cols[:, i : i + 1] for i in range(5))
    if not raw_b:
        mine, other = mine * b_mine[7:8], other * b_other[7:8]
    out = mine * scale0 + other * scale1
    shift0, shift1 = b_mine[2:3] - b_full[2], b_other[2:3] - b_full[2]
    out = out + half_rows * (diff0 * shift0 + diff1 * shift1)
    return out * (inverse * (b_full[3] * (0.5 / half_rows)))


def columns_of(at_ref, mine, other, full, cols_ref, rows):
    width = mine.shape[1]
    stack = [mine[6:7], other[6:7], mine[0:1] - full[0], other[0:1] - full[0], full[1]]
    stack = jnp.concatenate(stack + [jnp.zeros((123, width), f32)], axis=0)
    cols_ref[...] = stack.T
    first = pl.multiple_of((at_ref[0] * 4 + at_ref[1]) * rows, rows)
    return cols_ref[pl.ds(first, rows), :]


def merge_kernel(half_rows, at_ref, mine_ref, got_ref, *refs):
    left_ref, right_ref, trio_ref, *facts_refs, cols_ref = refs[-7:]
    rows = left_ref.shape[0]
    facts = [
        (mine_ref[first : first + 8, :], got_ref[first : first + 8, :])
        for first in (3 * rows, 3 * rows + 8, 3 * rows + 16)
    ]
    full = [full_facts(*both) for both in facts]
    for ref, values in zip(facts_refs, full):
        for i in range(8):
            ref[i : i + 1, :] = values[i]
    cols = columns_of(at_ref, *facts[0], full[0], cols_ref, rows)
    for kind in range(3):
        first = kind * rows
        chunk = merged(
            mine_ref[first : first + rows, :],
            got_ref[first : first + rows, :],
            cols,
            *facts[kind],
            full[kind],
            half_rows,
            kind > 0,
        )
        trio_ref[first : first + rows, :] = chunk
        if kind == 1:
            left_ref[...] = chunk
        if kind == 2:
            right_ref[...] = chunk


def merge(at, mine, got, half_rows):
    width = mine.shape[1]
    rows = (mine.shape[0] - 24) // 3
    return call(
        functools.partial(merge_kernel, half_rows),
        in_specs=[smem_spec] + [vmem_spec] * 2,
        out_specs=[vmem_spec] * 6,
        out_shape=[shape(rows, width)] * 2 + [shape(3 * rows, width)] + [shape(8, width)] * 3,
        scratch_shapes=[pltpu.VMEM((width, 128), f32)],
        name="merge",
    )(at, mine, got)


def pack(parts, wait_for=()):
    rows, width = parts[0].shape

    def kernel(*refs):
        for i in range(4):
            refs[-1][i] = refs[i][...]

    return call(
        kernel,
        in_specs=[vmem_spec] * 4 + [any_spec] * len(wait_for),
        out_specs=vmem_spec,
        out_shape=shape(4, rows, width),
        name="pack",
    )(*parts, *wait_for)


def join(first, second, carried):
    rows, width = first.shape
    count = len(carried)

    def kernel(first_ref, second_ref, *refs):
        refs[count][0:rows, :] = first_ref[...]
        refs[count][rows:, :] = second_ref[...]

    return call(
        kernel,
        in_specs=[vmem_spec] * 2 + [any_spec] * count,
        out_specs=[vmem_spec] + [any_spec] * count,
        out_shape=[shape(2 * rows, width)] + [shape(*c.shape) for c in carried],
        input_output_aliases={2 + i: 1 + i for i in range(count)},
        name="join",
    )(first, second, *carried)


def row_of(at_ref, core_flip, slot, rows):
    core, x = at_ref[0], at_ref[1]
    core = 1 - core if core_flip else core
    return pl.multiple_of((core * 4 + ((x - slot) & 3)) * rows, rows)


def build(at_ref, mine_ref, other_ref, kinds, own, corr_ref, pen_ref, transposed):
    width = corr_ref.shape[1]
    rows = width // 8
    for flip, ref in ((False, mine_ref), (True, other_ref)):
        for slot in range(4):
            at = row_of(at_ref, flip, slot, rows)
            for i, kind in enumerate(kinds):
                corr_ref[i, pl.ds(at, rows), :] = ref[slot, kind * rows : (kind + 1) * rows, :]
    cross = jnp.zeros((1, width), f32)
    for i, kind in enumerate(kinds):
        corr = corr_ref[i]
        corr = corr.T if transposed else corr
        pen = 2.0 * off_weight * corr
        if kind == own:
            row_index = lax.broadcasted_iota(jnp.int32, corr.shape, 0)
            column = lax.broadcasted_iota(jnp.int32, corr.shape, 1)
            pen = jnp.where(row_index == column, -2.0 * (1.0 - corr), pen)
        cross = cross + jnp.sum(pen * corr, axis=0, keepdims=True)
        high, low = split(pen)
        first = i * 3 * width
        pen_ref[first : first + width, :] = high
        pen_ref[first + width : first + 2 * width, :] = low
        pen_ref[first + 2 * width : first + 3 * width, :] = high
    return cross


def scratch_for(kinds, width):
    return [
        pltpu.VMEM((kinds, width, width), f32),
        pltpu.VMEM((3 * kinds * width, width), bf16),
        pltpu.VMEM((8, width), f32),
    ]


def presplit_kernel(b_ref, prev_ref, next_ref, a_ref, f_ref, pf_ref, nf_ref, *refs):
    bs_ref, a_out_ref = refs[-2:]
    width = a_ref.shape[1]
    for kind, (ref, facts_ref) in enumerate(
        ((b_ref, f_ref), (prev_ref, pf_ref), (next_ref, nf_ref))
    ):
        high, low = split((ref[...] - facts_ref[2:3, :]) * facts_ref[3:4, :])
        bs_ref[:, 2 * kind * width : (2 * kind + 1) * width] = high
        bs_ref[:, (2 * kind + 1) * width : (2 * kind + 2) * width] = low
    high, low = split((a_ref[...] - f_ref[0:1, :]) * f_ref[1:2, :])
    a_out_ref[:, 0:width] = high
    a_out_ref[:, width:] = low


def presplit(b, prev_b, next_b, a, facts, wait_for):
    rows, width = a.shape
    tile = 256
    spec = pl.BlockSpec((tile, width), lambda i: (i, 0))
    whole = pl.BlockSpec((8, width), lambda i: (0, 0))
    return call(
        presplit_kernel,
        mib=16,
        grid=(rows // tile,),
        in_specs=[spec] * 4 + [whole] * 3 + [any_spec] * len(wait_for),
        out_specs=[
            pl.BlockSpec((tile, 6 * width), lambda i: (i, 0)),
            pl.BlockSpec((tile, 2 * width), lambda i: (i, 0)),
        ],
        out_shape=[
            jax.ShapeDtypeStruct((rows, 6 * width), bf16),
            jax.ShapeDtypeStruct((rows, 2 * width), bf16),
        ],
        name="presplit",
    )(b, prev_b, next_b, a, *facts, *wait_for)


def repeated(parts, width):
    blocks = []
    for first in range(0, parts.shape[1], 2 * width):
        high = parts[:, first : first + width]
        blocks += [high, high, parts[:, first + width : first + 2 * width]]
    return jnp.concatenate(blocks, axis=1)


def finish_a_kernel(at_ref, mine_ref, other_ref, *refs):
    facts, (a_ref, parts_ref) = refs[:3], refs[3:5]
    out_ref, ready_ref, corr_ref, pen_ref, vec_ref = refs[-5:]

    @pl.when(pl.program_id(0) == 0)
    def _():
        ready_ref[...] = jnp.zeros_like(ready_ref)
        kinds = (0, 1, 2)
        cross = build(at_ref, mine_ref, other_ref, kinds, 0, corr_ref, pen_ref, True)
        left = jnp.concatenate([thrice(ref[...]) for ref in facts], axis=1)
        vec_ref[0:1, :] = mm(left, pen_ref[...])[5:6]
        vec_ref[1:2, :] = cross

    grad = mm(repeated(parts_ref[...], a_ref.shape[1]), pen_ref[...])
    inverse = facts[0][1:2, :]
    normed = (a_ref[...] - facts[0][0:1, :]) * inverse
    out_ref[...] = (grad - vec_ref[0:1, :] - normed * vec_ref[1:2, :]) * inverse


def finish_a(at, mine, other, facts, a, parts):
    rows, width = a.shape
    tile = 256
    spec = pl.BlockSpec((tile, width), lambda i: (i, 0))
    whole = pl.BlockSpec((8, width), lambda i: (0, 0))
    slots = pl.BlockSpec(mine.shape, lambda i: (0, 0, 0))
    return call(
        finish_a_kernel,
        mib=40,
        grid=(rows // tile,),
        in_specs=[smem_spec, slots, slots]
        + [whole] * 3
        + [spec, pl.BlockSpec((tile, 6 * width), lambda i: (i, 0))],
        out_specs=[spec, whole],
        out_shape=[shape(rows, width), shape(8, width)],
        scratch_shapes=scratch_for(3, width),
        name="finish_a",
    )(at, mine, other, *facts, a, parts)


def own_b_kernel(at_ref, mine_ref, other_ref, facts_ref, parts_ref, *refs):
    out_ref, sums_ref, corr_ref, pen_ref, _ = refs[-5:]

    @pl.when(pl.program_id(0) == 0)
    def _():
        sums_ref[...] = jnp.zeros_like(sums_ref)
        cross = build(at_ref, mine_ref, other_ref, (0,), 0, corr_ref, pen_ref, False)
        sums_ref[0:1, :] = mm(thrice(facts_ref[...]), pen_ref[...])[4:5]
        sums_ref[1:2, :] = cross

    out_ref[...] = mm(repeated(parts_ref[...], out_ref.shape[1]), pen_ref[...])


def own_b(at, mine, other, facts, parts, wait_for):
    rows, width = parts.shape[0], parts.shape[1] // 2
    tile = 256
    spec = pl.BlockSpec((tile, width), lambda i: (i, 0))
    whole = pl.BlockSpec((8, width), lambda i: (0, 0))
    slots = pl.BlockSpec(mine.shape, lambda i: (0, 0, 0))
    return call(
        own_b_kernel,
        mib=24,
        grid=(rows // tile,),
        in_specs=[smem_spec, slots, slots, whole]
        + [pl.BlockSpec((tile, 2 * width), lambda i: (i, 0))]
        + [any_spec] * len(wait_for),
        out_specs=[spec, whole],
        out_shape=[shape(rows, width), shape(8, width)],
        scratch_shapes=scratch_for(1, width),
        name="own_b",
    )(at, mine, other, facts, parts, *wait_for)


def finish_b_kernel(bounds, at_ref, mine_ref, other_ref, f_ref, pf_ref, nf_ref, *refs):
    sums_ref, part_ref, b_ref, *halos = refs[:15]
    out_ref, corr_ref, pen_ref, vec_ref = refs[-4:]
    step = pl.program_id(0)

    @pl.when(step == 0)
    def _():
        cross = build(at_ref, mine_ref, other_ref, (0, 1), 2, corr_ref, pen_ref, False)
        left = jnp.concatenate([thrice(pf_ref[...]), thrice(nf_ref[...])], axis=1)
        vec_ref[0:1, :] = sums_ref[0:1, :] + mm(left, pen_ref[...])[4:5]
        vec_ref[1:2, :] = sums_ref[1:2, :] + cross

    def current(parts):
        blocks = []
        for i in (0, 1):
            at = 2 * step + i
            rest = jnp.where(at < bounds[2], parts[3 * i + 1][...], parts[3 * i + 2][...])
            blocks.append(jnp.where(at < bounds[1], parts[3 * i][...], rest))
        return jnp.concatenate(blocks, axis=0)

    prev = current(halos[:6]) * pf_ref[6:7, :] + pf_ref[7:8, :]
    next_ = current(halos[6:]) * nf_ref[6:7, :] + nf_ref[7:8, :]
    both = jnp.concatenate([thrice(prev), thrice(next_)], axis=1)
    grad = part_ref[...] + mm(both, pen_ref[...])
    normed = (b_ref[...] - f_ref[2:3, :]) * f_ref[3:4, :]
    out_ref[...] = (grad - vec_ref[0:1, :] - normed * vec_ref[1:2, :]) * f_ref[3:4, :]


def finish_b(at, mine, other, facts, sums, part, b, halos):
    rows, width = b.shape
    block = 128
    tile = 2 * block
    _, bounds, maps = halo_cuts(rows, block)
    spec = pl.BlockSpec((tile, width), lambda i: (i, 0))
    parts = [
        pl.BlockSpec((block, width), lambda i, half=half, part=part: part(2 * i + half))
        for half in (0, 1)
        for part in maps
    ]
    whole = pl.BlockSpec((8, width), lambda i: (0, 0))
    slots = pl.BlockSpec(mine.shape, lambda i: (0, 0, 0))
    return call(
        functools.partial(finish_b_kernel, bounds),
        mib=24,
        grid=(rows // tile,),
        in_specs=[smem_spec, slots, slots] + [whole] * 4 + [spec] * 2 + parts * 2,
        out_specs=spec,
        out_shape=shape(rows, width),
        scratch_shapes=scratch_for(2, width),
        name="finish_b",
    )(at, mine, other, *facts, sums, part, b, *halos[:3] * 2, *halos[3:] * 2)


def per_device(view_a, view_b):
    local_rows, width = view_a.shape
    half_rows = local_rows * lax.axis_size("row") // 2
    index = lax.axis_index("row")
    at = jnp.stack([index & 1, (index >> 1) & 3])

    prev_raw = across(view_b, 1)
    next_raw = across(view_b, -1)
    sums = sums_of(view_a, view_b)
    sums = sums + to_core(sums)
    parts = [sums] + [to_x(sums, shift) for shift in (1, 2, 3)]

    a_top, a_mid, a_low, half_facts, keep, send = own_corr(at, view_a, view_b, parts, half_rows)
    slots = fan(keep, to_core(send))
    own_parts = [slots[0]] + [to_x(slots[shift], shift) for shift in (1, 2, 3)]
    own, a_top = own_sum(own_parts, a_top, half_facts)
    prev_top = across(a_top, 1)
    next_top = across(a_top, -1)

    keep, *sends = side_corr(at, view_a, prev_raw, next_raw, half_facts, [own])
    slots = fan(keep, *[to_core(send) for send in sends])
    side_parts = [slots[0]] + [to_x(slots[shift], shift) for shift in (1, 2, 3)]
    mine = message(own, side_parts, half_facts, prev_top, next_top)
    left, right, trio, *facts = merge(at, mine, to_y(mine), half_rows)
    from_next = across(left, -1)
    from_prev = across(right, 1)
    trio_slots = [trio] + [to_x(trio, shift) for shift in (1, 2, 3)]
    ends, a_mid, a_low = join(from_prev, from_next, [a_mid, a_low])
    prev_mid = across(a_mid, 1)
    next_mid = across(a_mid, -1)
    prev_low = across(a_low, 1)
    next_low = across(a_low, -1)
    end_slots = [ends] + [to_x(ends, shift) for shift in (1, 2, 3)]
    b_parts, a_parts = presplit(view_b, prev_raw, next_raw, view_a, facts, [ends])
    mine = pack(trio_slots, [a_parts, prev_mid, next_mid])
    other = to_core(mine)
    grad_a, ready = finish_a(at, mine, other, facts, view_a, b_parts)
    ends = pack(end_slots, [ready, prev_low, next_low])
    part_b, sums = own_b(at, mine, other, facts[0], a_parts, [ends])
    halos = [prev_top, prev_mid, prev_low, next_top, next_mid, next_low]
    grad_b = finish_b(at, ends, to_core(ends), facts, sums, part_b, view_b, halos)
    return (grad_a, grad_b)


def solution(mesh):
    placed = (P("row", "grp"), P("row", "grp"))
    return jax.shard_map(
        per_device,
        mesh=mesh,
        in_specs=placed,
        out_specs=(P("row", "grp"), P("row", "grp")),
        check_vma=False,
    )
```

```python
import functools

import jax
import jax.numpy as jnp
from jax import lax
from jax.experimental import pallas as pl
from jax.experimental.pallas import tpu as pltpu
from jax.sharding import PartitionSpec as P

epsilon = 1e-05
off_weight = 0.0051
f32 = jnp.float32
bf16 = jnp.bfloat16


any_spec = pl.BlockSpec(memory_space=pl.ANY)
smem_spec = pl.BlockSpec(memory_space=pltpu.SMEM)
vmem_spec = pl.BlockSpec(memory_space=pltpu.VMEM)
cheap = pl.CostEstimate(flops=1, transcendentals=0, bytes_accessed=1)
top_rows, mid_rows = 640, 128


def call(kernel, mib=8, **rest):
    params = pltpu.CompilerParams(vmem_limit_bytes=mib * 1024 * 1024)
    return pl.pallas_call(kernel, compiler_params=params, cost_estimate=cheap, **rest)


def shape(*dims):
    return jax.ShapeDtypeStruct(dims, f32)


def across(block, shift):
    count = lax.axis_size("grp")
    return lax.ppermute(block, "grp", [(i, (i + shift) % count) for i in range(count)])


def to_core(block):
    return lax.ppermute(block, "row", [(i, i ^ 1) for i in range(16)])


def to_y(block):
    return lax.ppermute(block, "row", [(i, i ^ 8) for i in range(16)])


def to_x(block, shift):
    pairs = [(i, (i & 9) | ((((i >> 1) + shift) & 3) << 1)) for i in range(16)]
    return lax.ppermute(block, "row", pairs)


def split(value):
    high = value.astype(bf16)
    return high, (value - high.astype(f32)).astype(bf16)


def mm(a, b):
    return lax.dot_general(a, b, (((1,), (0,)), ((), ())), preferred_element_type=f32)


def gram(a_high, a_low, b):
    b_high, b_low = split(b)
    return mm(
        jnp.concatenate([a_high, a_high, a_low], axis=1),
        jnp.concatenate([b_high, b_low, b_high], axis=0),
    )


def thrice(value):
    high, low = split(value)
    return jnp.concatenate([high, high, low], axis=1)


def sums_kernel(a_ref, b_ref, out_ref):
    @pl.when(pl.program_id(0) == 0)
    def _():
        out_ref[...] = jnp.zeros_like(out_ref)

    a, b = a_ref[...], b_ref[...]
    for row, value in enumerate((a, a * a, b, b * b)):
        out_ref[row : row + 1, :] += jnp.sum(value, axis=0, keepdims=True)


def sums_of(a, b):
    rows, width = a.shape
    tile = rows // 4
    spec = pl.BlockSpec((tile, width), lambda i: (i, 0))
    return call(
        sums_kernel,
        grid=(4,),
        in_specs=[spec, spec],
        out_specs=pl.BlockSpec((8, width), lambda i: (0, 0)),
        out_shape=shape(8, width),
        name="sums",
    )(a, b)


def put_slots(at_ref, acc, keep_ref, send_ref):
    core, x = at_ref[0], at_ref[1]
    rows = keep_ref.shape[1]
    for slot in range(4):
        chunk = (x + slot) & 3
        mine = pl.multiple_of((core * 4 + chunk) * rows, rows)
        theirs = pl.multiple_of(((1 - core) * 4 + chunk) * rows, rows)
        keep_ref[slot] = acc[pl.ds(mine, rows), :]
        send_ref[slot] = acc[pl.ds(theirs, rows), :]


def own_corr_kernel(half_rows, steps, bounds, at_ref, a_ref, b_ref, *refs):
    parts, halos, refs = refs[:4], refs[4:7], refs[7:]
    facts_ref, keep_ref, send_ref, high_ref, low_ref, acc_ref = refs
    step = pl.program_id(0)

    @pl.when(step == 0)
    def _():
        total = parts[0][...] + parts[1][...] + parts[2][...] + parts[3][...]
        total = total / half_rows
        for view in (0, 1):
            mean, square = total[2 * view : 2 * view + 1], total[2 * view + 1 : 2 * view + 2]
            scale = jnp.sqrt(square - mean * mean + epsilon)
            facts_ref[2 * view : 2 * view + 1, :] = mean
            facts_ref[2 * view + 1 : 2 * view + 2, :] = 1.0 / scale
            facts_ref[4 + view : 5 + view, :] = square
            facts_ref[6 + view : 7 + view, :] = scale
        acc_ref[...] = jnp.zeros_like(acc_ref)

    norm_a = (a_ref[...] - facts_ref[0:1, :]) * facts_ref[1:2, :]
    norm_b = (b_ref[...] - facts_ref[2:3, :]) * facts_ref[3:4, :]

    for ref, first, last in zip(halos, bounds[:-1], bounds[1:]):

        @pl.when((step >= first) & (step < last))
        def _(ref=ref):
            ref[...] = norm_a

    a_parts = split(norm_a.T)
    high_ref[...], low_ref[...] = a_parts
    acc_ref[...] += gram(*a_parts, norm_b)

    @pl.when(step == steps - 1)
    def _():
        put_slots(at_ref, acc_ref, keep_ref, send_ref)


def halo_cuts(rows, tile):
    sizes = (top_rows, mid_rows, rows - top_rows - mid_rows)
    bounds = (0, sizes[0] // tile, (sizes[0] + sizes[1]) // tile, rows // tile)

    def spec(first, last):
        return lambda i: (jnp.clip(i - first, 0, last - first - 1), 0)

    maps = [spec(first, last) for first, last in zip(bounds[:-1], bounds[1:])]
    return sizes, bounds, maps


def own_corr(at, a, b, parts, half_rows):
    rows, width = a.shape
    tile = 128
    sizes, bounds, maps = halo_cuts(rows, tile)
    spec = pl.BlockSpec((tile, width), lambda i: (i, 0))
    whole = pl.BlockSpec((8, width), lambda i: (0, 0))
    slots = pl.BlockSpec((4, width // 8, width), lambda i: (0, 0, 0))
    return call(
        functools.partial(own_corr_kernel, half_rows, rows // tile, bounds),
        grid=(rows // tile,),
        in_specs=[smem_spec, spec, spec] + [whole] * 4,
        out_specs=[pl.BlockSpec((tile, width), part) for part in maps] + [whole, slots, slots]
        + [pl.BlockSpec((width, tile), lambda i: (0, i))] * 2,
        out_shape=[shape(size, width) for size in sizes]
        + [shape(8, width)]
        + [shape(4, width // 8, width)] * 2
        + [jax.ShapeDtypeStruct((width, rows), bf16)] * 2,
        scratch_shapes=[pltpu.VMEM((width, width), f32)],
        mib=16,
        name="own_corr",
    )(at, a, b, *parts)


def side_corr_kernel(steps, at_ref, high_ref, low_ref, b_ref, *refs):
    keep_ref, send_ref, acc_ref = refs[-3:]
    step = pl.program_id(0)

    @pl.when(step == 0)
    def _():
        acc_ref[...] = gram(high_ref[...], low_ref[...], b_ref[...])

    @pl.when(step > 0)
    def _():
        acc_ref[...] += gram(high_ref[...], low_ref[...], b_ref[...])

    @pl.when(step == steps - 1)
    def _():
        put_slots(at_ref, acc_ref, keep_ref, send_ref)


def side_corr(at, a_high, a_low, b, wait_for):
    rows, width = b.shape
    tile = rows
    steps = rows // tile
    spec = pl.BlockSpec((tile, width), lambda i: (i, 0))
    lanes = pl.BlockSpec((width, tile), lambda i: (0, i))
    slots = pl.BlockSpec((4, width // 8, width), lambda i: (0, 0, 0))
    return call(
        functools.partial(side_corr_kernel, steps),
        grid=(steps,),
        in_specs=[smem_spec, lanes, lanes, spec] + [any_spec] * len(wait_for),
        out_specs=[slots, slots],
        out_shape=[shape(4, width // 8, width)] * 2,
        scratch_shapes=[pltpu.VMEM((width, width), f32)],
        mib=24,
        name="side_corr",
    )(at, a_high, a_low, b, *wait_for)


def fan_kernel(count, *refs):
    keeps, gots, outs = refs[:count], refs[count : 2 * count], refs[2 * count :]
    for i in range(count):
        for slot in range(4):
            outs[4 * i + slot][...] = keeps[i][slot] + gots[i][slot]


def fan(keeps, gots):
    count = len(keeps)
    return call(
        functools.partial(fan_kernel, count),
        in_specs=[vmem_spec] * (2 * count),
        out_specs=[vmem_spec] * (4 * count),
        out_shape=[shape(*keep.shape[1:]) for keep in keeps for _ in range(4)],
        name="fan",
    )(*keeps, *gots)


def joined_fan_kernel(left_ref, right_ref, got_left_ref, got_right_ref, *outs):
    rows = left_ref.shape[1]
    for slot in range(4):
        outs[slot][0:rows, :] = left_ref[slot] + got_left_ref[slot]
        outs[slot][rows:, :] = right_ref[slot] + got_right_ref[slot]


def joined_fan(keeps, gots):
    rows, width = keeps[0].shape[1:]
    return call(
        joined_fan_kernel,
        in_specs=[vmem_spec] * 4,
        out_specs=[vmem_spec] * 4,
        out_shape=[shape(2 * rows, width)] * 4,
        name="joined_fan",
    )(*keeps, *gots)


def own_sum_kernel(*refs):
    top_ref, facts_ref, sum_ref, halo_ref = refs[4:]
    sum_ref[...] = refs[0][...] + refs[1][...] + refs[2][...] + refs[3][...]
    rows = top_ref.shape[0]
    halo_ref[0:rows, :] = top_ref[...]
    halo_ref[rows:, :] = facts_ref[...]


def own_sum(parts, top, facts):
    rows, width = top.shape
    return call(
        own_sum_kernel,
        in_specs=[vmem_spec] * 6,
        out_specs=[vmem_spec] * 2,
        out_shape=[shape(*parts[0].shape), shape(rows + 8, width)],
        name="own_sum",
    )(*parts, top, facts)


def message_kernel(own_ref, *refs):
    side, facts, out_ref = refs[:4], refs[4:7], refs[7]
    first = own_ref.shape[0]
    last = first + side[0].shape[0]
    out_ref[0:first, :] = own_ref[...]
    out_ref[first:last, :] = side[0][...] + side[1][...] + side[2][...] + side[3][...]
    for i, ref in enumerate(facts):
        out_ref[last + 8 * i : last + 8 * i + 8, :] = ref[...]


def message(own, side, facts, prev_top, next_top):
    rows = own.shape[0] + side[0].shape[0] + 24
    width = own.shape[1]
    below = pl.BlockSpec((8, width), lambda i: (top_rows // 8, 0))
    wholes = [pl.BlockSpec(block.shape, lambda i: (0, 0)) for block in (own, *side, facts)]
    return call(
        message_kernel,
        grid=(1,),
        in_specs=wholes + [below] * 2,
        out_specs=pl.BlockSpec((rows, width), lambda i: (0, 0)),
        out_shape=shape(rows, width),
        name="message",
    )(own, *side, facts, prev_top, next_top)


def full_facts(mine, other):
    rows = []
    for view in (0, 1):
        mean = 0.5 * (mine[2 * view : 2 * view + 1] + other[2 * view : 2 * view + 1])
        square = 0.5 * (mine[4 + view : 5 + view] + other[4 + view : 5 + view])
        rows += [mean, 1.0 / jnp.sqrt(square - mean * mean + epsilon)]
    for view in (0, 1):
        average = 0.5 * (mine[2 * view : 2 * view + 1] + other[2 * view : 2 * view + 1])
        rows.append((average - rows[2 * view]) * rows[2 * view + 1])
    rows += [mine[6:7] * rows[1], (mine[0:1] - rows[0]) * rows[1]]
    return rows


def merged(mine, other, a_cols, b_mine, b_other, b_full, half_rows, raw_b):
    scale0, scale1, diff0, diff1, inverse = (a_cols[:, i : i + 1] for i in range(5))
    if not raw_b:
        mine, other = mine * b_mine[7:8], other * b_other[7:8]
    out = mine * scale0 + other * scale1
    shift0, shift1 = b_mine[2:3] - b_full[2], b_other[2:3] - b_full[2]
    out = out + half_rows * (diff0 * shift0 + diff1 * shift1)
    return out * (inverse * (b_full[3] * (0.5 / half_rows)))


def columns_of(at_ref, mine, other, full, cols_ref, rows):
    width = mine.shape[1]
    stack = [mine[6:7], other[6:7], mine[0:1] - full[0], other[0:1] - full[0], full[1]]
    stack = jnp.concatenate(stack + [jnp.zeros((123, width), f32)], axis=0)
    cols_ref[...] = stack.T
    first = pl.multiple_of((at_ref[0] * 4 + at_ref[1]) * rows, rows)
    return cols_ref[pl.ds(first, rows), :]


def merge_kernel(half_rows, at_ref, mine_ref, got_ref, *refs):
    left_ref, right_ref, trio_ref, *facts_refs, cols_ref = refs[-7:]
    rows = left_ref.shape[0]
    facts = [
        (mine_ref[first : first + 8, :], got_ref[first : first + 8, :])
        for first in (3 * rows, 3 * rows + 8, 3 * rows + 16)
    ]
    full = [full_facts(*both) for both in facts]
    for ref, values in zip(facts_refs, full):
        for i in range(8):
            ref[i : i + 1, :] = values[i]
    cols = columns_of(at_ref, *facts[0], full[0], cols_ref, rows)
    for kind in range(3):
        first = kind * rows
        chunk = merged(
            mine_ref[first : first + rows, :],
            got_ref[first : first + rows, :],
            cols,
            *facts[kind],
            full[kind],
            half_rows,
            kind > 0,
        )
        trio_ref[first : first + rows, :] = chunk
        if kind == 1:
            left_ref[...] = chunk
        if kind == 2:
            right_ref[...] = chunk


def merge(at, mine, got, half_rows):
    width = mine.shape[1]
    rows = (mine.shape[0] - 24) // 3
    return call(
        functools.partial(merge_kernel, half_rows),
        in_specs=[smem_spec] + [vmem_spec] * 2,
        out_specs=[vmem_spec] * 6,
        out_shape=[shape(rows, width)] * 2 + [shape(3 * rows, width)] + [shape(8, width)] * 3,
        scratch_shapes=[pltpu.VMEM((width, 128), f32)],
        name="merge",
    )(at, mine, got)


def pack(parts, wait_for=()):
    rows, width = parts[0].shape

    def kernel(*refs):
        for i in range(4):
            refs[-1][i] = refs[i][...]

    return call(
        kernel,
        in_specs=[vmem_spec] * 4 + [any_spec] * len(wait_for),
        out_specs=vmem_spec,
        out_shape=shape(4, rows, width),
        name="pack",
    )(*parts, *wait_for)


def join(first, second, carried):
    rows, width = first.shape
    count = len(carried)

    def kernel(first_ref, second_ref, *refs):
        refs[count][0:rows, :] = first_ref[...]
        refs[count][rows:, :] = second_ref[...]

    return call(
        kernel,
        in_specs=[vmem_spec] * 2 + [any_spec] * count,
        out_specs=[vmem_spec] + [any_spec] * count,
        out_shape=[shape(2 * rows, width)] + [shape(*c.shape) for c in carried],
        input_output_aliases={2 + i: 1 + i for i in range(count)},
        name="join",
    )(first, second, *carried)


def row_of(at_ref, core_flip, slot, rows):
    core, x = at_ref[0], at_ref[1]
    core = 1 - core if core_flip else core
    return pl.multiple_of((core * 4 + ((x - slot) & 3)) * rows, rows)


def build(at_ref, mine_ref, other_ref, kinds, own, corr_ref, pen_ref, transposed):
    width = corr_ref.shape[1]
    rows = width // 8
    for flip, ref in ((False, mine_ref), (True, other_ref)):
        for slot in range(4):
            at = row_of(at_ref, flip, slot, rows)
            for i, kind in enumerate(kinds):
                corr_ref[i, pl.ds(at, rows), :] = ref[slot, kind * rows : (kind + 1) * rows, :]
    cross = jnp.zeros((1, width), f32)
    for i, kind in enumerate(kinds):
        corr = corr_ref[i]
        corr = corr.T if transposed else corr
        pen = 2.0 * off_weight * corr
        if kind == own:
            row_index = lax.broadcasted_iota(jnp.int32, corr.shape, 0)
            column = lax.broadcasted_iota(jnp.int32, corr.shape, 1)
            pen = jnp.where(row_index == column, -2.0 * (1.0 - corr), pen)
        cross = cross + jnp.sum(pen * corr, axis=0, keepdims=True)
        high, low = split(pen)
        first = i * 3 * width
        pen_ref[first : first + width, :] = high
        pen_ref[first + width : first + 2 * width, :] = low
        pen_ref[first + 2 * width : first + 3 * width, :] = high
    return cross


def scratch_for(kinds, width):
    return [
        pltpu.VMEM((kinds, width, width), f32),
        pltpu.VMEM((3 * kinds * width, width), bf16),
        pltpu.VMEM((8, width), f32),
    ]


def presplit_kernel(b_ref, prev_ref, next_ref, a_ref, f_ref, pf_ref, nf_ref, *refs):
    bs_ref, a_out_ref = refs[-2:]
    width = a_ref.shape[1]
    for kind, (ref, facts_ref) in enumerate(
        ((b_ref, f_ref), (prev_ref, pf_ref), (next_ref, nf_ref))
    ):
        high, low = split((ref[...] - facts_ref[2:3, :]) * facts_ref[3:4, :])
        bs_ref[:, 2 * kind * width : (2 * kind + 1) * width] = high
        bs_ref[:, (2 * kind + 1) * width : (2 * kind + 2) * width] = low
    high, low = split((a_ref[...] - f_ref[0:1, :]) * f_ref[1:2, :])
    a_out_ref[:, 0:width] = high
    a_out_ref[:, width:] = low


def presplit(b, prev_b, next_b, a, facts, wait_for):
    rows, width = a.shape
    tile = 256
    spec = pl.BlockSpec((tile, width), lambda i: (i, 0))
    whole = pl.BlockSpec((8, width), lambda i: (0, 0))
    return call(
        presplit_kernel,
        mib=16,
        grid=(rows // tile,),
        in_specs=[spec] * 4 + [whole] * 3 + [any_spec] * len(wait_for),
        out_specs=[
            pl.BlockSpec((tile, 6 * width), lambda i: (i, 0)),
            pl.BlockSpec((tile, 2 * width), lambda i: (i, 0)),
        ],
        out_shape=[
            jax.ShapeDtypeStruct((rows, 6 * width), bf16),
            jax.ShapeDtypeStruct((rows, 2 * width), bf16),
        ],
        name="presplit",
    )(b, prev_b, next_b, a, *facts, *wait_for)


def repeated(parts, width):
    blocks = []
    for first in range(0, parts.shape[1], 2 * width):
        high = parts[:, first : first + width]
        blocks += [high, high, parts[:, first + width : first + 2 * width]]
    return jnp.concatenate(blocks, axis=1)


def finish_a_kernel(at_ref, mine_ref, other_ref, *refs):
    facts, (a_ref, parts_ref) = refs[:3], refs[3:5]
    out_ref, ready_ref, corr_ref, pen_ref, vec_ref = refs[-5:]

    @pl.when(pl.program_id(0) == 0)
    def _():
        ready_ref[...] = jnp.zeros_like(ready_ref)
        kinds = (0, 1, 2)
        cross = build(at_ref, mine_ref, other_ref, kinds, 0, corr_ref, pen_ref, True)
        left = jnp.concatenate([thrice(ref[...]) for ref in facts], axis=1)
        vec_ref[0:1, :] = mm(left, pen_ref[...])[5:6]
        vec_ref[1:2, :] = cross

    grad = mm(repeated(parts_ref[...], a_ref.shape[1]), pen_ref[...])
    inverse = facts[0][1:2, :]
    normed = (a_ref[...] - facts[0][0:1, :]) * inverse
    out_ref[...] = (grad - vec_ref[0:1, :] - normed * vec_ref[1:2, :]) * inverse


def finish_a(at, mine, other, facts, a, parts):
    rows, width = a.shape
    tile = 256
    spec = pl.BlockSpec((tile, width), lambda i: (i, 0))
    whole = pl.BlockSpec((8, width), lambda i: (0, 0))
    slots = pl.BlockSpec(mine.shape, lambda i: (0, 0, 0))
    return call(
        finish_a_kernel,
        mib=40,
        grid=(rows // tile,),
        in_specs=[smem_spec, slots, slots]
        + [whole] * 3
        + [spec, pl.BlockSpec((tile, 6 * width), lambda i: (i, 0))],
        out_specs=[spec, whole],
        out_shape=[shape(rows, width), shape(8, width)],
        scratch_shapes=scratch_for(3, width),
        name="finish_a",
    )(at, mine, other, *facts, a, parts)


def own_b_kernel(at_ref, mine_ref, other_ref, facts_ref, parts_ref, *refs):
    out_ref, sums_ref, corr_ref, pen_ref, _ = refs[-5:]

    @pl.when(pl.program_id(0) == 0)
    def _():
        sums_ref[...] = jnp.zeros_like(sums_ref)
        cross = build(at_ref, mine_ref, other_ref, (0,), 0, corr_ref, pen_ref, False)
        sums_ref[0:1, :] = mm(thrice(facts_ref[...]), pen_ref[...])[4:5]
        sums_ref[1:2, :] = cross

    out_ref[...] = mm(repeated(parts_ref[...], out_ref.shape[1]), pen_ref[...])


def own_b(at, mine, other, facts, parts, wait_for):
    rows, width = parts.shape[0], parts.shape[1] // 2
    tile = 256
    spec = pl.BlockSpec((tile, width), lambda i: (i, 0))
    whole = pl.BlockSpec((8, width), lambda i: (0, 0))
    slots = pl.BlockSpec(mine.shape, lambda i: (0, 0, 0))
    return call(
        own_b_kernel,
        mib=24,
        grid=(rows // tile,),
        in_specs=[smem_spec, slots, slots, whole]
        + [pl.BlockSpec((tile, 2 * width), lambda i: (i, 0))]
        + [any_spec] * len(wait_for),
        out_specs=[spec, whole],
        out_shape=[shape(rows, width), shape(8, width)],
        scratch_shapes=scratch_for(1, width),
        name="own_b",
    )(at, mine, other, facts, parts, *wait_for)


def finish_b_kernel(bounds, at_ref, mine_ref, other_ref, f_ref, pf_ref, nf_ref, *refs):
    sums_ref, part_ref, b_ref, *halos = refs[:15]
    out_ref, corr_ref, pen_ref, vec_ref = refs[-4:]
    step = pl.program_id(0)

    @pl.when(step == 0)
    def _():
        cross = build(at_ref, mine_ref, other_ref, (0, 1), 2, corr_ref, pen_ref, False)
        left = jnp.concatenate([thrice(pf_ref[...]), thrice(nf_ref[...])], axis=1)
        vec_ref[0:1, :] = sums_ref[0:1, :] + mm(left, pen_ref[...])[4:5]
        vec_ref[1:2, :] = sums_ref[1:2, :] + cross

    def current(parts):
        blocks = []
        for i in (0, 1):
            at = 2 * step + i
            rest = jnp.where(at < bounds[2], parts[3 * i + 1][...], parts[3 * i + 2][...])
            blocks.append(jnp.where(at < bounds[1], parts[3 * i][...], rest))
        return jnp.concatenate(blocks, axis=0)

    prev = current(halos[:6]) * pf_ref[6:7, :] + pf_ref[7:8, :]
    next_ = current(halos[6:]) * nf_ref[6:7, :] + nf_ref[7:8, :]
    both = jnp.concatenate([thrice(prev), thrice(next_)], axis=1)
    grad = part_ref[...] + mm(both, pen_ref[...])
    normed = (b_ref[...] - f_ref[2:3, :]) * f_ref[3:4, :]
    out_ref[...] = (grad - vec_ref[0:1, :] - normed * vec_ref[1:2, :]) * f_ref[3:4, :]


def finish_b(at, mine, other, facts, sums, part, b, halos):
    rows, width = b.shape
    block = 128
    tile = 2 * block
    _, bounds, maps = halo_cuts(rows, block)
    spec = pl.BlockSpec((tile, width), lambda i: (i, 0))
    parts = [
        pl.BlockSpec((block, width), lambda i, half=half, part=part: part(2 * i + half))
        for half in (0, 1)
        for part in maps
    ]
    whole = pl.BlockSpec((8, width), lambda i: (0, 0))
    slots = pl.BlockSpec(mine.shape, lambda i: (0, 0, 0))
    return call(
        functools.partial(finish_b_kernel, bounds),
        mib=24,
        grid=(rows // tile,),
        in_specs=[smem_spec, slots, slots] + [whole] * 4 + [spec] * 2 + parts * 2,
        out_specs=spec,
        out_shape=shape(rows, width),
        scratch_shapes=scratch_for(2, width),
        name="finish_b",
    )(at, mine, other, *facts, sums, part, b, *halos[:3] * 2, *halos[3:] * 2)


def per_device(view_a, view_b):
    local_rows, width = view_a.shape
    half_rows = local_rows * lax.axis_size("row") // 2
    index = lax.axis_index("row")
    at = jnp.stack([index & 1, (index >> 1) & 3])

    prev_raw = across(view_b, 1)
    next_raw = across(view_b, -1)
    sums = sums_of(view_a, view_b)
    sums = sums + to_core(sums)
    parts = [sums] + [to_x(sums, shift) for shift in (1, 2, 3)]

    a_top, a_mid, a_low, half_facts, keep, send, a_high_t, a_low_t = own_corr(
        at, view_a, view_b, parts, half_rows
    )
    slots = fan([keep], [to_core(send)])
    own_parts = [slots[0]] + [to_x(slots[shift], shift) for shift in (1, 2, 3)]
    own, a_top = own_sum(own_parts, a_top, half_facts)
    prev_top = across(a_top, 1)
    next_top = across(a_top, -1)

    left_keep, left_send = side_corr(at, a_high_t, a_low_t, prev_raw, [own])
    right_keep, right_send = side_corr(at, a_high_t, a_low_t, next_raw, [own])
    slots = joined_fan([left_keep, right_keep], [to_core(left_send), to_core(right_send)])
    side_parts = [slots[0]] + [to_x(slots[shift], shift) for shift in (1, 2, 3)]
    mine = message(own, side_parts, half_facts, prev_top, next_top)
    left, right, trio, *facts = merge(at, mine, to_y(mine), half_rows)
    from_next = across(left, -1)
    from_prev = across(right, 1)
    trio_slots = [trio] + [to_x(trio, shift) for shift in (1, 2, 3)]
    ends, a_mid, a_low = join(from_prev, from_next, [a_mid, a_low])
    prev_mid = across(a_mid, 1)
    next_mid = across(a_mid, -1)
    prev_low = across(a_low, 1)
    next_low = across(a_low, -1)
    end_slots = [ends] + [to_x(ends, shift) for shift in (1, 2, 3)]
    b_parts, a_parts = presplit(view_b, prev_raw, next_raw, view_a, facts, [ends])
    mine = pack(trio_slots, [a_parts, prev_mid, next_mid])
    other = to_core(mine)
    grad_a, ready = finish_a(at, mine, other, facts, view_a, b_parts)
    ends = pack(end_slots, [ready, prev_low, next_low])
    part_b, sums = own_b(at, mine, other, facts[0], a_parts, [ends])
    halos = [prev_top, prev_mid, prev_low, next_top, next_mid, next_low]
    grad_b = finish_b(at, ends, to_core(ends), facts, sums, part_b, view_b, halos)
    return (grad_a, grad_b)


def solution(mesh):
    placed = (P("row", "grp"), P("row", "grp"))
    return jax.shard_map(
        per_device,
        mesh=mesh,
        in_specs=placed,
        out_specs=(P("row", "grp"), P("row", "grp")),
        check_vma=False,
    )
```

```python
import functools

import jax
import jax.numpy as jnp
from jax import lax
from jax.experimental import pallas as pl
from jax.experimental.pallas import tpu as pltpu
from jax.sharding import PartitionSpec as P

epsilon = 1e-05
off_weight = 0.0051
f32 = jnp.float32
bf16 = jnp.bfloat16


any_spec = pl.BlockSpec(memory_space=pl.ANY)
smem_spec = pl.BlockSpec(memory_space=pltpu.SMEM)
vmem_spec = pl.BlockSpec(memory_space=pltpu.VMEM)
cheap = pl.CostEstimate(flops=1, transcendentals=0, bytes_accessed=1)
top_rows, mid_rows = 640, 128


def call(kernel, mib=8, **rest):
    params = pltpu.CompilerParams(vmem_limit_bytes=mib * 1024 * 1024)
    return pl.pallas_call(kernel, compiler_params=params, cost_estimate=cheap, **rest)


def shape(*dims):
    return jax.ShapeDtypeStruct(dims, f32)


def across(block, shift):
    count = lax.axis_size("grp")
    return lax.ppermute(block, "grp", [(i, (i + shift) % count) for i in range(count)])


def to_core(block):
    return lax.ppermute(block, "row", [(i, i ^ 1) for i in range(16)])


def to_y(block):
    return lax.ppermute(block, "row", [(i, i ^ 8) for i in range(16)])


def to_x(block, shift):
    pairs = [(i, (i & 9) | ((((i >> 1) + shift) & 3) << 1)) for i in range(16)]
    return lax.ppermute(block, "row", pairs)


def split(value):
    high = value.astype(bf16)
    return high, (value - high.astype(f32)).astype(bf16)


def mm(a, b):
    return lax.dot_general(a, b, (((1,), (0,)), ((), ())), preferred_element_type=f32)


def gram(a, b):
    a_high, a_low = split(a.T)
    b_high, b_low = split(b)
    return mm(
        jnp.concatenate([a_high, a_high, a_low], axis=1),
        jnp.concatenate([b_high, b_low, b_high], axis=0),
    )


def thrice(value):
    high, low = split(value)
    return jnp.concatenate([high, high, low], axis=1)


def sums_kernel(a_ref, b_ref, out_ref):
    @pl.when(pl.program_id(0) == 0)
    def _():
        out_ref[...] = jnp.zeros_like(out_ref)

    a, b = a_ref[...], b_ref[...]
    for row, value in enumerate((a, a * a, b, b * b)):
        out_ref[row : row + 1, :] += jnp.sum(value, axis=0, keepdims=True)


def sums_of(a, b):
    rows, width = a.shape
    tile = rows // 4
    spec = pl.BlockSpec((tile, width), lambda i: (i, 0))
    return call(
        sums_kernel,
        grid=(4,),
        in_specs=[spec, spec],
        out_specs=pl.BlockSpec((8, width), lambda i: (0, 0)),
        out_shape=shape(8, width),
        name="sums",
    )(a, b)


def put_slots(at_ref, acc, keep_ref, sends, first, rows):
    core, x = at_ref[0], at_ref[1]
    for slot in range(4):
        chunk = (x + slot) & 3
        mine = pl.multiple_of((core * 4 + chunk) * rows, rows)
        theirs = pl.multiple_of(((1 - core) * 4 + chunk) * rows, rows)
        keep_ref[slot, first : first + rows, :] = acc[pl.ds(mine, rows), :]
        each = 4 // len(sends)
        sends[slot // each][slot % each, first : first + rows, :] = acc[pl.ds(theirs, rows), :]


def own_corr_kernel(half_rows, steps, bounds, at_ref, a_ref, b_ref, *refs):
    parts, halos, (facts_ref, keep_ref, send_ref, acc_ref) = refs[:4], refs[4:7], refs[7:]
    step = pl.program_id(0)

    @pl.when(step == 0)
    def _():
        total = parts[0][...] + parts[1][...] + parts[2][...] + parts[3][...]
        total = total / half_rows
        for view in (0, 1):
            mean, square = total[2 * view : 2 * view + 1], total[2 * view + 1 : 2 * view + 2]
            scale = jnp.sqrt(jnp.maximum(square - mean * mean, 0.0) + epsilon)
            facts_ref[2 * view : 2 * view + 1, :] = mean
            facts_ref[2 * view + 1 : 2 * view + 2, :] = 1.0 / scale
            facts_ref[4 + view : 5 + view, :] = square
            facts_ref[6 + view : 7 + view, :] = scale
        acc_ref[...] = jnp.zeros_like(acc_ref)

    norm_a = (a_ref[...] - facts_ref[0:1, :]) * facts_ref[1:2, :]
    norm_b = (b_ref[...] - facts_ref[2:3, :]) * facts_ref[3:4, :]

    for ref, first, last in zip(halos, bounds[:-1], bounds[1:]):

        @pl.when((step >= first) & (step < last))
        def _(ref=ref):
            ref[...] = norm_a

    acc_ref[...] += gram(norm_a, norm_b)

    @pl.when(step == steps - 1)
    def _():
        put_slots(at_ref, acc_ref, keep_ref, [send_ref], 0, keep_ref.shape[1])


def halo_cuts(rows, tile):
    sizes = (top_rows, mid_rows, rows - top_rows - mid_rows)
    bounds = (0, sizes[0] // tile, (sizes[0] + sizes[1]) // tile, rows // tile)

    def spec(first, last):
        return lambda i: (jnp.clip(i - first, 0, last - first - 1), 0)

    maps = [spec(first, last) for first, last in zip(bounds[:-1], bounds[1:])]
    return sizes, bounds, maps


def own_corr(at, a, b, parts, half_rows):
    rows, width = a.shape
    tile = 128
    sizes, bounds, maps = halo_cuts(rows, tile)
    spec = pl.BlockSpec((tile, width), lambda i: (i, 0))
    whole = pl.BlockSpec((8, width), lambda i: (0, 0))
    slots = pl.BlockSpec((4, width // 8, width), lambda i: (0, 0, 0))
    return call(
        functools.partial(own_corr_kernel, half_rows, rows // tile, bounds),
        grid=(rows // tile,),
        in_specs=[smem_spec, spec, spec] + [whole] * 4,
        out_specs=[pl.BlockSpec((tile, width), part) for part in maps] + [whole, slots, slots],
        out_shape=[shape(size, width) for size in sizes]
        + [shape(8, width)]
        + [shape(4, width // 8, width)] * 2,
        scratch_shapes=[pltpu.VMEM((width, width), f32)],
        mib=16,
        name="own_corr",
    )(at, a, b, *parts)


def side_corr_kernel(steps, at_ref, a_ref, prev_ref, next_ref, f_ref, *refs):
    keep_ref, *sends, left_ref, right_ref = refs[-5:]
    step = pl.program_id(0)

    @pl.when(step == 0)
    def _():
        left_ref[...] = jnp.zeros_like(left_ref)
        right_ref[...] = jnp.zeros_like(right_ref)

    norm_a = (a_ref[...] - f_ref[0:1, :]) * f_ref[1:2, :]
    for acc_ref, b_ref in ((left_ref, prev_ref), (right_ref, next_ref)):
        acc_ref[...] += gram(norm_a, b_ref[...])

    @pl.when(step == steps - 1)
    def _():
        rows = keep_ref.shape[1] // 2
        put_slots(at_ref, left_ref, keep_ref, sends, 0, rows)
        put_slots(at_ref, right_ref, keep_ref, sends, rows, rows)


def side_corr(at, a, prev_b, next_b, facts, wait_for):
    rows, width = a.shape
    steps = 4
    spec = pl.BlockSpec((rows // steps, width), lambda i: (i, 0))
    whole = pl.BlockSpec((8, width), lambda i: (0, 0))
    slots = pl.BlockSpec((4, width // 4, width), lambda i: (0, 0, 0))
    pair = pl.BlockSpec((2, width // 4, width), lambda i: (0, 0, 0))
    return call(
        functools.partial(side_corr_kernel, steps),
        grid=(steps,),
        in_specs=[smem_spec, spec, spec, spec, whole] + [any_spec] * len(wait_for),
        out_specs=[slots, pair, pair],
        out_shape=[shape(4, width // 4, width)] + [shape(2, width // 4, width)] * 2,
        scratch_shapes=[pltpu.VMEM((width, width), f32)] * 2,
        mib=24,
        name="side_corr",
    )(at, a, prev_b, next_b, facts, *wait_for)


def fan_kernel(keep_ref, *refs):
    gots, outs = refs[:-4], refs[-4:]
    each = 4 // len(gots)
    for slot in range(4):
        outs[slot][...] = keep_ref[slot] + gots[slot // each][slot % each]


def fan(keep, *gots):
    return call(
        fan_kernel,
        in_specs=[vmem_spec] * (1 + len(gots)),
        out_specs=[vmem_spec] * 4,
        out_shape=[shape(*keep.shape[1:])] * 4,
        name="fan",
    )(keep, *gots)


def own_sum_kernel(*refs):
    top_ref, facts_ref, sum_ref, halo_ref = refs[4:]
    sum_ref[...] = refs[0][...] + refs[1][...] + refs[2][...] + refs[3][...]
    rows = top_ref.shape[0]
    halo_ref[0:rows, :] = top_ref[...]
    halo_ref[rows:, :] = facts_ref[...]


def own_sum(parts, top, facts):
    rows, width = top.shape
    return call(
        own_sum_kernel,
        in_specs=[vmem_spec] * 6,
        out_specs=[vmem_spec] * 2,
        out_shape=[shape(*parts[0].shape), shape(rows + 8, width)],
        name="own_sum",
    )(*parts, top, facts)


def message_kernel(own_ref, *refs):
    side, facts, out_ref = refs[:4], refs[4:7], refs[7]
    first = own_ref.shape[0]
    last = first + side[0].shape[0]
    out_ref[0:first, :] = own_ref[...]
    out_ref[first:last, :] = side[0][...] + side[1][...] + side[2][...] + side[3][...]
    for i, ref in enumerate(facts):
        out_ref[last + 8 * i : last + 8 * i + 8, :] = ref[...]


def message(own, side, facts, prev_top, next_top):
    rows = own.shape[0] + side[0].shape[0] + 24
    width = own.shape[1]
    below = pl.BlockSpec((8, width), lambda i: (top_rows // 8, 0))
    wholes = [pl.BlockSpec(block.shape, lambda i: (0, 0)) for block in (own, *side, facts)]
    return call(
        message_kernel,
        grid=(1,),
        in_specs=wholes + [below] * 2,
        out_specs=pl.BlockSpec((rows, width), lambda i: (0, 0)),
        out_shape=shape(rows, width),
        name="message",
    )(own, *side, facts, prev_top, next_top)


def full_facts(mine, other):
    rows = []
    for view in (0, 1):
        mean = 0.5 * (mine[2 * view : 2 * view + 1] + other[2 * view : 2 * view + 1])
        square = 0.5 * (mine[4 + view : 5 + view] + other[4 + view : 5 + view])
        rows += [mean, 1.0 / jnp.sqrt(square - mean * mean + epsilon)]
    for view in (0, 1):
        average = 0.5 * (mine[2 * view : 2 * view + 1] + other[2 * view : 2 * view + 1])
        rows.append((average - rows[2 * view]) * rows[2 * view + 1])
    rows += [mine[6:7] * rows[1], (mine[0:1] - rows[0]) * rows[1]]
    return rows


def merged(mine, other, a_cols, b_mine, b_other, b_full, half_rows, raw_b):
    scale0, scale1, diff0, diff1, inverse = (a_cols[:, i : i + 1] for i in range(5))
    if not raw_b:
        mine, other = mine * b_mine[7:8], other * b_other[7:8]
    out = mine * scale0 + other * scale1
    shift0, shift1 = b_mine[2:3] - b_full[2], b_other[2:3] - b_full[2]
    out = out + half_rows * (diff0 * shift0 + diff1 * shift1)
    return out * (inverse * (b_full[3] * (0.5 / half_rows)))


def columns_of(at_ref, mine, other, full, cols_ref, rows):
    width = mine.shape[1]
    stack = [mine[6:7], other[6:7], mine[0:1] - full[0], other[0:1] - full[0], full[1]]
    stack = jnp.concatenate(stack + [jnp.zeros((123, width), f32)], axis=0)
    cols_ref[...] = stack.T
    first = pl.multiple_of((at_ref[0] * 4 + at_ref[1]) * rows, rows)
    return cols_ref[pl.ds(first, rows), :]


def merge_kernel(half_rows, at_ref, mine_ref, got_ref, *refs):
    left_ref, right_ref, trio_ref, *facts_refs, cols_ref = refs[-7:]
    rows = left_ref.shape[0]
    facts = [
        (mine_ref[first : first + 8, :], got_ref[first : first + 8, :])
        for first in (3 * rows, 3 * rows + 8, 3 * rows + 16)
    ]
    full = [full_facts(*both) for both in facts]
    for ref, values in zip(facts_refs, full):
        for i in range(8):
            ref[i : i + 1, :] = values[i]
    cols = columns_of(at_ref, *facts[0], full[0], cols_ref, rows)
    for kind in range(3):
        first = kind * rows
        chunk = merged(
            mine_ref[first : first + rows, :],
            got_ref[first : first + rows, :],
            cols,
            *facts[kind],
            full[kind],
            half_rows,
            kind > 0,
        )
        trio_ref[first : first + rows, :] = chunk
        if kind == 1:
            left_ref[...] = chunk
        if kind == 2:
            right_ref[...] = chunk


def merge(at, mine, got, half_rows):
    width = mine.shape[1]
    rows = (mine.shape[0] - 24) // 3
    return call(
        functools.partial(merge_kernel, half_rows),
        in_specs=[smem_spec] + [vmem_spec] * 2,
        out_specs=[vmem_spec] * 6,
        out_shape=[shape(rows, width)] * 2 + [shape(3 * rows, width)] + [shape(8, width)] * 3,
        scratch_shapes=[pltpu.VMEM((width, 128), f32)],
        name="merge",
    )(at, mine, got)


def pack(parts, wait_for=()):
    rows, width = parts[0].shape

    def kernel(*refs):
        for i in range(4):
            refs[-1][i] = refs[i][...]

    return call(
        kernel,
        in_specs=[vmem_spec] * 4 + [any_spec] * len(wait_for),
        out_specs=vmem_spec,
        out_shape=shape(4, rows, width),
        name="pack",
    )(*parts, *wait_for)


def join(first, second, carried):
    rows, width = first.shape
    count = len(carried)

    def kernel(first_ref, second_ref, *refs):
        refs[count][0:rows, :] = first_ref[...]
        refs[count][rows:, :] = second_ref[...]

    return call(
        kernel,
        in_specs=[vmem_spec] * 2 + [any_spec] * count,
        out_specs=[vmem_spec] + [any_spec] * count,
        out_shape=[shape(2 * rows, width)] + [shape(*c.shape) for c in carried],
        input_output_aliases={2 + i: 1 + i for i in range(count)},
        name="join",
    )(first, second, *carried)


def row_of(at_ref, core_flip, slot, rows):
    core, x = at_ref[0], at_ref[1]
    core = 1 - core if core_flip else core
    return pl.multiple_of((core * 4 + ((x - slot) & 3)) * rows, rows)


def build(at_ref, mine_ref, other_ref, kinds, own, corr_ref, pen_ref, transposed):
    width = corr_ref.shape[1]
    rows = width // 8
    for flip, ref in ((False, mine_ref), (True, other_ref)):
        for slot in range(4):
            at = row_of(at_ref, flip, slot, rows)
            for i, kind in enumerate(kinds):
                corr_ref[i, pl.ds(at, rows), :] = ref[slot, kind * rows : (kind + 1) * rows, :]
    cross = jnp.zeros((1, width), f32)
    for i, kind in enumerate(kinds):
        corr = corr_ref[i]
        corr = corr.T if transposed else corr
        pen = 2.0 * off_weight * corr
        if kind == own:
            row_index = lax.broadcasted_iota(jnp.int32, corr.shape, 0)
            column = lax.broadcasted_iota(jnp.int32, corr.shape, 1)
            pen = jnp.where(row_index == column, -2.0 * (1.0 - corr), pen)
        cross = cross + jnp.sum(pen * corr, axis=0, keepdims=True)
        high, low = split(pen)
        first = i * 3 * width
        pen_ref[first : first + width, :] = high
        pen_ref[first + width : first + 2 * width, :] = low
        pen_ref[first + 2 * width : first + 3 * width, :] = high
    return cross


def scratch_for(kinds, width):
    return [
        pltpu.VMEM((kinds, width, width), f32),
        pltpu.VMEM((3 * kinds * width, width), bf16),
        pltpu.VMEM((8, width), f32),
    ]


def presplit_kernel(b_ref, prev_ref, next_ref, a_ref, f_ref, pf_ref, nf_ref, *refs):
    bs_ref, a_out_ref = refs[-2:]
    width = a_ref.shape[1]
    for kind, (ref, facts_ref) in enumerate(
        ((b_ref, f_ref), (prev_ref, pf_ref), (next_ref, nf_ref))
    ):
        high, low = split((ref[...] - facts_ref[2:3, :]) * facts_ref[3:4, :])
        bs_ref[:, 2 * kind * width : (2 * kind + 1) * width] = high
        bs_ref[:, (2 * kind + 1) * width : (2 * kind + 2) * width] = low
    high, low = split((a_ref[...] - f_ref[0:1, :]) * f_ref[1:2, :])
    a_out_ref[:, 0:width] = high
    a_out_ref[:, width:] = low


def presplit(b, prev_b, next_b, a, facts, wait_for):
    rows, width = a.shape
    tile = 256
    spec = pl.BlockSpec((tile, width), lambda i: (i, 0))
    whole = pl.BlockSpec((8, width), lambda i: (0, 0))
    return call(
        presplit_kernel,
        mib=16,
        grid=(rows // tile,),
        in_specs=[spec] * 4 + [whole] * 3 + [any_spec] * len(wait_for),
        out_specs=[
            pl.BlockSpec((tile, 6 * width), lambda i: (i, 0)),
            pl.BlockSpec((tile, 2 * width), lambda i: (i, 0)),
        ],
        out_shape=[
            jax.ShapeDtypeStruct((rows, 6 * width), bf16),
            jax.ShapeDtypeStruct((rows, 2 * width), bf16),
        ],
        name="presplit",
    )(b, prev_b, next_b, a, *facts, *wait_for)


def repeated(parts, width):
    blocks = []
    for first in range(0, parts.shape[1], 2 * width):
        high = parts[:, first : first + width]
        blocks += [high, high, parts[:, first + width : first + 2 * width]]
    return jnp.concatenate(blocks, axis=1)


def finish_a_kernel(at_ref, mine_ref, other_ref, *refs):
    facts, (a_ref, parts_ref) = refs[:3], refs[3:5]
    out_ref, ready_ref, corr_ref, pen_ref, vec_ref = refs[-5:]

    @pl.when(pl.program_id(0) == 0)
    def _():
        ready_ref[...] = jnp.zeros_like(ready_ref)
        kinds = (0, 1, 2)
        cross = build(at_ref, mine_ref, other_ref, kinds, 0, corr_ref, pen_ref, True)
        left = jnp.concatenate([thrice(ref[...]) for ref in facts], axis=1)
        vec_ref[0:1, :] = mm(left, pen_ref[...])[5:6]
        vec_ref[1:2, :] = cross

    grad = mm(repeated(parts_ref[...], a_ref.shape[1]), pen_ref[...])
    inverse = facts[0][1:2, :]
    normed = (a_ref[...] - facts[0][0:1, :]) * inverse
    out_ref[...] = (grad - vec_ref[0:1, :] - normed * vec_ref[1:2, :]) * inverse


def finish_a(at, mine, other, facts, a, parts):
    rows, width = a.shape
    tile = 512
    spec = pl.BlockSpec((tile, width), lambda i: (i, 0))
    whole = pl.BlockSpec((8, width), lambda i: (0, 0))
    slots = pl.BlockSpec(mine.shape, lambda i: (0, 0, 0))
    return call(
        finish_a_kernel,
        mib=40,
        grid=(rows // tile,),
        in_specs=[smem_spec, slots, slots]
        + [whole] * 3
        + [spec, pl.BlockSpec((tile, 6 * width), lambda i: (i, 0))],
        out_specs=[spec, whole],
        out_shape=[shape(rows, width), shape(8, width)],
        scratch_shapes=scratch_for(3, width),
        name="finish_a",
    )(at, mine, other, *facts, a, parts)


def own_b_kernel(at_ref, mine_ref, other_ref, facts_ref, parts_ref, *refs):
    out_ref, sums_ref, corr_ref, pen_ref, _ = refs[-5:]

    @pl.when(pl.program_id(0) == 0)
    def _():
        sums_ref[...] = jnp.zeros_like(sums_ref)
        cross = build(at_ref, mine_ref, other_ref, (0,), 0, corr_ref, pen_ref, False)
        sums_ref[0:1, :] = mm(thrice(facts_ref[...]), pen_ref[...])[4:5]
        sums_ref[1:2, :] = cross

    out_ref[...] = mm(repeated(parts_ref[...], out_ref.shape[1]), pen_ref[...])


def own_b(at, mine, other, facts, parts, wait_for):
    rows, width = parts.shape[0], parts.shape[1] // 2
    tile = 512
    spec = pl.BlockSpec((tile, width), lambda i: (i, 0))
    whole = pl.BlockSpec((8, width), lambda i: (0, 0))
    slots = pl.BlockSpec(mine.shape, lambda i: (0, 0, 0))
    return call(
        own_b_kernel,
        mib=24,
        grid=(rows // tile,),
        in_specs=[smem_spec, slots, slots, whole]
        + [pl.BlockSpec((tile, 2 * width), lambda i: (i, 0))]
        + [any_spec] * len(wait_for),
        out_specs=[spec, whole],
        out_shape=[shape(rows, width), shape(8, width)],
        scratch_shapes=scratch_for(1, width),
        name="own_b",
    )(at, mine, other, facts, parts, *wait_for)


def finish_b_kernel(bounds, at_ref, mine_ref, other_ref, f_ref, pf_ref, nf_ref, *refs):
    sums_ref, part_ref, b_ref, *halos = refs[:15]
    out_ref, corr_ref, pen_ref, vec_ref = refs[-4:]
    step = pl.program_id(0)

    @pl.when(step == 0)
    def _():
        cross = build(at_ref, mine_ref, other_ref, (0, 1), 2, corr_ref, pen_ref, False)
        left = jnp.concatenate([thrice(pf_ref[...]), thrice(nf_ref[...])], axis=1)
        vec_ref[0:1, :] = sums_ref[0:1, :] + mm(left, pen_ref[...])[4:5]
        vec_ref[1:2, :] = sums_ref[1:2, :] + cross

    def current(parts):
        blocks = []
        for i in (0, 1):
            at = 2 * step + i
            rest = jnp.where(at < bounds[2], parts[3 * i + 1][...], parts[3 * i + 2][...])
            blocks.append(jnp.where(at < bounds[1], parts[3 * i][...], rest))
        return jnp.concatenate(blocks, axis=0)

    prev = current(halos[:6]) * pf_ref[6:7, :] + pf_ref[7:8, :]
    next_ = current(halos[6:]) * nf_ref[6:7, :] + nf_ref[7:8, :]
    both = jnp.concatenate([thrice(prev), thrice(next_)], axis=1)
    grad = part_ref[...] + mm(both, pen_ref[...])
    normed = (b_ref[...] - f_ref[2:3, :]) * f_ref[3:4, :]
    out_ref[...] = (grad - vec_ref[0:1, :] - normed * vec_ref[1:2, :]) * f_ref[3:4, :]


def finish_b(at, mine, other, facts, sums, part, b, halos):
    rows, width = b.shape
    block = 128
    tile = 2 * block
    _, bounds, maps = halo_cuts(rows, block)
    spec = pl.BlockSpec((tile, width), lambda i: (i, 0))
    parts = [
        pl.BlockSpec((block, width), lambda i, half=half, part=part: part(2 * i + half))
        for half in (0, 1)
        for part in maps
    ]
    whole = pl.BlockSpec((8, width), lambda i: (0, 0))
    slots = pl.BlockSpec(mine.shape, lambda i: (0, 0, 0))
    return call(
        functools.partial(finish_b_kernel, bounds),
        mib=24,
        grid=(rows // tile,),
        in_specs=[smem_spec, slots, slots] + [whole] * 4 + [spec] * 2 + parts * 2,
        out_specs=spec,
        out_shape=shape(rows, width),
        scratch_shapes=scratch_for(2, width),
        name="finish_b",
    )(at, mine, other, *facts, sums, part, b, *halos[:3] * 2, *halos[3:] * 2)


def per_device(view_a, view_b):
    local_rows, width = view_a.shape
    half_rows = local_rows * lax.axis_size("row") // 2
    index = lax.axis_index("row")
    at = jnp.stack([index & 1, (index >> 1) & 3])

    prev_raw = across(view_b, 1)
    next_raw = across(view_b, -1)
    sums = sums_of(view_a, view_b)
    sums = sums + to_core(sums)
    parts = [sums] + [to_x(sums, shift) for shift in (1, 2, 3)]

    a_top, a_mid, a_low, half_facts, keep, send = own_corr(at, view_a, view_b, parts, half_rows)
    slots = fan(keep, to_core(send))
    own_parts = [slots[0]] + [to_x(slots[shift], shift) for shift in (1, 2, 3)]
    own, a_top = own_sum(own_parts, a_top, half_facts)
    prev_top = across(a_top, 1)
    next_top = across(a_top, -1)

    keep, *sends = side_corr(at, view_a, prev_raw, next_raw, half_facts, [own])
    slots = fan(keep, *[to_core(send) for send in sends])
    side_parts = [slots[0]] + [to_x(slots[shift], shift) for shift in (1, 2, 3)]
    mine = message(own, side_parts, half_facts, prev_top, next_top)
    left, right, trio, *facts = merge(at, mine, to_y(mine), half_rows)
    from_next = across(left, -1)
    from_prev = across(right, 1)
    trio_slots = [trio] + [to_x(trio, shift) for shift in (1, 2, 3)]
    ends, a_mid, a_low = join(from_prev, from_next, [a_mid, a_low])
    prev_mid = across(a_mid, 1)
    next_mid = across(a_mid, -1)
    prev_low = across(a_low, 1)
    next_low = across(a_low, -1)
    end_slots = [ends] + [to_x(ends, shift) for shift in (1, 2, 3)]
    b_parts, a_parts = presplit(view_b, prev_raw, next_raw, view_a, facts, [ends])
    mine = pack(trio_slots, [a_parts, prev_mid, next_mid])
    other = to_core(mine)
    grad_a, ready = finish_a(at, mine, other, facts, view_a, b_parts)
    ends = pack(end_slots, [ready, prev_low, next_low])
    part_b, sums = own_b(at, mine, other, facts[0], a_parts, [ends])
    halos = [prev_top, prev_mid, prev_low, next_top, next_mid, next_low]
    grad_b = finish_b(at, ends, to_core(ends), facts, sums, part_b, view_b, halos)
    return (grad_a, grad_b)


def solution(mesh):
    placed = (P("row", "grp"), P("row", "grp"))
    return jax.shard_map(
        per_device,
        mesh=mesh,
        in_specs=placed,
        out_specs=(P("row", "grp"), P("row", "grp")),
        check_vma=False,
    )
```

```python
import functools

import jax
import jax.numpy as jnp
from jax import lax
from jax.experimental import pallas as pl
from jax.experimental.pallas import tpu as pltpu
from jax.sharding import PartitionSpec as P

epsilon = 1e-05
off_weight = 0.0051
f32 = jnp.float32
bf16 = jnp.bfloat16


any_spec = pl.BlockSpec(memory_space=pl.ANY)
smem_spec = pl.BlockSpec(memory_space=pltpu.SMEM)
vmem_spec = pl.BlockSpec(memory_space=pltpu.VMEM)
cheap = pl.CostEstimate(flops=1, transcendentals=0, bytes_accessed=1)
top_rows, mid_rows = 640, 128


def call(kernel, mib=8, **rest):
    params = pltpu.CompilerParams(vmem_limit_bytes=mib * 1024 * 1024)
    return pl.pallas_call(kernel, compiler_params=params, cost_estimate=cheap, **rest)


def shape(*dims):
    return jax.ShapeDtypeStruct(dims, f32)


def across(block, shift):
    count = lax.axis_size("grp")
    return lax.ppermute(block, "grp", [(i, (i + shift) % count) for i in range(count)])


def to_core(block):
    return lax.ppermute(block, "row", [(i, i ^ 1) for i in range(16)])


def to_y(block):
    return lax.ppermute(block, "row", [(i, i ^ 8) for i in range(16)])


def to_x(block, shift):
    pairs = [(i, (i & 9) | ((((i >> 1) + shift) & 3) << 1)) for i in range(16)]
    return lax.ppermute(block, "row", pairs)


def split(value):
    high = value.astype(bf16)
    return high, (value - high.astype(f32)).astype(bf16)


def mm(a, b):
    return lax.dot_general(a, b, (((1,), (0,)), ((), ())), preferred_element_type=f32)


def gram(a, b):
    a_high, a_low = split(a.T)
    b_high, b_low = split(b)
    return mm(
        jnp.concatenate([a_high, a_high, a_low], axis=1),
        jnp.concatenate([b_high, b_low, b_high], axis=0),
    )


def thrice(value):
    high, low = split(value)
    return jnp.concatenate([high, high, low], axis=1)


def sums_kernel(a_ref, b_ref, out_ref):
    @pl.when(pl.program_id(0) == 0)
    def _():
        out_ref[...] = jnp.zeros_like(out_ref)

    a, b = a_ref[...], b_ref[...]
    for row, value in enumerate((a, a * a, b, b * b)):
        out_ref[row : row + 1, :] += jnp.sum(value, axis=0, keepdims=True)


def sums_of(a, b):
    rows, width = a.shape
    tile = rows // 4
    spec = pl.BlockSpec((tile, width), lambda i: (i, 0))
    return call(
        sums_kernel,
        grid=(4,),
        in_specs=[spec, spec],
        out_specs=pl.BlockSpec((8, width), lambda i: (0, 0)),
        out_shape=shape(8, width),
        name="sums",
    )(a, b)


def put_slots(at_ref, acc, keep_ref, sends, first, rows):
    core, x = at_ref[0], at_ref[1]
    for slot in range(4):
        chunk = (x + slot) & 3
        mine = pl.multiple_of((core * 4 + chunk) * rows, rows)
        theirs = pl.multiple_of(((1 - core) * 4 + chunk) * rows, rows)
        keep_ref[slot, first : first + rows, :] = acc[pl.ds(mine, rows), :]
        each = 4 // len(sends)
        sends[slot // each][slot % each, first : first + rows, :] = acc[pl.ds(theirs, rows), :]


def own_corr_kernel(half_rows, steps, bounds, at_ref, a_ref, b_ref, *refs):
    parts, halos, (facts_ref, keep_ref, send_ref, acc_ref) = refs[:4], refs[4:7], refs[7:]
    step = pl.program_id(0)

    @pl.when(step == 0)
    def _():
        total = parts[0][...] + parts[1][...] + parts[2][...] + parts[3][...]
        total = total / half_rows
        for view in (0, 1):
            mean, square = total[2 * view : 2 * view + 1], total[2 * view + 1 : 2 * view + 2]
            scale = jnp.sqrt(jnp.maximum(square - mean * mean, 0.0) + epsilon)
            facts_ref[2 * view : 2 * view + 1, :] = mean
            facts_ref[2 * view + 1 : 2 * view + 2, :] = 1.0 / scale
            facts_ref[4 + view : 5 + view, :] = square
            facts_ref[6 + view : 7 + view, :] = scale
        acc_ref[...] = jnp.zeros_like(acc_ref)

    norm_a = (a_ref[...] - facts_ref[0:1, :]) * facts_ref[1:2, :]
    norm_b = (b_ref[...] - facts_ref[2:3, :]) * facts_ref[3:4, :]

    for ref, first, last in zip(halos, bounds[:-1], bounds[1:]):

        @pl.when((step >= first) & (step < last))
        def _(ref=ref):
            ref[...] = norm_a

    acc_ref[...] += gram(norm_a, norm_b)

    @pl.when(step == steps - 1)
    def _():
        put_slots(at_ref, acc_ref, keep_ref, [send_ref], 0, keep_ref.shape[1])


def halo_cuts(rows, tile):
    sizes = (top_rows, mid_rows, rows - top_rows - mid_rows)
    bounds = (0, sizes[0] // tile, (sizes[0] + sizes[1]) // tile, rows // tile)

    def spec(first, last):
        return lambda i: (jnp.clip(i - first, 0, last - first - 1), 0)

    maps = [spec(first, last) for first, last in zip(bounds[:-1], bounds[1:])]
    return sizes, bounds, maps


def own_corr(at, a, b, parts, half_rows):
    rows, width = a.shape
    tile = 128
    sizes, bounds, maps = halo_cuts(rows, tile)
    spec = pl.BlockSpec((tile, width), lambda i: (i, 0))
    whole = pl.BlockSpec((8, width), lambda i: (0, 0))
    slots = pl.BlockSpec((4, width // 8, width), lambda i: (0, 0, 0))
    return call(
        functools.partial(own_corr_kernel, half_rows, rows // tile, bounds),
        grid=(rows // tile,),
        in_specs=[smem_spec, spec, spec] + [whole] * 4,
        out_specs=[pl.BlockSpec((tile, width), part) for part in maps] + [whole, slots, slots],
        out_shape=[shape(size, width) for size in sizes]
        + [shape(8, width)]
        + [shape(4, width // 8, width)] * 2,
        scratch_shapes=[pltpu.VMEM((width, width), f32)],
        mib=16,
        name="own_corr",
    )(at, a, b, *parts)


def side_corr_kernel(steps, at_ref, a_ref, prev_ref, next_ref, f_ref, *refs):
    keep_ref, *sends, left_ref, right_ref = refs[-5:]
    step = pl.program_id(0)

    @pl.when(step == 0)
    def _():
        left_ref[...] = jnp.zeros_like(left_ref)
        right_ref[...] = jnp.zeros_like(right_ref)

    norm_a = (a_ref[...] - f_ref[0:1, :]) * f_ref[1:2, :]
    for acc_ref, b_ref in ((left_ref, prev_ref), (right_ref, next_ref)):
        acc_ref[...] += gram(norm_a, b_ref[...])

    @pl.when(step == steps - 1)
    def _():
        rows = keep_ref.shape[1] // 2
        put_slots(at_ref, left_ref, keep_ref, sends, 0, rows)
        put_slots(at_ref, right_ref, keep_ref, sends, rows, rows)


def side_corr(at, a, prev_b, next_b, facts, wait_for):
    rows, width = a.shape
    steps = 4
    spec = pl.BlockSpec((rows // steps, width), lambda i: (i, 0))
    whole = pl.BlockSpec((8, width), lambda i: (0, 0))
    slots = pl.BlockSpec((4, width // 4, width), lambda i: (0, 0, 0))
    pair = pl.BlockSpec((2, width // 4, width), lambda i: (0, 0, 0))
    return call(
        functools.partial(side_corr_kernel, steps),
        grid=(steps,),
        in_specs=[smem_spec, spec, spec, spec, whole] + [any_spec] * len(wait_for),
        out_specs=[slots, pair, pair],
        out_shape=[shape(4, width // 4, width)] + [shape(2, width // 4, width)] * 2,
        scratch_shapes=[pltpu.VMEM((width, width), f32)] * 2,
        mib=24,
        name="side_corr",
    )(at, a, prev_b, next_b, facts, *wait_for)


def fan_kernel(keep_ref, *refs):
    gots, outs = refs[:-4], refs[-4:]
    each = 4 // len(gots)
    for slot in range(4):
        outs[slot][...] = keep_ref[slot] + gots[slot // each][slot % each]


def fan(keep, *gots):
    return call(
        fan_kernel,
        in_specs=[vmem_spec] * (1 + len(gots)),
        out_specs=[vmem_spec] * 4,
        out_shape=[shape(*keep.shape[1:])] * 4,
        name="fan",
    )(keep, *gots)


def own_sum_kernel(*refs):
    top_ref, facts_ref, sum_ref, halo_ref = refs[4:]
    sum_ref[...] = refs[0][...] + refs[1][...] + refs[2][...] + refs[3][...]
    rows = top_ref.shape[0]
    halo_ref[0:rows, :] = top_ref[...]
    halo_ref[rows:, :] = facts_ref[...]


def own_sum(parts, top, facts):
    rows, width = top.shape
    return call(
        own_sum_kernel,
        in_specs=[vmem_spec] * 6,
        out_specs=[vmem_spec] * 2,
        out_shape=[shape(*parts[0].shape), shape(rows + 8, width)],
        name="own_sum",
    )(*parts, top, facts)


def message_kernel(own_ref, *refs):
    side, facts, out_ref = refs[:4], refs[4:7], refs[7]
    first = own_ref.shape[0]
    last = first + side[0].shape[0]
    out_ref[0:first, :] = own_ref[...]
    out_ref[first:last, :] = side[0][...] + side[1][...] + side[2][...] + side[3][...]
    out_ref[last : last + 8, :] = facts[0][...]
    for i, ref in enumerate(facts[1:]):
        for j, row in enumerate((0, 2, 4, 5)):
            at = last + 8 + 4 * i + j
            out_ref[at : at + 1, :] = ref[row : row + 1, :]


def message(own, side, facts, prev_top, next_top):
    rows = own.shape[0] + side[0].shape[0] + 16
    width = own.shape[1]
    below = pl.BlockSpec((8, width), lambda i: (top_rows // 8, 0))
    wholes = [pl.BlockSpec(block.shape, lambda i: (0, 0)) for block in (own, *side, facts)]
    return call(
        message_kernel,
        grid=(1,),
        in_specs=wholes + [below] * 2,
        out_specs=pl.BlockSpec((rows, width), lambda i: (0, 0)),
        out_shape=shape(rows, width),
        name="message",
    )(own, *side, facts, prev_top, next_top)


def full_facts(mine, other):
    rows = []
    for view in (0, 1):
        mean = 0.5 * (mine[2 * view : 2 * view + 1] + other[2 * view : 2 * view + 1])
        square = 0.5 * (mine[4 + view : 5 + view] + other[4 + view : 5 + view])
        rows += [mean, 1.0 / jnp.sqrt(square - mean * mean + epsilon)]
    for view in (0, 1):
        average = 0.5 * (mine[2 * view : 2 * view + 1] + other[2 * view : 2 * view + 1])
        rows.append((average - rows[2 * view]) * rows[2 * view + 1])
    rows += [mine[6:7] * rows[1], (mine[0:1] - rows[0]) * rows[1]]
    return rows


def merged(mine, other, a_cols, b_mine, b_other, b_full, half_rows, raw_b):
    scale0, scale1, diff0, diff1, inverse = (a_cols[:, i : i + 1] for i in range(5))
    if not raw_b:
        mine, other = mine * b_mine[7:8], other * b_other[7:8]
    out = mine * scale0 + other * scale1
    shift0, shift1 = b_mine[2:3] - b_full[2], b_other[2:3] - b_full[2]
    out = out + half_rows * (diff0 * shift0 + diff1 * shift1)
    return out * (inverse * (b_full[3] * (0.5 / half_rows)))


def columns_of(at_ref, mine, other, full, cols_ref, rows):
    width = mine.shape[1]
    stack = [mine[6:7], other[6:7], mine[0:1] - full[0], other[0:1] - full[0], full[1]]
    stack = jnp.concatenate(stack + [jnp.zeros((123, width), f32)], axis=0)
    cols_ref[...] = stack.T
    first = pl.multiple_of((at_ref[0] * 4 + at_ref[1]) * rows, rows)
    return cols_ref[pl.ds(first, rows), :]


def lengthened(short):
    mean, square = short[0:2], short[2:4]
    scale = jnp.sqrt(jnp.maximum(square - mean * mean, 0.0) + epsilon)
    return jnp.concatenate([mean[0:1], mean[0:1], mean[1:2], mean[1:2], square, scale], axis=0)


def merge_kernel(half_rows, at_ref, mine_ref, got_ref, *refs):
    left_ref, right_ref, trio_ref, *facts_refs, cols_ref = refs[-7:]
    rows = left_ref.shape[0]
    first = 3 * rows
    facts = [(mine_ref[first : first + 8, :], got_ref[first : first + 8, :])]
    for first in (3 * rows + 8, 3 * rows + 12):
        short = mine_ref[first : first + 4, :], got_ref[first : first + 4, :]
        facts.append(tuple(lengthened(rows) for rows in short))
    full = [full_facts(*both) for both in facts]
    for ref, values in zip(facts_refs, full):
        for i in range(8):
            ref[i : i + 1, :] = values[i]
    cols = columns_of(at_ref, *facts[0], full[0], cols_ref, rows)
    for kind in range(3):
        first = kind * rows
        chunk = merged(
            mine_ref[first : first + rows, :],
            got_ref[first : first + rows, :],
            cols,
            *facts[kind],
            full[kind],
            half_rows,
            kind > 0,
        )
        trio_ref[first : first + rows, :] = chunk
        if kind == 1:
            left_ref[...] = chunk
        if kind == 2:
            right_ref[...] = chunk


def merge(at, mine, got, half_rows):
    width = mine.shape[1]
    rows = (mine.shape[0] - 16) // 3
    return call(
        functools.partial(merge_kernel, half_rows),
        in_specs=[smem_spec] + [vmem_spec] * 2,
        out_specs=[vmem_spec] * 6,
        out_shape=[shape(rows, width)] * 2 + [shape(3 * rows, width)] + [shape(8, width)] * 3,
        scratch_shapes=[pltpu.VMEM((width, 128), f32)],
        name="merge",
    )(at, mine, got)


def pack(parts, wait_for=()):
    rows, width = parts[0].shape

    def kernel(*refs):
        for i in range(4):
            refs[-1][i] = refs[i][...]

    return call(
        kernel,
        in_specs=[vmem_spec] * 4 + [any_spec] * len(wait_for),
        out_specs=vmem_spec,
        out_shape=shape(4, rows, width),
        name="pack",
    )(*parts, *wait_for)


def join(first, second, carried):
    rows, width = first.shape
    count = len(carried)

    def kernel(first_ref, second_ref, *refs):
        refs[count][0:rows, :] = first_ref[...]
        refs[count][rows:, :] = second_ref[...]

    return call(
        kernel,
        in_specs=[vmem_spec] * 2 + [any_spec] * count,
        out_specs=[vmem_spec] + [any_spec] * count,
        out_shape=[shape(2 * rows, width)] + [shape(*c.shape) for c in carried],
        input_output_aliases={2 + i: 1 + i for i in range(count)},
        name="join",
    )(first, second, *carried)


def row_of(at_ref, core_flip, slot, rows):
    core, x = at_ref[0], at_ref[1]
    core = 1 - core if core_flip else core
    return pl.multiple_of((core * 4 + ((x - slot) & 3)) * rows, rows)


def build(at_ref, mine_ref, other_ref, kinds, own, corr_ref, pen_ref, transposed):
    width = corr_ref.shape[1]
    rows = width // 8
    for flip, ref in ((False, mine_ref), (True, other_ref)):
        for slot in range(4):
            at = row_of(at_ref, flip, slot, rows)
            for i, kind in enumerate(kinds):
                corr_ref[i, pl.ds(at, rows), :] = ref[slot, kind * rows : (kind + 1) * rows, :]
    cross = jnp.zeros((1, width), f32)
    for i, kind in enumerate(kinds):
        corr = corr_ref[i]
        corr = corr.T if transposed else corr
        pen = 2.0 * off_weight * corr
        if kind == own:
            row_index = lax.broadcasted_iota(jnp.int32, corr.shape, 0)
            column = lax.broadcasted_iota(jnp.int32, corr.shape, 1)
            pen = jnp.where(row_index == column, -2.0 * (1.0 - corr), pen)
        cross = cross + jnp.sum(pen * corr, axis=0, keepdims=True)
        high, low = split(pen)
        first = i * 3 * width
        pen_ref[first : first + width, :] = high
        pen_ref[first + width : first + 2 * width, :] = low
        pen_ref[first + 2 * width : first + 3 * width, :] = high
    return cross


def scratch_for(kinds, width):
    return [
        pltpu.VMEM((kinds, width, width), f32),
        pltpu.VMEM((3 * kinds * width, width), bf16),
        pltpu.VMEM((8, width), f32),
    ]


def presplit_kernel(b_ref, prev_ref, next_ref, a_ref, f_ref, pf_ref, nf_ref, *refs):
    bs_ref, a_out_ref = refs[-2:]
    width = a_ref.shape[1]
    for kind, (ref, facts_ref) in enumerate(
        ((b_ref, f_ref), (prev_ref, pf_ref), (next_ref, nf_ref))
    ):
        high, low = split((ref[...] - facts_ref[2:3, :]) * facts_ref[3:4, :])
        bs_ref[:, 2 * kind * width : (2 * kind + 1) * width] = high
        bs_ref[:, (2 * kind + 1) * width : (2 * kind + 2) * width] = low
    high, low = split((a_ref[...] - f_ref[0:1, :]) * f_ref[1:2, :])
    a_out_ref[:, 0:width] = high
    a_out_ref[:, width:] = low


def presplit(b, prev_b, next_b, a, facts, wait_for):
    rows, width = a.shape
    tile = 256
    spec = pl.BlockSpec((tile, width), lambda i: (i, 0))
    whole = pl.BlockSpec((8, width), lambda i: (0, 0))
    return call(
        presplit_kernel,
        mib=16,
        grid=(rows // tile,),
        in_specs=[spec] * 4 + [whole] * 3 + [any_spec] * len(wait_for),
        out_specs=[
            pl.BlockSpec((tile, 6 * width), lambda i: (i, 0)),
            pl.BlockSpec((tile, 2 * width), lambda i: (i, 0)),
        ],
        out_shape=[
            jax.ShapeDtypeStruct((rows, 6 * width), bf16),
            jax.ShapeDtypeStruct((rows, 2 * width), bf16),
        ],
        name="presplit",
    )(b, prev_b, next_b, a, *facts, *wait_for)


def repeated(parts, width):
    blocks = []
    for first in range(0, parts.shape[1], 2 * width):
        high = parts[:, first : first + width]
        blocks += [high, high, parts[:, first + width : first + 2 * width]]
    return jnp.concatenate(blocks, axis=1)


def finish_a_kernel(at_ref, mine_ref, other_ref, *refs):
    facts, (a_ref, parts_ref) = refs[:3], refs[3:5]
    out_ref, ready_ref, corr_ref, pen_ref, vec_ref = refs[-5:]

    @pl.when(pl.program_id(0) == 0)
    def _():
        ready_ref[...] = jnp.zeros_like(ready_ref)
        kinds = (0, 1, 2)
        cross = build(at_ref, mine_ref, other_ref, kinds, 0, corr_ref, pen_ref, True)
        left = jnp.concatenate([thrice(ref[...]) for ref in facts], axis=1)
        vec_ref[0:1, :] = mm(left, pen_ref[...])[5:6]
        vec_ref[1:2, :] = cross

    grad = mm(repeated(parts_ref[...], a_ref.shape[1]), pen_ref[...])
    inverse = facts[0][1:2, :]
    normed = (a_ref[...] - facts[0][0:1, :]) * inverse
    out_ref[...] = (grad - vec_ref[0:1, :] - normed * vec_ref[1:2, :]) * inverse


def finish_a(at, mine, other, facts, a, parts):
    rows, width = a.shape
    tile = 512
    spec = pl.BlockSpec((tile, width), lambda i: (i, 0))
    whole = pl.BlockSpec((8, width), lambda i: (0, 0))
    slots = pl.BlockSpec(mine.shape, lambda i: (0, 0, 0))
    return call(
        finish_a_kernel,
        mib=40,
        grid=(rows // tile,),
        in_specs=[smem_spec, slots, slots]
        + [whole] * 3
        + [spec, pl.BlockSpec((tile, 6 * width), lambda i: (i, 0))],
        out_specs=[spec, whole],
        out_shape=[shape(rows, width), shape(8, width)],
        scratch_shapes=scratch_for(3, width),
        name="finish_a",
    )(at, mine, other, *facts, a, parts)


def own_b_kernel(at_ref, mine_ref, other_ref, facts_ref, parts_ref, *refs):
    out_ref, sums_ref, corr_ref, pen_ref, _ = refs[-5:]

    @pl.when(pl.program_id(0) == 0)
    def _():
        sums_ref[...] = jnp.zeros_like(sums_ref)
        cross = build(at_ref, mine_ref, other_ref, (0,), 0, corr_ref, pen_ref, False)
        sums_ref[0:1, :] = mm(thrice(facts_ref[...]), pen_ref[...])[4:5]
        sums_ref[1:2, :] = cross

    out_ref[...] = mm(repeated(parts_ref[...], out_ref.shape[1]), pen_ref[...])


def own_b(at, mine, other, facts, parts, wait_for):
    rows, width = parts.shape[0], parts.shape[1] // 2
    tile = 512
    spec = pl.BlockSpec((tile, width), lambda i: (i, 0))
    whole = pl.BlockSpec((8, width), lambda i: (0, 0))
    slots = pl.BlockSpec(mine.shape, lambda i: (0, 0, 0))
    return call(
        own_b_kernel,
        mib=24,
        grid=(rows // tile,),
        in_specs=[smem_spec, slots, slots, whole]
        + [pl.BlockSpec((tile, 2 * width), lambda i: (i, 0))]
        + [any_spec] * len(wait_for),
        out_specs=[spec, whole],
        out_shape=[shape(rows, width), shape(8, width)],
        scratch_shapes=scratch_for(1, width),
        name="own_b",
    )(at, mine, other, facts, parts, *wait_for)


def finish_b_kernel(bounds, at_ref, mine_ref, other_ref, f_ref, pf_ref, nf_ref, *refs):
    sums_ref, part_ref, b_ref, *halos = refs[:15]
    out_ref, corr_ref, pen_ref, vec_ref = refs[-4:]
    step = pl.program_id(0)

    @pl.when(step == 0)
    def _():
        cross = build(at_ref, mine_ref, other_ref, (0, 1), 2, corr_ref, pen_ref, False)
        left = jnp.concatenate([thrice(pf_ref[...]), thrice(nf_ref[...])], axis=1)
        vec_ref[0:1, :] = sums_ref[0:1, :] + mm(left, pen_ref[...])[4:5]
        vec_ref[1:2, :] = sums_ref[1:2, :] + cross

    def current(parts):
        blocks = []
        for i in (0, 1):
            at = 2 * step + i
            rest = jnp.where(at < bounds[2], parts[3 * i + 1][...], parts[3 * i + 2][...])
            blocks.append(jnp.where(at < bounds[1], parts[3 * i][...], rest))
        return jnp.concatenate(blocks, axis=0)

    prev = current(halos[:6]) * pf_ref[6:7, :] + pf_ref[7:8, :]
    next_ = current(halos[6:]) * nf_ref[6:7, :] + nf_ref[7:8, :]
    both = jnp.concatenate([thrice(prev), thrice(next_)], axis=1)
    grad = part_ref[...] + mm(both, pen_ref[...])
    normed = (b_ref[...] - f_ref[2:3, :]) * f_ref[3:4, :]
    out_ref[...] = (grad - vec_ref[0:1, :] - normed * vec_ref[1:2, :]) * f_ref[3:4, :]


def finish_b(at, mine, other, facts, sums, part, b, halos):
    rows, width = b.shape
    block = 128
    tile = 2 * block
    _, bounds, maps = halo_cuts(rows, block)
    spec = pl.BlockSpec((tile, width), lambda i: (i, 0))
    parts = [
        pl.BlockSpec((block, width), lambda i, half=half, part=part: part(2 * i + half))
        for half in (0, 1)
        for part in maps
    ]
    whole = pl.BlockSpec((8, width), lambda i: (0, 0))
    slots = pl.BlockSpec(mine.shape, lambda i: (0, 0, 0))
    return call(
        functools.partial(finish_b_kernel, bounds),
        mib=24,
        grid=(rows // tile,),
        in_specs=[smem_spec, slots, slots] + [whole] * 4 + [spec] * 2 + parts * 2,
        out_specs=spec,
        out_shape=shape(rows, width),
        scratch_shapes=scratch_for(2, width),
        name="finish_b",
    )(at, mine, other, *facts, sums, part, b, *halos[:3] * 2, *halos[3:] * 2)


def per_device(view_a, view_b):
    local_rows, width = view_a.shape
    half_rows = local_rows * lax.axis_size("row") // 2
    index = lax.axis_index("row")
    at = jnp.stack([index & 1, (index >> 1) & 3])

    prev_raw = across(view_b, 1)
    next_raw = across(view_b, -1)
    sums = sums_of(view_a, view_b)
    sums = sums + to_core(sums)
    parts = [sums] + [to_x(sums, shift) for shift in (1, 2, 3)]

    a_top, a_mid, a_low, half_facts, keep, send = own_corr(at, view_a, view_b, parts, half_rows)
    slots = fan(keep, to_core(send))
    own_parts = [slots[0]] + [to_x(slots[shift], shift) for shift in (1, 2, 3)]
    own, a_top = own_sum(own_parts, a_top, half_facts)
    prev_top = across(a_top, 1)
    next_top = across(a_top, -1)

    keep, *sends = side_corr(at, view_a, prev_raw, next_raw, half_facts, [own])
    slots = fan(keep, *[to_core(send) for send in sends])
    side_parts = [slots[0]] + [to_x(slots[shift], shift) for shift in (1, 2, 3)]
    mine = message(own, side_parts, half_facts, prev_top, next_top)
    left, right, trio, *facts = merge(at, mine, to_y(mine), half_rows)
    from_next = across(left, -1)
    from_prev = across(right, 1)
    trio_slots = [trio] + [to_x(trio, shift) for shift in (1, 2, 3)]
    ends, a_mid, a_low = join(from_prev, from_next, [a_mid, a_low])
    prev_mid = across(a_mid, 1)
    next_mid = across(a_mid, -1)
    prev_low = across(a_low, 1)
    next_low = across(a_low, -1)
    end_slots = [ends] + [to_x(ends, shift) for shift in (1, 2, 3)]
    b_parts, a_parts = presplit(view_b, prev_raw, next_raw, view_a, facts, [ends])
    mine = pack(trio_slots, [a_parts, prev_mid, next_mid])
    other = to_core(mine)
    grad_a, ready = finish_a(at, mine, other, facts, view_a, b_parts)
    ends = pack(end_slots, [ready, prev_low, next_low])
    part_b, sums = own_b(at, mine, other, facts[0], a_parts, [ends])
    halos = [prev_top, prev_mid, prev_low, next_top, next_mid, next_low]
    grad_b = finish_b(at, ends, to_core(ends), facts, sums, part_b, view_b, halos)
    return (grad_a, grad_b)


def solution(mesh):
    placed = (P("row", "grp"), P("row", "grp"))
    return jax.shard_map(
        per_device,
        mesh=mesh,
        in_specs=placed,
        out_specs=(P("row", "grp"), P("row", "grp")),
        check_vma=False,
    )
```
